256 devices in a mesh: grp: 32 (over z, x_lo, core), freq: 8 (over x_hi, y).
Axes of the slice: x: 4 (x_hi: 2, x_lo: 2; x = x_hi * 2 + x_lo), y: 4, z: 8, core: 2. Of those that a mesh axis runs over, the one named last changes fastest.
Arguments:
- spectra: bfloat16 [8, 8192, 1024], P('freq', 'grp'), may hold values from -3000 to 3000
- valid: int32 [8192, 512], P('grp'), may hold values 0 or 1
- station_index: int32 [16], replicated, may hold values from 0 to 8191, as said below
Outputs:
- cross: bfloat16 [8, 2, 8192, 8192], P('freq', None, 'grp')
- station_gather: float32 [16, 8192, 256], P(None, 'grp', 'freq')
The draws below stay inside these ranges and needn't reach their ends.
Inputs may be any that keep to these rules, and one draw needn't show every extreme that they name: `station_index`: 16 distinct channel numbers.
All inputs are finite; a program needn't handle non-finite values. No bound on the sum of `valid` on one device may be relied on, other than what follows from the above.
Results may differ from the reference program's by a relative error of at most 0.0056.
Values may be sent and summed in bfloat16 or wider, within the bound.
A program may use at most 128 MiB of HBM per device.

```python
import math
import jax
import jax.numpy as jnp
from jax import lax

WINDOWS = 512
STATIONS = 16
LAGS = 256
BINS = 8
CHANNELS = 8192


def draw_spectra(key, part):
    keys = jax.random.split(key, 4)
    shape = (BINS, CHANNELS, 2 * WINDOWS)
    base = jnp.clip(jax.random.normal(keys[0], shape, jnp.float32), -6.0, 6.0)
    bin_axis = jnp.arange(BINS).astype(jnp.float32)
    rise = jnp.exp(math.log(3.0) * bin_axis / max(BINS - 1, 1))
    jitter = jnp.exp(jax.random.uniform(keys[1], (BINS,), jnp.float32, -0.5, 0.5))
    channel_scale = jnp.exp(jax.random.uniform(keys[2], (CHANNELS,), jnp.float32, 0.0, math.log(10.0)))
    window_scale = jnp.exp(jax.random.uniform(keys[3], (WINDOWS,), jnp.float32, 0.0, math.log(10.0)))
    window_both = jnp.concatenate([window_scale, window_scale])
    values = base * (rise * jitter)[:, None, None] * channel_scale[None, :, None] * window_both[None, None, :]
    return values.astype(jnp.bfloat16)


def draw_station_index(key, part):
    order = jax.random.permutation(jax.random.fold_in(key, 7), CHANNELS)
    return order[:STATIONS].astype(jnp.int32)


def touch_ends(values, own_key, low, largest):
    longest = values.shape.index(max(values.shape))
    spots = []
    for shift in (0, 1):
        where = [jax.random.randint(jax.random.fold_in(own_key, axis), (), 0, length) for axis, length in enumerate(values.shape)]
        where[longest] = (where[longest] + shift) % values.shape[longest]
        spots.append(tuple(where))
    return values.at[spots[0]].set(low).at[spots[1]].set(largest)


def setup_inputs(seed: int = 0) -> dict:
    splits = jax.random.split(jax.random.key(seed), 4)
    spectra = draw_spectra(jax.random.fold_in(splits[3], 71), 0)
    valid = touch_ends((jax.random.randint(splits[1], (CHANNELS, WINDOWS), 0, 8) < 7).astype(jnp.int32), jax.random.fold_in(splits[1], 1), 0, 1)
    station_index = draw_station_index(jax.random.fold_in(splits[3], 71), 0)
    return {"spectra": spectra, "valid": valid, "station_index": station_index}


def reference(spectra, valid, station_index):
    spectrum_f32 = spectra.astype(jnp.float32)
    real_part = spectrum_f32[..., :WINDOWS]
    imag_part = spectrum_f32[..., WINDOWS:]
    band_power = lax.optimization_barrier(jnp.sum(real_part * real_part + imag_part * imag_part, axis=0))
    factor = lax.rsqrt(band_power / BINS + 1e-05) * valid.astype(jnp.float32)
    whitened = (spectrum_f32 * jnp.concatenate([factor, factor], axis=1)[None]).astype(jnp.bfloat16)
    swapped = jnp.concatenate([whitened[..., WINDOWS:], -whitened[..., :WINDOWS]], axis=2)
    stacked = jnp.concatenate([whitened, swapped], axis=1)
    scaling = 1.0 / math.sqrt(WINDOWS)

    def one_bin(operands):
        left_rows, right_rows = operands
        product = jnp.dot(left_rows, right_rows.T, preferred_element_type=jnp.float32)
        return (product * scaling).astype(jnp.bfloat16).reshape(2, CHANNELS, CHANNELS)
    cross = lax.map(one_bin, (stacked, whitened))
    station_left = jnp.concatenate([whitened[:, station_index], swapped[:, station_index]], axis=1)
    kernel = jnp.einsum('fkw,fjw->fkj', station_left.astype(jnp.float32), whitened.astype(jnp.float32), precision=lax.Precision.HIGHEST) * scaling
    kernel = kernel.reshape(BINS, 2, STATIONS, CHANNELS)
    bin_values = jnp.arange(BINS).astype(jnp.float32) + 1.0
    lag_values = jnp.arange(LAGS).astype(jnp.float32)
    phase = math.pi * bin_values[:, None] * lag_values[None, :] / LAGS
    lag_table = jnp.stack([jnp.cos(phase), -jnp.sin(phase)], axis=1)
    station_gather = jnp.einsum('frsc,frl->scl', kernel, lag_table, precision=lax.Precision.HIGHEST) / math.sqrt(BINS)
    return (cross, station_gather)
```

```python
import math

import jax
import jax.numpy as jnp
from jax import lax
from jax.sharding import Mesh
from jax.sharding import PartitionSpec as P

LAGS = 256
GRP = ("chip", "core")


def on_device(spectra, valid, station_index):
    bin_count, chan_count, double_width = spectra.shape
    window_count = double_width // 2
    spectrum_f32 = spectra.astype(jnp.float32)
    real_part = spectrum_f32[..., :window_count]
    imag_part = spectrum_f32[..., window_count:]
    local_power = jnp.sum(real_part * real_part + imag_part * imag_part, axis=0)
    band_power = lax.psum(local_power, "freq")
    freq_count = lax.axis_size("freq")
    total_bins = bin_count * freq_count
    factor = lax.rsqrt(band_power / total_bins + 1e-05) * valid.astype(jnp.float32)
    whitened = (spectrum_f32 * jnp.concatenate([factor, factor], axis=1)[None]).astype(jnp.bfloat16)
    swapped = jnp.concatenate([whitened[..., window_count:], -whitened[..., :window_count]], axis=2)
    stacked = jnp.concatenate([whitened, swapped], axis=1)
    scaling = 1.0 / math.sqrt(window_count)

    chip_count = lax.axis_size("chip")
    core_count = lax.axis_size("core")
    same_core = lax.all_gather(whitened, "chip", axis=1)
    both_cores = lax.all_gather(same_core, "core", axis=2)
    peer_rows = both_cores.reshape(bin_count, chip_count * core_count * chan_count, double_width)

    product = jnp.einsum("bkw,bjw->bkj", stacked, peer_rows, preferred_element_type=jnp.float32)
    cross = (
        (product * scaling)
        .astype(jnp.bfloat16)
        .reshape(bin_count, 2, chan_count, peer_rows.shape[1])
    )

    station_count = station_index.shape[0]
    station_rows = jnp.take(peer_rows, station_index, axis=1)
    station_swapped = jnp.concatenate(
        [station_rows[..., window_count:], -station_rows[..., :window_count]], axis=2
    )
    station_left = jnp.concatenate([station_rows, station_swapped], axis=1)
    kernel = (
        jnp.einsum("bkw,bjw->bkj", station_left, whitened, preferred_element_type=jnp.float32)
        * scaling
    )
    kernel = kernel.reshape(bin_count, 2, station_count, chan_count)
    all_bins = lax.all_gather(kernel, "freq", axis=0, tiled=True)

    lag_share = LAGS // freq_count
    freq_index = lax.axis_index("freq")
    bin_values = jnp.arange(total_bins, dtype=jnp.float32) + 1.0
    lag_values = (freq_index * lag_share + jnp.arange(lag_share, dtype=jnp.int32)).astype(jnp.float32)
    phase = math.pi * bin_values[:, None] * lag_values[None, :] / LAGS
    lag_table = jnp.stack([jnp.cos(phase), -jnp.sin(phase)], axis=1)
    station_gather = jnp.einsum(
        "frsc,frl->scl", all_bins, lag_table, precision=lax.Precision.HIGHEST
    ) / math.sqrt(total_bins)
    return (cross, station_gather)


def solution(mesh):
    grp_size, freq_size = mesh.devices.shape
    fine = Mesh(mesh.devices.reshape(grp_size // 2, 2, freq_size), ("chip", "core", "freq"))
    placed = (P("freq", GRP, None), P(GRP, None), P())
    return jax.shard_map(
        on_device,
        mesh=fine,
        in_specs=placed,
        out_specs=(P("freq", None, GRP, None), P(None, GRP, "freq")),
        check_vma=False,
    )
```

```python
import functools
import math

import jax
import jax.numpy as jnp
from jax import lax
from jax.experimental import pallas as pl
from jax.experimental.pallas import tpu as pltpu
from jax.sharding import PartitionSpec as P

LAGS = 256
MESH = pl.DeviceIdType.MESH


def _greet(peers, here):
    barrier = pltpu.get_barrier_semaphore()
    for k in range(1, peers):
        pl.semaphore_signal(barrier, inc=1, device_id=here((lax.axis_index("freq") + k) % peers), device_id_type=MESH)
    pl.semaphore_wait(barrier, peers - 1)


def _psum_kernel(peers, x_ref, out_ref, parts, send_a, recv_a, send_b, recv_b):
    me = lax.axis_index("freq")
    grp = lax.axis_index("grp")
    rows = x_ref.shape[0] // peers

    def here(peer):
        return (grp, peer)

    _greet(peers, here)
    scatter = []
    for k in range(1, peers):
        peer = (me + k) % peers
        copy = pltpu.make_async_remote_copy(
            src_ref=x_ref.at[pl.ds(pl.multiple_of(peer * rows, rows), rows)],
            dst_ref=parts.at[me],
            send_sem=send_a.at[peer],
            recv_sem=recv_a.at[me],
            device_id=here(peer),
            device_id_type=MESH,
        )
        copy.start()
        scatter.append(copy)
    own = x_ref[pl.ds(pl.multiple_of(me * rows, rows), rows), :]
    for k in range(1, peers):
        src = (me + peers - k) % peers
        pltpu.make_async_remote_copy(
            src_ref=x_ref.at[pl.ds(0, rows)],
            dst_ref=parts.at[src],
            send_sem=send_a.at[src],
            recv_sem=recv_a.at[src],
            device_id=here(src),
            device_id_type=MESH,
        ).wait_recv()
    for copy in scatter:
        copy.wait_send()
    parts[me] = own
    total = parts[0]
    for src in range(1, peers):
        total = total + parts[src]
    out_ref[pl.ds(pl.multiple_of(me * rows, rows), rows), :] = total
    gather = []
    for k in range(1, peers):
        peer = (me + k) % peers
        copy = pltpu.make_async_remote_copy(
            src_ref=out_ref.at[pl.ds(pl.multiple_of(me * rows, rows), rows)],
            dst_ref=out_ref.at[pl.ds(pl.multiple_of(me * rows, rows), rows)],
            send_sem=send_b.at[peer],
            recv_sem=recv_b.at[me],
            device_id=here(peer),
            device_id_type=MESH,
        )
        copy.start()
        gather.append(copy)
    for k in range(1, peers):
        src = (me + peers - k) % peers
        pltpu.make_async_remote_copy(
            src_ref=out_ref.at[pl.ds(pl.multiple_of(src * rows, rows), rows)],
            dst_ref=out_ref.at[pl.ds(pl.multiple_of(src * rows, rows), rows)],
            send_sem=send_b.at[src],
            recv_sem=recv_b.at[src],
            device_id=here(src),
            device_id_type=MESH,
        ).wait_recv()
    for copy in gather:
        copy.wait_send()


def freq_psum(x, peers):
    rows, cols = x.shape
    return pl.pallas_call(
        functools.partial(_psum_kernel, peers),
        out_shape=jax.ShapeDtypeStruct((rows, cols), x.dtype),
        in_specs=[pl.BlockSpec(memory_space=pltpu.VMEM)],
        out_specs=pl.BlockSpec(memory_space=pltpu.VMEM),
        scratch_shapes=[
            pltpu.VMEM((peers, rows // peers, cols), x.dtype),
            pltpu.SemaphoreType.DMA((peers,)),
            pltpu.SemaphoreType.DMA((peers,)),
            pltpu.SemaphoreType.DMA((peers,)),
            pltpu.SemaphoreType.DMA((peers,)),
        ],
        compiler_params=pltpu.CompilerParams(collective_id=0, has_side_effects=True),
    )(x)


def _gather_kernel(peers, x_ref, out_ref, send_sem, recv_sem):
    me = lax.axis_index("freq")
    grp = lax.axis_index("grp")

    def here(peer):
        return (grp, peer)

    _greet(peers, here)
    sent = []
    for k in range(1, peers):
        peer = (me + k) % peers
        copy = pltpu.make_async_remote_copy(
            src_ref=x_ref,
            dst_ref=out_ref.at[me],
            send_sem=send_sem.at[peer],
            recv_sem=recv_sem.at[me],
            device_id=here(peer),
            device_id_type=MESH,
        )
        copy.start()
        sent.append(copy)
    out_ref[me] = x_ref[...]
    for k in range(1, peers):
        src = (me + peers - k) % peers
        pltpu.make_async_remote_copy(
            src_ref=x_ref,
            dst_ref=out_ref.at[src],
            send_sem=send_sem.at[src],
            recv_sem=recv_sem.at[src],
            device_id=here(src),
            device_id_type=MESH,
        ).wait_recv()
    for copy in sent:
        copy.wait_send()


def freq_gather(x, peers):
    return pl.pallas_call(
        functools.partial(_gather_kernel, peers),
        out_shape=jax.ShapeDtypeStruct((peers, *x.shape), x.dtype),
        in_specs=[pl.BlockSpec(memory_space=pltpu.VMEM)],
        out_specs=pl.BlockSpec(memory_space=pltpu.VMEM),
        scratch_shapes=[
            pltpu.SemaphoreType.DMA((peers,)),
            pltpu.SemaphoreType.DMA((peers,)),
        ],
        compiler_params=pltpu.CompilerParams(collective_id=1, has_side_effects=True),
    )(x)


def on_device(spectra, valid, station_index):
    bin_count, chan_count, double_width = spectra.shape
    window_count = double_width // 2
    freq_count = lax.axis_size("freq")
    spectrum_f32 = spectra.astype(jnp.float32)
    real_part = spectrum_f32[..., :window_count]
    imag_part = spectrum_f32[..., window_count:]
    local_power = jnp.sum(real_part * real_part + imag_part * imag_part, axis=0)
    band_power = freq_psum(local_power, freq_count)
    total_bins = bin_count * freq_count
    factor = lax.rsqrt(band_power / total_bins + 1e-05) * valid.astype(jnp.float32)
    whitened = (spectrum_f32 * jnp.concatenate([factor, factor], axis=1)[None]).astype(jnp.bfloat16)
    swapped = jnp.concatenate([whitened[..., window_count:], -whitened[..., :window_count]], axis=2)
    stacked = jnp.concatenate([whitened, swapped], axis=1)
    scaling = 1.0 / math.sqrt(window_count)
    peer_rows = lax.all_gather(whitened, "grp", axis=1, tiled=True)
    product = jnp.einsum("bkw,bjw->bkj", stacked, peer_rows, preferred_element_type=jnp.float32)
    cross = (
        (product * scaling)
        .astype(jnp.bfloat16)
        .reshape(bin_count, 2, chan_count, peer_rows.shape[1])
    )

    station_count = station_index.shape[0]
    station_rows = jnp.take(peer_rows, station_index, axis=1, mode="clip")
    station_swapped = jnp.concatenate(
        [station_rows[..., window_count:], -station_rows[..., :window_count]], axis=2
    )
    station_left = jnp.concatenate([station_rows, station_swapped], axis=1)
    kernel = (
        jnp.einsum("bkw,bjw->bkj", station_left, whitened, preferred_element_type=jnp.float32)
        * scaling
    )
    kernel = kernel.reshape(2, station_count, chan_count)
    all_bins = freq_gather(kernel, freq_count)

    lag_share = LAGS // freq_count
    freq_index = lax.axis_index("freq")
    bin_values = jnp.arange(total_bins, dtype=jnp.float32) + 1.0
    lag_values = (freq_index * lag_share + jnp.arange(lag_share, dtype=jnp.int32)).astype(jnp.float32)
    phase = math.pi * bin_values[:, None] * lag_values[None, :] / LAGS
    lag_table = jnp.stack([jnp.cos(phase), -jnp.sin(phase)], axis=1)
    station_gather = jnp.einsum(
        "frsc,frl->scl", all_bins, lag_table, precision=lax.Precision.HIGHEST
    ) / math.sqrt(total_bins)
    return (cross, station_gather)


def solution(mesh):
    placed = (P("freq", "grp", None), P("grp", None), P())
    return jax.shard_map(
        on_device,
        mesh=mesh,
        in_specs=placed,
        out_specs=(P("freq", None, "grp", None), P(None, "grp", "freq")),
        check_vma=False,
    )
```

```python
import functools
import math

import jax
import jax.numpy as jnp
from jax import lax
from jax.experimental import pallas as pl
from jax.experimental.pallas import tpu as pltpu
from jax.sharding import PartitionSpec as P

LAGS = 256
MESH = pl.DeviceIdType.MESH


def _greet(peers, here):
    barrier = pltpu.get_barrier_semaphore()
    for k in range(1, peers):
        pl.semaphore_signal(barrier, inc=1, device_id=here((lax.axis_index("freq") + k) % peers), device_id_type=MESH)
    pl.semaphore_wait(barrier, peers - 1)


def _psum_kernel(peers, x_ref, out_ref, parts, send_a, recv_a, send_b, recv_b):
    me = lax.axis_index("freq")
    grp = lax.axis_index("grp")
    rows = x_ref.shape[0] // peers

    def here(peer):
        return (grp, peer)

    _greet(peers, here)
    scatter = []
    for k in range(1, peers):
        peer = (me + k) % peers
        copy = pltpu.make_async_remote_copy(
            src_ref=x_ref.at[pl.ds(pl.multiple_of(peer * rows, rows), rows)],
            dst_ref=parts.at[me],
            send_sem=send_a.at[peer],
            recv_sem=recv_a.at[me],
            device_id=here(peer),
            device_id_type=MESH,
        )
        copy.start()
        scatter.append(copy)
    own = x_ref[pl.ds(pl.multiple_of(me * rows, rows), rows), :]
    for k in range(1, peers):
        src = (me + peers - k) % peers
        pltpu.make_async_remote_copy(
            src_ref=x_ref.at[pl.ds(0, rows)],
            dst_ref=parts.at[src],
            send_sem=send_a.at[src],
            recv_sem=recv_a.at[src],
            device_id=here(src),
            device_id_type=MESH,
        ).wait_recv()
    for copy in scatter:
        copy.wait_send()
    parts[me] = own
    total = parts[0]
    for src in range(1, peers):
        total = total + parts[src]
    out_ref[pl.ds(pl.multiple_of(me * rows, rows), rows), :] = total
    gather = []
    for k in range(1, peers):
        peer = (me + k) % peers
        copy = pltpu.make_async_remote_copy(
            src_ref=out_ref.at[pl.ds(pl.multiple_of(me * rows, rows), rows)],
            dst_ref=out_ref.at[pl.ds(pl.multiple_of(me * rows, rows), rows)],
            send_sem=send_b.at[peer],
            recv_sem=recv_b.at[me],
            device_id=here(peer),
            device_id_type=MESH,
        )
        copy.start()
        gather.append(copy)
    for k in range(1, peers):
        src = (me + peers - k) % peers
        pltpu.make_async_remote_copy(
            src_ref=out_ref.at[pl.ds(pl.multiple_of(src * rows, rows), rows)],
            dst_ref=out_ref.at[pl.ds(pl.multiple_of(src * rows, rows), rows)],
            send_sem=send_b.at[src],
            recv_sem=recv_b.at[src],
            device_id=here(src),
            device_id_type=MESH,
        ).wait_recv()
    for copy in gather:
        copy.wait_send()


def freq_psum(x, peers):
    rows, cols = x.shape
    return pl.pallas_call(
        functools.partial(_psum_kernel, peers),
        out_shape=jax.ShapeDtypeStruct((rows, cols), x.dtype),
        in_specs=[pl.BlockSpec(memory_space=pltpu.VMEM)],
        out_specs=pl.BlockSpec(memory_space=pltpu.VMEM),
        scratch_shapes=[
            pltpu.VMEM((peers, rows // peers, cols), x.dtype),
            pltpu.SemaphoreType.DMA((peers,)),
            pltpu.SemaphoreType.DMA((peers,)),
            pltpu.SemaphoreType.DMA((peers,)),
            pltpu.SemaphoreType.DMA((peers,)),
        ],
        compiler_params=pltpu.CompilerParams(collective_id=0, has_side_effects=True),
    )(x)


def _gather_kernel(peers, x_ref, out_ref, send_sem, recv_sem):
    me = lax.axis_index("freq")
    grp = lax.axis_index("grp")

    def here(peer):
        return (grp, peer)

    _greet(peers, here)
    sent = []
    for k in range(1, peers):
        peer = (me + k) % peers
        copy = pltpu.make_async_remote_copy(
            src_ref=x_ref,
            dst_ref=out_ref.at[me],
            send_sem=send_sem.at[peer],
            recv_sem=recv_sem.at[me],
            device_id=here(peer),
            device_id_type=MESH,
        )
        copy.start()
        sent.append(copy)
    out_ref[me] = x_ref[...]
    for k in range(1, peers):
        src = (me + peers - k) % peers
        pltpu.make_async_remote_copy(
            src_ref=x_ref,
            dst_ref=out_ref.at[src],
            send_sem=send_sem.at[src],
            recv_sem=recv_sem.at[src],
            device_id=here(src),
            device_id_type=MESH,
        ).wait_recv()
    for copy in sent:
        copy.wait_send()


def freq_gather(x, peers):
    return pl.pallas_call(
        functools.partial(_gather_kernel, peers),
        out_shape=jax.ShapeDtypeStruct((peers, *x.shape), x.dtype),
        in_specs=[pl.BlockSpec(memory_space=pltpu.VMEM)],
        out_specs=pl.BlockSpec(memory_space=pltpu.VMEM),
        scratch_shapes=[
            pltpu.SemaphoreType.DMA((peers,)),
            pltpu.SemaphoreType.DMA((peers,)),
        ],
        compiler_params=pltpu.CompilerParams(collective_id=1, has_side_effects=True),
    )(x)


def _rows_kernel(chips, x_ref, out_ref, pair, held, send_sem, recv_sem):
    me = lax.axis_index("grp")
    band = lax.axis_index("freq")
    core = me % 2
    chip = me // 2
    partner = me + 1 - 2 * core

    def dev(g):
        return (g, band)

    barrier = pltpu.get_barrier_semaphore()
    pl.semaphore_signal(barrier, inc=1, device_id=dev(partner), device_id_type=MESH)
    for k in range(1, chips):
        pl.semaphore_signal(barrier, inc=1, device_id=dev(((chip + k) % chips) * 2 + core), device_id_type=MESH)
    pl.semaphore_wait(barrier, chips)

    first = pltpu.make_async_remote_copy(
        src_ref=x_ref, dst_ref=pair, send_sem=send_sem.at[0], recv_sem=recv_sem.at[0],
        device_id=dev(partner), device_id_type=MESH,
    )
    first.start()
    first.wait_recv()
    first.wait_send()
    held[chip] = (x_ref[...].astype(jnp.float32) + pair[...].astype(jnp.float32)).astype(held.dtype)
    sent = []
    for k in range(1, chips):
        peer = (chip + k) % chips
        copy = pltpu.make_async_remote_copy(
            src_ref=held.at[chip], dst_ref=held.at[chip], send_sem=send_sem.at[1 + peer],
            recv_sem=recv_sem.at[1 + chip], device_id=dev(peer * 2 + core), device_id_type=MESH,
        )
        copy.start()
        sent.append(copy)
    for k in range(1, chips):
        src = (chip + chips - k) % chips
        pltpu.make_async_remote_copy(
            src_ref=held.at[src], dst_ref=held.at[src], send_sem=send_sem.at[1 + src],
            recv_sem=recv_sem.at[1 + src], device_id=dev(src * 2 + core), device_id_type=MESH,
        ).wait_recv()
    for copy in sent:
        copy.wait_send()
    total = held[0].astype(jnp.float32)
    for c in range(1, chips):
        total = total + held[c].astype(jnp.float32)
    out_ref[...] = total.astype(out_ref.dtype)


def grp_rows_sum(x, chips):
    return pl.pallas_call(
        functools.partial(_rows_kernel, chips),
        out_shape=jax.ShapeDtypeStruct(x.shape, x.dtype),
        in_specs=[pl.BlockSpec(memory_space=pltpu.VMEM)],
        out_specs=pl.BlockSpec(memory_space=pltpu.VMEM),
        scratch_shapes=[
            pltpu.VMEM(x.shape, x.dtype),
            pltpu.VMEM((chips, *x.shape), x.dtype),
            pltpu.SemaphoreType.DMA((chips + 1,)),
            pltpu.SemaphoreType.DMA((chips + 1,)),
        ],
        compiler_params=pltpu.CompilerParams(collective_id=2, has_side_effects=True),
    )(x)


def on_device(spectra, valid, station_index):
    bin_count, chan_count, double_width = spectra.shape
    window_count = double_width // 2
    freq_count = lax.axis_size("freq")
    spectrum_f32 = spectra.astype(jnp.float32)
    real_part = spectrum_f32[..., :window_count]
    imag_part = spectrum_f32[..., window_count:]
    local_power = jnp.sum(real_part * real_part + imag_part * imag_part, axis=0)
    band_power = freq_psum(local_power, freq_count)
    total_bins = bin_count * freq_count
    factor = lax.rsqrt(band_power / total_bins + 1e-05) * valid.astype(jnp.float32)
    whitened = (spectrum_f32 * jnp.concatenate([factor, factor], axis=1)[None]).astype(jnp.bfloat16)
    swapped = jnp.concatenate([whitened[..., window_count:], -whitened[..., :window_count]], axis=2)
    stacked = jnp.concatenate([whitened, swapped], axis=1)
    scaling = 1.0 / math.sqrt(window_count)
    peer_rows = lax.all_gather(whitened, "grp", axis=1, tiled=True)
    product = jnp.einsum("bkw,bjw->bkj", stacked, peer_rows, preferred_element_type=jnp.float32)
    cross = (
        (product * scaling)
        .astype(jnp.bfloat16)
        .reshape(bin_count, 2, chan_count, peer_rows.shape[1])
    )

    station_count = station_index.shape[0]
    group_index = lax.axis_index("grp")
    local_rel = station_index - group_index * chan_count
    selector = (local_rel[:, None] == jnp.arange(chan_count, dtype=jnp.int32)[None, :]).astype(
        jnp.bfloat16
    )
    picked = jnp.einsum("sc,cw->sw", selector, whitened[0], preferred_element_type=jnp.float32)
    station_rows = grp_rows_sum(picked.astype(jnp.bfloat16), lax.axis_size("grp") // 2)[None]
    station_swapped = jnp.concatenate(
        [station_rows[..., window_count:], -station_rows[..., :window_count]], axis=2
    )
    station_left = jnp.concatenate([station_rows, station_swapped], axis=1)
    kernel = (
        jnp.einsum("bkw,bjw->bkj", station_left, whitened, preferred_element_type=jnp.float32)
        * scaling
    )
    kernel = kernel.reshape(2, station_count, chan_count)
    all_bins = freq_gather(kernel, freq_count)

    lag_share = LAGS // freq_count
    freq_index = lax.axis_index("freq")
    bin_values = jnp.arange(total_bins, dtype=jnp.float32) + 1.0
    lag_values = (freq_index * lag_share + jnp.arange(lag_share, dtype=jnp.int32)).astype(jnp.float32)
    phase = math.pi * bin_values[:, None] * lag_values[None, :] / LAGS
    lag_table = jnp.stack([jnp.cos(phase), -jnp.sin(phase)], axis=1)
    station_gather = jnp.einsum(
        "frsc,frl->scl", all_bins, lag_table, precision=lax.Precision.HIGHEST
    ) / math.sqrt(total_bins)
    return (cross, station_gather)


def solution(mesh):
    placed = (P("freq", "grp", None), P("grp", None), P())
    return jax.shard_map(
        on_device,
        mesh=mesh,
        in_specs=placed,
        out_specs=(P("freq", None, "grp", None), P(None, "grp", "freq")),
        check_vma=False,
    )
```

```python
import functools
import math

import jax
import jax.numpy as jnp
from jax import lax
from jax.experimental import pallas as pl
from jax.experimental.pallas import tpu as pltpu
from jax.sharding import PartitionSpec as P

LAGS = 256
MESH = pl.DeviceIdType.MESH


def _greet(peers, here):
    barrier = pltpu.get_barrier_semaphore()
    for k in range(1, peers):
        pl.semaphore_signal(barrier, inc=1, device_id=here((lax.axis_index("freq") + k) % peers), device_id_type=MESH)
    pl.semaphore_wait(barrier, peers - 1)


def _psum_kernel(peers, x_ref, out_ref, parts, send_a, recv_a, send_b, recv_b):
    me = lax.axis_index("freq")
    grp = lax.axis_index("grp")
    rows = x_ref.shape[0] // peers

    def here(peer):
        return (grp, peer)

    _greet(peers, here)
    scatter = []
    for k in range(1, peers):
        peer = (me + k) % peers
        copy = pltpu.make_async_remote_copy(
            src_ref=x_ref.at[pl.ds(pl.multiple_of(peer * rows, rows), rows)],
            dst_ref=parts.at[me],
            send_sem=send_a.at[peer],
            recv_sem=recv_a.at[me],
            device_id=here(peer),
            device_id_type=MESH,
        )
        copy.start()
        scatter.append(copy)
    own = x_ref[pl.ds(pl.multiple_of(me * rows, rows), rows), :]
    for k in range(1, peers):
        src = (me + peers - k) % peers
        pltpu.make_async_remote_copy(
            src_ref=x_ref.at[pl.ds(0, rows)],
            dst_ref=parts.at[src],
            send_sem=send_a.at[src],
            recv_sem=recv_a.at[src],
            device_id=here(src),
            device_id_type=MESH,
        ).wait_recv()
    for copy in scatter:
        copy.wait_send()
    parts[me] = own
    total = parts[0]
    for src in range(1, peers):
        total = total + parts[src]
    out_ref[pl.ds(pl.multiple_of(me * rows, rows), rows), :] = total
    gather = []
    for k in range(1, peers):
        peer = (me + k) % peers
        copy = pltpu.make_async_remote_copy(
            src_ref=out_ref.at[pl.ds(pl.multiple_of(me * rows, rows), rows)],
            dst_ref=out_ref.at[pl.ds(pl.multiple_of(me * rows, rows), rows)],
            send_sem=send_b.at[peer],
            recv_sem=recv_b.at[me],
            device_id=here(peer),
            device_id_type=MESH,
        )
        copy.start()
        gather.append(copy)
    for k in range(1, peers):
        src = (me + peers - k) % peers
        pltpu.make_async_remote_copy(
            src_ref=out_ref.at[pl.ds(pl.multiple_of(src * rows, rows), rows)],
            dst_ref=out_ref.at[pl.ds(pl.multiple_of(src * rows, rows), rows)],
            send_sem=send_b.at[src],
            recv_sem=recv_b.at[src],
            device_id=here(src),
            device_id_type=MESH,
        ).wait_recv()
    for copy in gather:
        copy.wait_send()


def freq_psum(x, peers):
    rows, cols = x.shape
    return pl.pallas_call(
        functools.partial(_psum_kernel, peers),
        out_shape=jax.ShapeDtypeStruct((rows, cols), x.dtype),
        in_specs=[pl.BlockSpec(memory_space=pltpu.VMEM)],
        out_specs=pl.BlockSpec(memory_space=pltpu.VMEM),
        scratch_shapes=[
            pltpu.VMEM((peers, rows // peers, cols), x.dtype),
            pltpu.SemaphoreType.DMA((peers,)),
            pltpu.SemaphoreType.DMA((peers,)),
            pltpu.SemaphoreType.DMA((peers,)),
            pltpu.SemaphoreType.DMA((peers,)),
        ],
        compiler_params=pltpu.CompilerParams(collective_id=0, has_side_effects=True),
    )(x)


def _gather_kernel(peers, x_ref, out_ref, send_sem, recv_sem):
    me = lax.axis_index("freq")
    grp = lax.axis_index("grp")

    def here(peer):
        return (grp, peer)

    _greet(peers, here)
    sent = []
    for k in range(1, peers):
        peer = (me + k) % peers
        copy = pltpu.make_async_remote_copy(
            src_ref=x_ref,
            dst_ref=out_ref.at[me],
            send_sem=send_sem.at[peer],
            recv_sem=recv_sem.at[me],
            device_id=here(peer),
            device_id_type=MESH,
        )
        copy.start()
        sent.append(copy)
    out_ref[me] = x_ref[...]
    for k in range(1, peers):
        src = (me + peers - k) % peers
        pltpu.make_async_remote_copy(
            src_ref=x_ref,
            dst_ref=out_ref.at[src],
            send_sem=send_sem.at[src],
            recv_sem=recv_sem.at[src],
            device_id=here(src),
            device_id_type=MESH,
        ).wait_recv()
    for copy in sent:
        copy.wait_send()


def freq_gather(x, peers):
    return pl.pallas_call(
        functools.partial(_gather_kernel, peers),
        out_shape=jax.ShapeDtypeStruct((peers, *x.shape), x.dtype),
        in_specs=[pl.BlockSpec(memory_space=pltpu.VMEM)],
        out_specs=pl.BlockSpec(memory_space=pltpu.VMEM),
        scratch_shapes=[
            pltpu.SemaphoreType.DMA((peers,)),
            pltpu.SemaphoreType.DMA((peers,)),
        ],
        compiler_params=pltpu.CompilerParams(collective_id=1, has_side_effects=True),
    )(x)


def _rows_kernel(chips, x_ref, out_ref, pair, held, send_sem, recv_sem):
    me = lax.axis_index("grp")
    band = lax.axis_index("freq")
    core = me % 2
    chip = me // 2
    partner = me + 1 - 2 * core

    def dev(g):
        return (g, band)

    barrier = pltpu.get_barrier_semaphore()
    pl.semaphore_signal(barrier, inc=1, device_id=dev(partner), device_id_type=MESH)
    for k in range(1, chips):
        pl.semaphore_signal(barrier, inc=1, device_id=dev(((chip + k) % chips) * 2 + core), device_id_type=MESH)
    pl.semaphore_wait(barrier, chips)

    first = pltpu.make_async_remote_copy(
        src_ref=x_ref, dst_ref=pair, send_sem=send_sem.at[0], recv_sem=recv_sem.at[0],
        device_id=dev(partner), device_id_type=MESH,
    )
    first.start()
    first.wait_recv()
    first.wait_send()
    held[chip] = (x_ref[...].astype(jnp.float32) + pair[...].astype(jnp.float32)).astype(held.dtype)
    sent = []
    for k in range(1, chips):
        peer = (chip + k) % chips
        copy = pltpu.make_async_remote_copy(
            src_ref=held.at[chip], dst_ref=held.at[chip], send_sem=send_sem.at[1 + peer],
            recv_sem=recv_sem.at[1 + chip], device_id=dev(peer * 2 + core), device_id_type=MESH,
        )
        copy.start()
        sent.append(copy)
    for k in range(1, chips):
        src = (chip + chips - k) % chips
        pltpu.make_async_remote_copy(
            src_ref=held.at[src], dst_ref=held.at[src], send_sem=send_sem.at[1 + src],
            recv_sem=recv_sem.at[1 + src], device_id=dev(src * 2 + core), device_id_type=MESH,
        ).wait_recv()
    for copy in sent:
        copy.wait_send()
    total = held[0].astype(jnp.float32)
    for c in range(1, chips):
        total = total + held[c].astype(jnp.float32)
    out_ref[...] = total.astype(out_ref.dtype)


def grp_rows_sum(x, chips):
    return pl.pallas_call(
        functools.partial(_rows_kernel, chips),
        out_shape=jax.ShapeDtypeStruct(x.shape, x.dtype),
        in_specs=[pl.BlockSpec(memory_space=pltpu.VMEM)],
        out_specs=pl.BlockSpec(memory_space=pltpu.VMEM),
        scratch_shapes=[
            pltpu.VMEM(x.shape, x.dtype),
            pltpu.VMEM((chips, *x.shape), x.dtype),
            pltpu.SemaphoreType.DMA((chips + 1,)),
            pltpu.SemaphoreType.DMA((chips + 1,)),
        ],
        compiler_params=pltpu.CompilerParams(collective_id=2, has_side_effects=True),
    )(x)


def _gather_grp_kernel(zs, x_ref, out_ref, send_sem, recv_ring, recv_x, recv_sib, local_sem):
    me = lax.axis_index("grp")
    band = lax.axis_index("freq")
    c = me % 2
    xl = (me // 2) % 2
    z = me // 4
    step = 1 - 2 * c
    half = x_ref.shape[0] // 2

    def blk(zz, xx, cc):
        return (zz * 2 + xx) * 2 + cc

    def dev(g):
        return (g, band)

    sib = blk(z, xl, 1 - c)
    partner = blk(z, 1 - xl, c)
    nxt = blk((z + step + zs) % zs, xl, c)
    prv = blk((z - step + zs) % zs, xl, c)

    barrier = pltpu.get_barrier_semaphore()
    for g in (sib, partner, nxt, prv):
        pl.semaphore_signal(barrier, inc=1, device_id=dev(g), device_id_type=MESH)
    pl.semaphore_wait(barrier, 4)

    sends = []

    def send(src, dst, recv, g):
        copy = pltpu.make_async_remote_copy(
            src_ref=src, dst_ref=dst, send_sem=send_sem.at[len(sends)], recv_sem=recv,
            device_id=dev(g), device_id_type=MESH,
        )
        copy.start()
        sends.append(copy)

    def wait(dst, recv, g):
        pltpu.make_async_remote_copy(
            src_ref=dst, dst_ref=dst, send_sem=send_sem.at[0], recv_sem=recv,
            device_id=dev(g), device_id_type=MESH,
        ).wait_recv()

    def rows(b, h):
        return out_ref.at[b, pl.ds(pl.multiple_of(h * half, half), half)]

    own = blk(z, xl, c)
    local = pltpu.make_async_copy(x_ref, out_ref.at[own], local_sem.at[0])
    local.start()
    send(x_ref, out_ref.at[own], recv_sib.at[0], sib)
    send(x_ref, out_ref.at[own], recv_x.at[0], partner)
    send(x_ref, out_ref.at[own], recv_ring.at[0, 0], nxt)
    across = blk(z, 1 - xl, c)
    wait(out_ref.at[across], recv_x.at[0], partner)
    send(out_ref.at[across], out_ref.at[across], recv_sib.at[1], sib)
    send(rows(across, xl), rows(across, xl), recv_ring.at[0, 1], nxt)
    for s in range(zs - 1):
        zo = (z - step * (s + 1) + 2 * zs) % zs
        full = blk(zo, xl, c)
        part = blk(zo, 1 - xl, c)
        wait(out_ref.at[full], recv_ring.at[s, 0], prv)
        wait(rows(part, xl), recv_ring.at[s, 1], prv)
        if s < zs - 2:
            send(out_ref.at[full], out_ref.at[full], recv_ring.at[s + 1, 0], nxt)
            send(rows(part, xl), rows(part, xl), recv_ring.at[s + 1, 1], nxt)
        send(rows(full, xl), rows(full, xl), recv_x.at[1 + s], partner)
        send(out_ref.at[full], out_ref.at[full], recv_sib.at[2 + 2 * s], sib)
        send(rows(part, xl), rows(part, xl), recv_sib.at[3 + 2 * s], sib)
        wait(rows(part, 1 - xl), recv_x.at[1 + s], partner)
        send(rows(part, 1 - xl), rows(part, 1 - xl), recv_sib.at[2 * zs + s], sib)
    wait(out_ref.at[sib], recv_sib.at[0], sib)
    wait(out_ref.at[blk(z, 1 - xl, 1 - c)], recv_sib.at[1], sib)
    for s in range(zs - 1):
        zo = (z + step * (s + 1) + 2 * zs) % zs
        wait(out_ref.at[blk(zo, xl, 1 - c)], recv_sib.at[2 + 2 * s], sib)
        wait(rows(blk(zo, 1 - xl, 1 - c), xl), recv_sib.at[3 + 2 * s], sib)
        wait(rows(blk(zo, 1 - xl, 1 - c), 1 - xl), recv_sib.at[2 * zs + s], sib)
    local.wait()
    for copy in sends:
        copy.wait_send()


def grp_gather(x, zs):
    groups = lax.axis_size("grp")
    rows, cols = x.shape
    return pl.pallas_call(
        functools.partial(_gather_grp_kernel, zs),
        out_shape=jax.ShapeDtypeStruct((groups, rows, cols), x.dtype),
        in_specs=[pl.BlockSpec(memory_space=pl.ANY)],
        out_specs=pl.BlockSpec(memory_space=pl.ANY),
        scratch_shapes=[
            pltpu.SemaphoreType.DMA((6 * zs,)),
            pltpu.SemaphoreType.DMA((zs - 1, 2)),
            pltpu.SemaphoreType.DMA((zs,)),
            pltpu.SemaphoreType.DMA((3 * zs - 1,)),
            pltpu.SemaphoreType.DMA((1,)),
        ],
        compiler_params=pltpu.CompilerParams(collective_id=3, has_side_effects=True),
    )(x)


def on_device(spectra, valid, station_index):
    bin_count, chan_count, double_width = spectra.shape
    window_count = double_width // 2
    freq_count = lax.axis_size("freq")
    spectrum_f32 = spectra.astype(jnp.float32)
    real_part = spectrum_f32[..., :window_count]
    imag_part = spectrum_f32[..., window_count:]
    local_power = jnp.sum(real_part * real_part + imag_part * imag_part, axis=0)
    band_power = freq_psum(local_power, freq_count)
    total_bins = bin_count * freq_count
    factor = lax.rsqrt(band_power / total_bins + 1e-05) * valid.astype(jnp.float32)
    whitened = (spectrum_f32 * jnp.concatenate([factor, factor], axis=1)[None]).astype(jnp.bfloat16)
    swapped = jnp.concatenate([whitened[..., window_count:], -whitened[..., :window_count]], axis=2)
    stacked = jnp.concatenate([whitened, swapped], axis=1)
    scaling = 1.0 / math.sqrt(window_count)
    peer_rows = grp_gather(whitened[0], lax.axis_size("grp") // 4).reshape(
        bin_count, lax.axis_size("grp") * chan_count, double_width
    )
    product = jnp.einsum("bkw,bjw->bkj", stacked, peer_rows, preferred_element_type=jnp.float32)
    cross = (
        (product * scaling)
        .astype(jnp.bfloat16)
        .reshape(bin_count, 2, chan_count, peer_rows.shape[1])
    )

    station_count = station_index.shape[0]
    group_index = lax.axis_index("grp")
    local_rel = station_index - group_index * chan_count
    selector = (local_rel[:, None] == jnp.arange(chan_count, dtype=jnp.int32)[None, :]).astype(
        jnp.bfloat16
    )
    picked = jnp.einsum("sc,cw->sw", selector, whitened[0], preferred_element_type=jnp.float32)
    station_rows = grp_rows_sum(picked.astype(jnp.bfloat16), lax.axis_size("grp") // 2)[None]
    station_swapped = jnp.concatenate(
        [station_rows[..., window_count:], -station_rows[..., :window_count]], axis=2
    )
    station_left = jnp.concatenate([station_rows, station_swapped], axis=1)
    kernel = (
        jnp.einsum("bkw,bjw->bkj", station_left, whitened, preferred_element_type=jnp.float32)
        * scaling
    )
    kernel = kernel.reshape(2, station_count, chan_count)
    all_bins = freq_gather(kernel, freq_count)

    lag_share = LAGS // freq_count
    freq_index = lax.axis_index("freq")
    bin_values = jnp.arange(total_bins, dtype=jnp.float32) + 1.0
    lag_values = (freq_index * lag_share + jnp.arange(lag_share, dtype=jnp.int32)).astype(jnp.float32)
    phase = math.pi * bin_values[:, None] * lag_values[None, :] / LAGS
    lag_table = jnp.stack([jnp.cos(phase), -jnp.sin(phase)], axis=1)
    station_gather = jnp.einsum(
        "frsc,frl->scl", all_bins, lag_table, precision=lax.Precision.HIGHEST
    ) / math.sqrt(total_bins)
    return (cross, station_gather)


def solution(mesh):
    placed = (P("freq", "grp", None), P("grp", None), P())
    return jax.shard_map(
        on_device,
        mesh=mesh,
        in_specs=placed,
        out_specs=(P("freq", None, "grp", None), P(None, "grp", "freq")),
        check_vma=False,
    )
```

```python
import functools
import math

import jax
import jax.numpy as jnp
from jax import lax
from jax.experimental import pallas as pl
from jax.experimental.pallas import tpu as pltpu
from jax.sharding import PartitionSpec as P

LAGS = 256
MESH = pl.DeviceIdType.MESH


def _greet(peers, here):
    barrier = pltpu.get_barrier_semaphore()
    for k in range(1, peers):
        pl.semaphore_signal(barrier, inc=1, device_id=here((lax.axis_index("freq") + k) % peers), device_id_type=MESH)
    pl.semaphore_wait(barrier, peers - 1)


def _psum_kernel(peers, x_ref, out_ref, parts, send_a, recv_a, send_b, recv_b):
    me = lax.axis_index("freq")
    grp = lax.axis_index("grp")
    rows = x_ref.shape[0] // peers

    def here(peer):
        return (grp, peer)

    _greet(peers, here)
    scatter = []
    for k in range(1, peers):
        peer = (me + k) % peers
        copy = pltpu.make_async_remote_copy(
            src_ref=x_ref.at[pl.ds(pl.multiple_of(peer * rows, rows), rows)],
            dst_ref=parts.at[me],
            send_sem=send_a.at[peer],
            recv_sem=recv_a.at[me],
            device_id=here(peer),
            device_id_type=MESH,
        )
        copy.start()
        scatter.append(copy)
    own = x_ref[pl.ds(pl.multiple_of(me * rows, rows), rows), :]
    for k in range(1, peers):
        src = (me + peers - k) % peers
        pltpu.make_async_remote_copy(
            src_ref=x_ref.at[pl.ds(0, rows)],
            dst_ref=parts.at[src],
            send_sem=send_a.at[src],
            recv_sem=recv_a.at[src],
            device_id=here(src),
            device_id_type=MESH,
        ).wait_recv()
    for copy in scatter:
        copy.wait_send()
    parts[me] = own
    total = parts[0]
    for src in range(1, peers):
        total = total + parts[src]
    out_ref[pl.ds(pl.multiple_of(me * rows, rows), rows), :] = total
    gather = []
    for k in range(1, peers):
        peer = (me + k) % peers
        copy = pltpu.make_async_remote_copy(
            src_ref=out_ref.at[pl.ds(pl.multiple_of(me * rows, rows), rows)],
            dst_ref=out_ref.at[pl.ds(pl.multiple_of(me * rows, rows), rows)],
            send_sem=send_b.at[peer],
            recv_sem=recv_b.at[me],
            device_id=here(peer),
            device_id_type=MESH,
        )
        copy.start()
        gather.append(copy)
    for k in range(1, peers):
        src = (me + peers - k) % peers
        pltpu.make_async_remote_copy(
            src_ref=out_ref.at[pl.ds(pl.multiple_of(src * rows, rows), rows)],
            dst_ref=out_ref.at[pl.ds(pl.multiple_of(src * rows, rows), rows)],
            send_sem=send_b.at[src],
            recv_sem=recv_b.at[src],
            device_id=here(src),
            device_id_type=MESH,
        ).wait_recv()
    for copy in gather:
        copy.wait_send()


def freq_psum(x, peers):
    rows, cols = x.shape
    return pl.pallas_call(
        functools.partial(_psum_kernel, peers),
        out_shape=jax.ShapeDtypeStruct((rows, cols), x.dtype),
        in_specs=[pl.BlockSpec(memory_space=pltpu.VMEM)],
        out_specs=pl.BlockSpec(memory_space=pltpu.VMEM),
        scratch_shapes=[
            pltpu.VMEM((peers, rows // peers, cols), x.dtype),
            pltpu.SemaphoreType.DMA((peers,)),
            pltpu.SemaphoreType.DMA((peers,)),
            pltpu.SemaphoreType.DMA((peers,)),
            pltpu.SemaphoreType.DMA((peers,)),
        ],
        compiler_params=pltpu.CompilerParams(collective_id=0, has_side_effects=True),
    )(x)


def _gather_kernel(peers, x_ref, out_ref, send_sem, recv_sem):
    me = lax.axis_index("freq")
    grp = lax.axis_index("grp")

    def here(peer):
        return (grp, peer)

    _greet(peers, here)
    sent = []
    for k in range(1, peers):
        peer = (me + k) % peers
        copy = pltpu.make_async_remote_copy(
            src_ref=x_ref,
            dst_ref=out_ref.at[me],
            send_sem=send_sem.at[peer],
            recv_sem=recv_sem.at[me],
            device_id=here(peer),
            device_id_type=MESH,
        )
        copy.start()
        sent.append(copy)
    out_ref[me] = x_ref[...]
    for k in range(1, peers):
        src = (me + peers - k) % peers
        pltpu.make_async_remote_copy(
            src_ref=x_ref,
            dst_ref=out_ref.at[src],
            send_sem=send_sem.at[src],
            recv_sem=recv_sem.at[src],
            device_id=here(src),
            device_id_type=MESH,
        ).wait_recv()
    for copy in sent:
        copy.wait_send()


def freq_gather(x, peers):
    return pl.pallas_call(
        functools.partial(_gather_kernel, peers),
        out_shape=jax.ShapeDtypeStruct((peers, *x.shape), x.dtype),
        in_specs=[pl.BlockSpec(memory_space=pltpu.VMEM)],
        out_specs=pl.BlockSpec(memory_space=pltpu.VMEM),
        scratch_shapes=[
            pltpu.SemaphoreType.DMA((peers,)),
            pltpu.SemaphoreType.DMA((peers,)),
        ],
        compiler_params=pltpu.CompilerParams(collective_id=1, has_side_effects=True),
    )(x)


def _rows_kernel(chips, x_ref, out_ref, pair, held, send_sem, recv_sem):
    me = lax.axis_index("grp")
    band = lax.axis_index("freq")
    core = me % 2
    chip = me // 2
    partner = me + 1 - 2 * core

    def dev(g):
        return (g, band)

    barrier = pltpu.get_barrier_semaphore()
    pl.semaphore_signal(barrier, inc=1, device_id=dev(partner), device_id_type=MESH)
    for k in range(1, chips):
        pl.semaphore_signal(barrier, inc=1, device_id=dev(((chip + k) % chips) * 2 + core), device_id_type=MESH)
    pl.semaphore_wait(barrier, chips)

    first = pltpu.make_async_remote_copy(
        src_ref=x_ref, dst_ref=pair, send_sem=send_sem.at[0], recv_sem=recv_sem.at[0],
        device_id=dev(partner), device_id_type=MESH,
    )
    first.start()
    first.wait_recv()
    first.wait_send()
    held[chip] = (x_ref[...].astype(jnp.float32) + pair[...].astype(jnp.float32)).astype(held.dtype)
    sent = []
    for k in range(1, chips):
        peer = (chip + k) % chips
        copy = pltpu.make_async_remote_copy(
            src_ref=held.at[chip], dst_ref=held.at[chip], send_sem=send_sem.at[1 + peer],
            recv_sem=recv_sem.at[1 + chip], device_id=dev(peer * 2 + core), device_id_type=MESH,
        )
        copy.start()
        sent.append(copy)
    for k in range(1, chips):
        src = (chip + chips - k) % chips
        pltpu.make_async_remote_copy(
            src_ref=held.at[src], dst_ref=held.at[src], send_sem=send_sem.at[1 + src],
            recv_sem=recv_sem.at[1 + src], device_id=dev(src * 2 + core), device_id_type=MESH,
        ).wait_recv()
    for copy in sent:
        copy.wait_send()
    total = held[0].astype(jnp.float32)
    for c in range(1, chips):
        total = total + held[c].astype(jnp.float32)
    out_ref[...] = total.astype(out_ref.dtype)


def grp_rows_sum(x, chips):
    return pl.pallas_call(
        functools.partial(_rows_kernel, chips),
        out_shape=jax.ShapeDtypeStruct(x.shape, x.dtype),
        in_specs=[pl.BlockSpec(memory_space=pltpu.VMEM)],
        out_specs=pl.BlockSpec(memory_space=pltpu.VMEM),
        scratch_shapes=[
            pltpu.VMEM(x.shape, x.dtype),
            pltpu.VMEM((chips, *x.shape), x.dtype),
            pltpu.SemaphoreType.DMA((chips + 1,)),
            pltpu.SemaphoreType.DMA((chips + 1,)),
        ],
        compiler_params=pltpu.CompilerParams(collective_id=2, has_side_effects=True),
    )(x)


def _cross_kernel(zs, scaling, x_ref, left_ref, sel_ref, cross_ref, rows_ref, held, stage, picked,
                  send_sem, recv_ring, recv_x, recv_sib, out_sem):
    me = lax.axis_index("grp")
    band = lax.axis_index("freq")
    c = me % 2
    xl = (me // 2) % 2
    z = me // 4
    step = 1 - 2 * c
    width = x_ref.shape[0]
    half = width // 2

    def blk(zz, xx, cc):
        return (zz * 2 + xx) * 2 + cc

    def dev(g):
        return (g, band)

    sib = blk(z, xl, 1 - c)
    partner = blk(z, 1 - xl, c)
    nxt = blk((z + step + zs) % zs, xl, c)
    prv = blk((z - step + zs) % zs, xl, c)

    barrier = pltpu.get_barrier_semaphore()
    for g in (sib, partner, nxt, prv):
        pl.semaphore_signal(barrier, inc=1, device_id=dev(g), device_id_type=MESH)
    pl.semaphore_wait(barrier, 4)

    sends = []
    outs = []

    def send(src, dst, recv, g):
        copy = pltpu.make_async_remote_copy(
            src_ref=src, dst_ref=dst, send_sem=send_sem.at[len(sends)], recv_sem=recv,
            device_id=dev(g), device_id_type=MESH,
        )
        copy.start()
        sends.append(copy)

    def wait(dst, recv, g):
        pltpu.make_async_remote_copy(
            src_ref=dst, dst_ref=dst, send_sem=send_sem.at[0], recv_sem=recv,
            device_id=dev(g), device_id_type=MESH,
        ).wait_recv()

    def rows(b, h):
        return held.at[b, pl.ds(pl.multiple_of(h * half, half), half)]

    def compute(b):
        block = held[b]
        prod = lax.dot_general(
            left_ref[...], block, (((1,), (1,)), ((), ())), preferred_element_type=jnp.float32
        )
        slot = len(outs) % 2
        if len(outs) >= 2:
            outs[-2].wait()
        stage[slot] = (prod * scaling).astype(stage.dtype).reshape(stage.shape[1:])
        copy = pltpu.make_async_copy(
            stage.at[slot], cross_ref.at[:, :, pl.ds(pl.multiple_of(b * width, width), width)], out_sem.at[slot]
        )
        copy.start()
        outs.append(copy)
        picked[...] += jnp.dot(
            sel_ref[:, pl.ds(pl.multiple_of(b * width, width), width)], block,
            preferred_element_type=jnp.float32,
        )

    picked[...] = jnp.zeros_like(picked)
    own = blk(z, xl, c)
    held[own] = x_ref[...]
    send(x_ref, held.at[own], recv_x.at[0], partner)
    send(x_ref, held.at[own], recv_sib.at[0], sib)
    send(x_ref.at[pl.ds(0, half)], rows(own, 0), recv_ring.at[0, 0], nxt)
    send(x_ref.at[pl.ds(half, half)], rows(own, 1), recv_ring.at[0, 1], nxt)
    compute(own)
    across = blk(z, 1 - xl, c)
    wait(held.at[across], recv_x.at[0], partner)
    send(rows(across, xl), rows(across, xl), recv_ring.at[0, 2], nxt)
    send(held.at[across], held.at[across], recv_sib.at[1], sib)
    compute(across)
    wait(held.at[sib], recv_sib.at[0], sib)
    compute(sib)
    sib_across = blk(z, 1 - xl, 1 - c)
    wait(held.at[sib_across], recv_sib.at[1], sib)
    compute(sib_across)
    for s in range(zs - 1):
        zo = (z - step * (s + 1) + 2 * zs) % zs
        full = blk(zo, xl, c)
        part = blk(zo, 1 - xl, c)
        pieces = ((full, 0), (full, 1), (part, xl))
        for k, (b, h) in enumerate(pieces):
            wait(rows(b, h), recv_ring.at[s, k], prv)
            if s < zs - 2:
                send(rows(b, h), rows(b, h), recv_ring.at[s + 1, k], nxt)
            send(rows(b, h), rows(b, h), recv_sib.at[2 + 3 * s + k], sib)
        send(rows(full, xl), rows(full, xl), recv_x.at[1 + s], partner)
        compute(full)
        wait(rows(part, 1 - xl), recv_x.at[1 + s], partner)
        send(rows(part, 1 - xl), rows(part, 1 - xl), recv_sib.at[2 + 3 * (zs - 1) + s], sib)
        compute(part)
        zt = (z + step * (s + 1) + 2 * zs) % zs
        sfull = blk(zt, xl, 1 - c)
        spart = blk(zt, 1 - xl, 1 - c)
        for k, (b, h) in enumerate(((sfull, 0), (sfull, 1), (spart, xl))):
            wait(rows(b, h), recv_sib.at[2 + 3 * s + k], sib)
        compute(sfull)
        wait(rows(spart, 1 - xl), recv_sib.at[2 + 3 * (zs - 1) + s], sib)
        compute(spart)
    rows_ref[...] = picked[...].astype(rows_ref.dtype)
    for copy in outs[-2:]:
        copy.wait()
    for copy in sends:
        copy.wait_send()


def grp_cross(whitened, left, selector, scaling, zs):
    groups = lax.axis_size("grp")
    width, cols = whitened.shape
    return pl.pallas_call(
        functools.partial(_cross_kernel, zs, scaling),
        out_shape=(
            jax.ShapeDtypeStruct((2, width, groups * width), whitened.dtype),
            jax.ShapeDtypeStruct((selector.shape[0], cols), whitened.dtype),
        ),
        in_specs=[pl.BlockSpec(memory_space=pltpu.VMEM)] * 3,
        out_specs=(pl.BlockSpec(memory_space=pl.ANY), pl.BlockSpec(memory_space=pltpu.VMEM)),
        scratch_shapes=[
            pltpu.VMEM((groups, width, cols), whitened.dtype),
            pltpu.VMEM((2, 2, width, width), whitened.dtype),
            pltpu.VMEM((selector.shape[0], cols), jnp.float32),
            pltpu.SemaphoreType.DMA((8 * zs + 8,)),
            pltpu.SemaphoreType.DMA((zs - 1, 3)),
            pltpu.SemaphoreType.DMA((zs,)),
            pltpu.SemaphoreType.DMA((2 + 4 * (zs - 1),)),
            pltpu.SemaphoreType.DMA((2,)),
        ],
        compiler_params=pltpu.CompilerParams(
            collective_id=3, has_side_effects=True, vmem_limit_bytes=56 * 1024 * 1024
        ),
    )(whitened, left, selector)


def on_device(spectra, valid, station_index):
    bin_count, chan_count, double_width = spectra.shape
    window_count = double_width // 2
    freq_count = lax.axis_size("freq")
    spectrum_f32 = spectra.astype(jnp.float32)
    real_part = spectrum_f32[..., :window_count]
    imag_part = spectrum_f32[..., window_count:]
    local_power = jnp.sum(real_part * real_part + imag_part * imag_part, axis=0)
    band_power = freq_psum(local_power, freq_count)
    total_bins = bin_count * freq_count
    factor = lax.rsqrt(band_power / total_bins + 1e-05) * valid.astype(jnp.float32)
    whitened = (spectrum_f32 * jnp.concatenate([factor, factor], axis=1)[None]).astype(jnp.bfloat16)
    swapped = jnp.concatenate([whitened[..., window_count:], -whitened[..., :window_count]], axis=2)
    stacked = jnp.concatenate([whitened, swapped], axis=1)
    scaling = 1.0 / math.sqrt(window_count)
    station_count = station_index.shape[0]
    total_chans = lax.axis_size("grp") * chan_count
    selector = (station_index[:, None] == jnp.arange(total_chans, dtype=jnp.int32)[None, :]).astype(
        jnp.bfloat16
    )
    cross, station_rows = grp_cross(
        whitened[0], stacked[0], selector, scaling, lax.axis_size("grp") // 4
    )
    cross = cross[None]
    station_rows = station_rows[None]
    station_swapped = jnp.concatenate(
        [station_rows[..., window_count:], -station_rows[..., :window_count]], axis=2
    )
    station_left = jnp.concatenate([station_rows, station_swapped], axis=1)
    kernel = (
        jnp.einsum("bkw,bjw->bkj", station_left, whitened, preferred_element_type=jnp.float32)
        * scaling
    )
    kernel = kernel.reshape(2, station_count, chan_count)
    all_bins = freq_gather(kernel, freq_count)

    lag_share = LAGS // freq_count
    freq_index = lax.axis_index("freq")
    bin_values = jnp.arange(total_bins, dtype=jnp.float32) + 1.0
    lag_values = (freq_index * lag_share + jnp.arange(lag_share, dtype=jnp.int32)).astype(jnp.float32)
    phase = math.pi * bin_values[:, None] * lag_values[None, :] / LAGS
    lag_table = jnp.stack([jnp.cos(phase), -jnp.sin(phase)], axis=1)
    station_gather = jnp.einsum(
        "frsc,frl->scl", all_bins, lag_table, precision=lax.Precision.HIGHEST
    ) / math.sqrt(total_bins)
    return (cross, station_gather)


def solution(mesh):
    placed = (P("freq", "grp", None), P("grp", None), P())
    return jax.shard_map(
        on_device,
        mesh=mesh,
        in_specs=placed,
        out_specs=(P("freq", None, "grp", None), P(None, "grp", "freq")),
        check_vma=False,
    )
```

```python
import functools
import math

import jax
import jax.numpy as jnp
from jax import lax
from jax.experimental import pallas as pl
from jax.experimental.pallas import tpu as pltpu
from jax.sharding import PartitionSpec as P

LAGS = 256
MESH = pl.DeviceIdType.MESH


def _greet(peers, here):
    barrier = pltpu.get_barrier_semaphore()
    for k in range(1, peers):
        pl.semaphore_signal(barrier, inc=1, device_id=here((lax.axis_index("freq") + k) % peers), device_id_type=MESH)
    pl.semaphore_wait(barrier, peers - 1)


def _psum_kernel(peers, x_ref, out_ref, parts, send_a, recv_a, send_b, recv_b):
    me = lax.axis_index("freq")
    grp = lax.axis_index("grp")
    rows = x_ref.shape[0] // peers

    def here(peer):
        return (grp, peer)

    _greet(peers, here)
    scatter = []
    for k in range(1, peers):
        peer = (me + k) % peers
        copy = pltpu.make_async_remote_copy(
            src_ref=x_ref.at[pl.ds(pl.multiple_of(peer * rows, rows), rows)],
            dst_ref=parts.at[me],
            send_sem=send_a.at[peer],
            recv_sem=recv_a.at[me],
            device_id=here(peer),
            device_id_type=MESH,
        )
        copy.start()
        scatter.append(copy)
    own = x_ref[pl.ds(pl.multiple_of(me * rows, rows), rows), :]
    for k in range(1, peers):
        src = (me + peers - k) % peers
        pltpu.make_async_remote_copy(
            src_ref=x_ref.at[pl.ds(0, rows)],
            dst_ref=parts.at[src],
            send_sem=send_a.at[src],
            recv_sem=recv_a.at[src],
            device_id=here(src),
            device_id_type=MESH,
        ).wait_recv()
    for copy in scatter:
        copy.wait_send()
    parts[me] = own
    total = parts[0]
    for src in range(1, peers):
        total = total + parts[src]
    out_ref[pl.ds(pl.multiple_of(me * rows, rows), rows), :] = total
    gather = []
    for k in range(1, peers):
        peer = (me + k) % peers
        copy = pltpu.make_async_remote_copy(
            src_ref=out_ref.at[pl.ds(pl.multiple_of(me * rows, rows), rows)],
            dst_ref=out_ref.at[pl.ds(pl.multiple_of(me * rows, rows), rows)],
            send_sem=send_b.at[peer],
            recv_sem=recv_b.at[me],
            device_id=here(peer),
            device_id_type=MESH,
        )
        copy.start()
        gather.append(copy)
    for k in range(1, peers):
        src = (me + peers - k) % peers
        pltpu.make_async_remote_copy(
            src_ref=out_ref.at[pl.ds(pl.multiple_of(src * rows, rows), rows)],
            dst_ref=out_ref.at[pl.ds(pl.multiple_of(src * rows, rows), rows)],
            send_sem=send_b.at[src],
            recv_sem=recv_b.at[src],
            device_id=here(src),
            device_id_type=MESH,
        ).wait_recv()
    for copy in gather:
        copy.wait_send()


def freq_psum(x, peers):
    rows, cols = x.shape
    return pl.pallas_call(
        functools.partial(_psum_kernel, peers),
        out_shape=jax.ShapeDtypeStruct((rows, cols), x.dtype),
        in_specs=[pl.BlockSpec(memory_space=pltpu.VMEM)],
        out_specs=pl.BlockSpec(memory_space=pltpu.VMEM),
        scratch_shapes=[
            pltpu.VMEM((peers, rows // peers, cols), x.dtype),
            pltpu.SemaphoreType.DMA((peers,)),
            pltpu.SemaphoreType.DMA((peers,)),
            pltpu.SemaphoreType.DMA((peers,)),
            pltpu.SemaphoreType.DMA((peers,)),
        ],
        compiler_params=pltpu.CompilerParams(collective_id=0, has_side_effects=True),
    )(x)


def _gather_kernel(peers, x_ref, out_ref, send_sem, recv_sem):
    me = lax.axis_index("freq")
    grp = lax.axis_index("grp")

    def here(peer):
        return (grp, peer)

    _greet(peers, here)
    sent = []
    for k in range(1, peers):
        peer = (me + k) % peers
        copy = pltpu.make_async_remote_copy(
            src_ref=x_ref,
            dst_ref=out_ref.at[me],
            send_sem=send_sem.at[peer],
            recv_sem=recv_sem.at[me],
            device_id=here(peer),
            device_id_type=MESH,
        )
        copy.start()
        sent.append(copy)
    out_ref[me] = x_ref[...]
    for k in range(1, peers):
        src = (me + peers - k) % peers
        pltpu.make_async_remote_copy(
            src_ref=x_ref,
            dst_ref=out_ref.at[src],
            send_sem=send_sem.at[src],
            recv_sem=recv_sem.at[src],
            device_id=here(src),
            device_id_type=MESH,
        ).wait_recv()
    for copy in sent:
        copy.wait_send()


def freq_gather(x, peers):
    return pl.pallas_call(
        functools.partial(_gather_kernel, peers),
        out_shape=jax.ShapeDtypeStruct((peers, *x.shape), x.dtype),
        in_specs=[pl.BlockSpec(memory_space=pltpu.VMEM)],
        out_specs=pl.BlockSpec(memory_space=pltpu.VMEM),
        scratch_shapes=[
            pltpu.SemaphoreType.DMA((peers,)),
            pltpu.SemaphoreType.DMA((peers,)),
        ],
        compiler_params=pltpu.CompilerParams(collective_id=1, has_side_effects=True),
    )(x)


def _rows_kernel(chips, x_ref, out_ref, pair, held, send_sem, recv_sem):
    me = lax.axis_index("grp")
    band = lax.axis_index("freq")
    core = me % 2
    chip = me // 2
    partner = me + 1 - 2 * core

    def dev(g):
        return (g, band)

    barrier = pltpu.get_barrier_semaphore()
    pl.semaphore_signal(barrier, inc=1, device_id=dev(partner), device_id_type=MESH)
    for k in range(1, chips):
        pl.semaphore_signal(barrier, inc=1, device_id=dev(((chip + k) % chips) * 2 + core), device_id_type=MESH)
    pl.semaphore_wait(barrier, chips)

    first = pltpu.make_async_remote_copy(
        src_ref=x_ref, dst_ref=pair, send_sem=send_sem.at[0], recv_sem=recv_sem.at[0],
        device_id=dev(partner), device_id_type=MESH,
    )
    first.start()
    first.wait_recv()
    first.wait_send()
    held[chip] = (x_ref[...].astype(jnp.float32) + pair[...].astype(jnp.float32)).astype(held.dtype)
    sent = []
    for k in range(1, chips):
        peer = (chip + k) % chips
        copy = pltpu.make_async_remote_copy(
            src_ref=held.at[chip], dst_ref=held.at[chip], send_sem=send_sem.at[1 + peer],
            recv_sem=recv_sem.at[1 + chip], device_id=dev(peer * 2 + core), device_id_type=MESH,
        )
        copy.start()
        sent.append(copy)
    for k in range(1, chips):
        src = (chip + chips - k) % chips
        pltpu.make_async_remote_copy(
            src_ref=held.at[src], dst_ref=held.at[src], send_sem=send_sem.at[1 + src],
            recv_sem=recv_sem.at[1 + src], device_id=dev(src * 2 + core), device_id_type=MESH,
        ).wait_recv()
    for copy in sent:
        copy.wait_send()
    total = held[0].astype(jnp.float32)
    for c in range(1, chips):
        total = total + held[c].astype(jnp.float32)
    out_ref[...] = total.astype(out_ref.dtype)


def grp_rows_sum(x, chips):
    return pl.pallas_call(
        functools.partial(_rows_kernel, chips),
        out_shape=jax.ShapeDtypeStruct(x.shape, x.dtype),
        in_specs=[pl.BlockSpec(memory_space=pltpu.VMEM)],
        out_specs=pl.BlockSpec(memory_space=pltpu.VMEM),
        scratch_shapes=[
            pltpu.VMEM(x.shape, x.dtype),
            pltpu.VMEM((chips, *x.shape), x.dtype),
            pltpu.SemaphoreType.DMA((chips + 1,)),
            pltpu.SemaphoreType.DMA((chips + 1,)),
        ],
        compiler_params=pltpu.CompilerParams(collective_id=2, has_side_effects=True),
    )(x)


def _cross_kernel(zs, bands, scaling, x_ref, left_ref, sel_ref, cross_ref, bins_ref, held, stage, picked,
                  send_sem, recv_ring, recv_x, recv_sib, out_sem, recv_f):
    me = lax.axis_index("grp")
    band = lax.axis_index("freq")
    c = me % 2
    xl = (me // 2) % 2
    z = me // 4
    step = 1 - 2 * c
    width = x_ref.shape[0]
    half = width // 2

    def blk(zz, xx, cc):
        return (zz * 2 + xx) * 2 + cc

    def dev(g):
        return (g, band)

    sib = blk(z, xl, 1 - c)
    partner = blk(z, 1 - xl, c)
    nxt = blk((z + step + zs) % zs, xl, c)
    prv = blk((z - step + zs) % zs, xl, c)

    barrier = pltpu.get_barrier_semaphore()
    for g in (sib, partner, nxt, prv):
        pl.semaphore_signal(barrier, inc=1, device_id=dev(g), device_id_type=MESH)
    for k in range(1, bands):
        pl.semaphore_signal(barrier, inc=1, device_id=(me, (band + k) % bands), device_id_type=MESH)
    pl.semaphore_wait(barrier, 4 + bands - 1)

    sends = []
    outs = []

    def send(src, dst, recv, g):
        copy = pltpu.make_async_remote_copy(
            src_ref=src, dst_ref=dst, send_sem=send_sem.at[len(sends)], recv_sem=recv,
            device_id=dev(g), device_id_type=MESH,
        )
        copy.start()
        sends.append(copy)

    def wait(dst, recv, g):
        pltpu.make_async_remote_copy(
            src_ref=dst, dst_ref=dst, send_sem=send_sem.at[0], recv_sem=recv,
            device_id=dev(g), device_id_type=MESH,
        ).wait_recv()

    def rows(b, h):
        return held.at[b, pl.ds(pl.multiple_of(h * half, half), half)]

    def compute(b):
        block = held[b]
        prod = lax.dot_general(
            left_ref[...], block, (((1,), (1,)), ((), ())), preferred_element_type=jnp.float32
        )
        slot = len(outs) % 2
        if len(outs) >= 2:
            outs[-2].wait()
        stage[slot] = (prod * scaling).astype(stage.dtype).reshape(stage.shape[1:])
        copy = pltpu.make_async_copy(
            stage.at[slot], cross_ref.at[:, :, pl.ds(pl.multiple_of(b * width, width), width)], out_sem.at[slot]
        )
        copy.start()
        outs.append(copy)
        picked[...] += jnp.dot(
            sel_ref[:, pl.ds(pl.multiple_of(b * width, width), width)], block,
            preferred_element_type=jnp.float32,
        )

    picked[...] = jnp.zeros_like(picked)
    own = blk(z, xl, c)
    held[own] = x_ref[...]
    send(x_ref, held.at[own], recv_x.at[0], partner)
    send(x_ref, held.at[own], recv_sib.at[0], sib)
    send(x_ref.at[pl.ds(0, half)], rows(own, 0), recv_ring.at[0, 0], nxt)
    send(x_ref.at[pl.ds(half, half)], rows(own, 1), recv_ring.at[0, 1], nxt)
    compute(own)
    across = blk(z, 1 - xl, c)
    wait(held.at[across], recv_x.at[0], partner)
    send(rows(across, xl), rows(across, xl), recv_ring.at[0, 2], nxt)
    send(held.at[across], held.at[across], recv_sib.at[1], sib)
    compute(across)
    wait(held.at[sib], recv_sib.at[0], sib)
    compute(sib)
    sib_across = blk(z, 1 - xl, 1 - c)
    wait(held.at[sib_across], recv_sib.at[1], sib)
    compute(sib_across)
    for s in range(zs - 1):
        zo = (z - step * (s + 1) + 2 * zs) % zs
        full = blk(zo, xl, c)
        part = blk(zo, 1 - xl, c)
        pieces = ((full, 0), (full, 1), (part, xl))
        for k, (b, h) in enumerate(pieces):
            wait(rows(b, h), recv_ring.at[s, k], prv)
            if s < zs - 2:
                send(rows(b, h), rows(b, h), recv_ring.at[s + 1, k], nxt)
            send(rows(b, h), rows(b, h), recv_sib.at[2 + 3 * s + k], sib)
        send(rows(full, xl), rows(full, xl), recv_x.at[1 + s], partner)
        compute(full)
        wait(rows(part, 1 - xl), recv_x.at[1 + s], partner)
        send(rows(part, 1 - xl), rows(part, 1 - xl), recv_sib.at[2 + 3 * (zs - 1) + s], sib)
        compute(part)
        zt = (z + step * (s + 1) + 2 * zs) % zs
        sfull = blk(zt, xl, 1 - c)
        spart = blk(zt, 1 - xl, 1 - c)
        for k, (b, h) in enumerate(((sfull, 0), (sfull, 1), (spart, xl))):
            wait(rows(b, h), recv_sib.at[2 + 3 * s + k], sib)
        compute(sfull)
        wait(rows(spart, 1 - xl), recv_sib.at[2 + 3 * (zs - 1) + s], sib)
        compute(spart)
    station = picked[...]
    wide = station.shape[1] // 2
    swapped = jnp.concatenate([station[:, wide:], -station[:, :wide]], axis=1)
    left = jnp.concatenate([station, swapped], axis=0).astype(x_ref.dtype)
    values = lax.dot_general(
        left, x_ref[...], (((1,), (1,)), ((), ())), preferred_element_type=jnp.float32
    ) * scaling
    bins_ref[band] = values.reshape(bins_ref.shape[1:])
    for k in range(1, bands):
        peer = (band + k) % bands
        copy = pltpu.make_async_remote_copy(
            src_ref=bins_ref.at[band], dst_ref=bins_ref.at[band], send_sem=send_sem.at[len(sends)],
            recv_sem=recv_f.at[band], device_id=(me, peer), device_id_type=MESH,
        )
        copy.start()
        sends.append(copy)
    for k in range(1, bands):
        src = (band + bands - k) % bands
        pltpu.make_async_remote_copy(
            src_ref=bins_ref.at[src], dst_ref=bins_ref.at[src], send_sem=send_sem.at[0],
            recv_sem=recv_f.at[src], device_id=(me, src), device_id_type=MESH,
        ).wait_recv()
    for copy in outs[-2:]:
        copy.wait()
    for copy in sends:
        copy.wait_send()


def grp_cross(whitened, left, selector, scaling, zs):
    groups = lax.axis_size("grp")
    bands = lax.axis_size("freq")
    width, cols = whitened.shape
    return pl.pallas_call(
        functools.partial(_cross_kernel, zs, bands, scaling),
        out_shape=(
            jax.ShapeDtypeStruct((2, width, groups * width), whitened.dtype),
            jax.ShapeDtypeStruct((bands, 2, selector.shape[0], width), jnp.float32),
        ),
        in_specs=[pl.BlockSpec(memory_space=pltpu.VMEM)] * 3,
        out_specs=(pl.BlockSpec(memory_space=pl.ANY), pl.BlockSpec(memory_space=pltpu.VMEM)),
        scratch_shapes=[
            pltpu.VMEM((groups, width, cols), whitened.dtype),
            pltpu.VMEM((2, 2, width, width), whitened.dtype),
            pltpu.VMEM((selector.shape[0], cols), jnp.float32),
            pltpu.SemaphoreType.DMA((8 * zs + 16,)),
            pltpu.SemaphoreType.DMA((zs - 1, 3)),
            pltpu.SemaphoreType.DMA((zs,)),
            pltpu.SemaphoreType.DMA((2 + 4 * (zs - 1),)),
            pltpu.SemaphoreType.DMA((2,)),
            pltpu.SemaphoreType.DMA((bands,)),
        ],
        compiler_params=pltpu.CompilerParams(
            collective_id=3, has_side_effects=True, vmem_limit_bytes=56 * 1024 * 1024
        ),
    )(whitened, left, selector)


def on_device(spectra, valid, station_index):
    bin_count, chan_count, double_width = spectra.shape
    window_count = double_width // 2
    freq_count = lax.axis_size("freq")
    spectrum_f32 = spectra.astype(jnp.float32)
    real_part = spectrum_f32[..., :window_count]
    imag_part = spectrum_f32[..., window_count:]
    local_power = jnp.sum(real_part * real_part + imag_part * imag_part, axis=0)
    band_power = freq_psum(local_power, freq_count)
    total_bins = bin_count * freq_count
    factor = lax.rsqrt(band_power / total_bins + 1e-05) * valid.astype(jnp.float32)
    whitened = (spectrum_f32 * jnp.concatenate([factor, factor], axis=1)[None]).astype(jnp.bfloat16)
    swapped = jnp.concatenate([whitened[..., window_count:], -whitened[..., :window_count]], axis=2)
    stacked = jnp.concatenate([whitened, swapped], axis=1)
    scaling = 1.0 / math.sqrt(window_count)
    station_count = station_index.shape[0]
    total_chans = lax.axis_size("grp") * chan_count
    selector = (station_index[:, None] == jnp.arange(total_chans, dtype=jnp.int32)[None, :]).astype(
        jnp.bfloat16
    )
    cross, all_bins = grp_cross(
        whitened[0], stacked[0], selector, scaling, lax.axis_size("grp") // 4
    )
    cross = cross[None]

    lag_share = LAGS // freq_count
    freq_index = lax.axis_index("freq")
    bin_values = jnp.arange(total_bins, dtype=jnp.float32) + 1.0
    lag_values = (freq_index * lag_share + jnp.arange(lag_share, dtype=jnp.int32)).astype(jnp.float32)
    phase = math.pi * bin_values[:, None] * lag_values[None, :] / LAGS
    lag_table = jnp.stack([jnp.cos(phase), -jnp.sin(phase)], axis=1)
    station_gather = jnp.einsum(
        "frsc,frl->scl", all_bins, lag_table, precision=lax.Precision.HIGHEST
    ) / math.sqrt(total_bins)
    return (cross, station_gather)


def solution(mesh):
    placed = (P("freq", "grp", None), P("grp", None), P())
    return jax.shard_map(
        on_device,
        mesh=mesh,
        in_specs=placed,
        out_specs=(P("freq", None, "grp", None), P(None, "grp", "freq")),
        check_vma=False,
    )
```

```python
import functools
import math

import jax
import jax.numpy as jnp
from jax import lax
from jax.experimental import pallas as pl
from jax.experimental.pallas import tpu as pltpu
from jax.sharding import PartitionSpec as P

LAGS = 256
MESH = pl.DeviceIdType.MESH


def _greet(peers, here):
    barrier = pltpu.get_barrier_semaphore()
    for k in range(1, peers):
        pl.semaphore_signal(barrier, inc=1, device_id=here((lax.axis_index("freq") + k) % peers), device_id_type=MESH)
    pl.semaphore_wait(barrier, peers - 1)


def _psum_kernel(peers, x_ref, out_ref, parts, send_a, recv_a, send_b, recv_b):
    me = lax.axis_index("freq")
    grp = lax.axis_index("grp")
    rows = x_ref.shape[0] // peers

    def here(peer):
        return (grp, peer)

    _greet(peers, here)
    scatter = []
    for k in range(1, peers):
        peer = (me + k) % peers
        copy = pltpu.make_async_remote_copy(
            src_ref=x_ref.at[pl.ds(pl.multiple_of(peer * rows, rows), rows)],
            dst_ref=parts.at[me],
            send_sem=send_a.at[peer],
            recv_sem=recv_a.at[me],
            device_id=here(peer),
            device_id_type=MESH,
        )
        copy.start()
        scatter.append(copy)
    own = x_ref[pl.ds(pl.multiple_of(me * rows, rows), rows), :]
    for k in range(1, peers):
        src = (me + peers - k) % peers
        pltpu.make_async_remote_copy(
            src_ref=x_ref.at[pl.ds(0, rows)],
            dst_ref=parts.at[src],
            send_sem=send_a.at[src],
            recv_sem=recv_a.at[src],
            device_id=here(src),
            device_id_type=MESH,
        ).wait_recv()
    for copy in scatter:
        copy.wait_send()
    parts[me] = own
    total = parts[0]
    for src in range(1, peers):
        total = total + parts[src]
    out_ref[pl.ds(pl.multiple_of(me * rows, rows), rows), :] = total
    gather = []
    for k in range(1, peers):
        peer = (me + k) % peers
        copy = pltpu.make_async_remote_copy(
            src_ref=out_ref.at[pl.ds(pl.multiple_of(me * rows, rows), rows)],
            dst_ref=out_ref.at[pl.ds(pl.multiple_of(me * rows, rows), rows)],
            send_sem=send_b.at[peer],
            recv_sem=recv_b.at[me],
            device_id=here(peer),
            device_id_type=MESH,
        )
        copy.start()
        gather.append(copy)
    for k in range(1, peers):
        src = (me + peers - k) % peers
        pltpu.make_async_remote_copy(
            src_ref=out_ref.at[pl.ds(pl.multiple_of(src * rows, rows), rows)],
            dst_ref=out_ref.at[pl.ds(pl.multiple_of(src * rows, rows), rows)],
            send_sem=send_b.at[src],
            recv_sem=recv_b.at[src],
            device_id=here(src),
            device_id_type=MESH,
        ).wait_recv()
    for copy in gather:
        copy.wait_send()


def freq_psum(x, peers):
    rows, cols = x.shape
    return pl.pallas_call(
        functools.partial(_psum_kernel, peers),
        out_shape=jax.ShapeDtypeStruct((rows, cols), x.dtype),
        in_specs=[pl.BlockSpec(memory_space=pltpu.VMEM)],
        out_specs=pl.BlockSpec(memory_space=pltpu.VMEM),
        scratch_shapes=[
            pltpu.VMEM((peers, rows // peers, cols), x.dtype),
            pltpu.SemaphoreType.DMA((peers,)),
            pltpu.SemaphoreType.DMA((peers,)),
            pltpu.SemaphoreType.DMA((peers,)),
            pltpu.SemaphoreType.DMA((peers,)),
        ],
        compiler_params=pltpu.CompilerParams(collective_id=0, has_side_effects=True),
    )(x)


def _gather_kernel(peers, x_ref, out_ref, send_sem, recv_sem):
    me = lax.axis_index("freq")
    grp = lax.axis_index("grp")

    def here(peer):
        return (grp, peer)

    _greet(peers, here)
    sent = []
    for k in range(1, peers):
        peer = (me + k) % peers
        copy = pltpu.make_async_remote_copy(
            src_ref=x_ref,
            dst_ref=out_ref.at[me],
            send_sem=send_sem.at[peer],
            recv_sem=recv_sem.at[me],
            device_id=here(peer),
            device_id_type=MESH,
        )
        copy.start()
        sent.append(copy)
    out_ref[me] = x_ref[...]
    for k in range(1, peers):
        src = (me + peers - k) % peers
        pltpu.make_async_remote_copy(
            src_ref=x_ref,
            dst_ref=out_ref.at[src],
            send_sem=send_sem.at[src],
            recv_sem=recv_sem.at[src],
            device_id=here(src),
            device_id_type=MESH,
        ).wait_recv()
    for copy in sent:
        copy.wait_send()


def freq_gather(x, peers):
    return pl.pallas_call(
        functools.partial(_gather_kernel, peers),
        out_shape=jax.ShapeDtypeStruct((peers, *x.shape), x.dtype),
        in_specs=[pl.BlockSpec(memory_space=pltpu.VMEM)],
        out_specs=pl.BlockSpec(memory_space=pltpu.VMEM),
        scratch_shapes=[
            pltpu.SemaphoreType.DMA((peers,)),
            pltpu.SemaphoreType.DMA((peers,)),
        ],
        compiler_params=pltpu.CompilerParams(collective_id=1, has_side_effects=True),
    )(x)


def _rows_kernel(chips, x_ref, out_ref, pair, held, send_sem, recv_sem):
    me = lax.axis_index("grp")
    band = lax.axis_index("freq")
    core = me % 2
    chip = me // 2
    partner = me + 1 - 2 * core

    def dev(g):
        return (g, band)

    barrier = pltpu.get_barrier_semaphore()
    pl.semaphore_signal(barrier, inc=1, device_id=dev(partner), device_id_type=MESH)
    for k in range(1, chips):
        pl.semaphore_signal(barrier, inc=1, device_id=dev(((chip + k) % chips) * 2 + core), device_id_type=MESH)
    pl.semaphore_wait(barrier, chips)

    first = pltpu.make_async_remote_copy(
        src_ref=x_ref, dst_ref=pair, send_sem=send_sem.at[0], recv_sem=recv_sem.at[0],
        device_id=dev(partner), device_id_type=MESH,
    )
    first.start()
    first.wait_recv()
    first.wait_send()
    held[chip] = (x_ref[...].astype(jnp.float32) + pair[...].astype(jnp.float32)).astype(held.dtype)
    sent = []
    for k in range(1, chips):
        peer = (chip + k) % chips
        copy = pltpu.make_async_remote_copy(
            src_ref=held.at[chip], dst_ref=held.at[chip], send_sem=send_sem.at[1 + peer],
            recv_sem=recv_sem.at[1 + chip], device_id=dev(peer * 2 + core), device_id_type=MESH,
        )
        copy.start()
        sent.append(copy)
    for k in range(1, chips):
        src = (chip + chips - k) % chips
        pltpu.make_async_remote_copy(
            src_ref=held.at[src], dst_ref=held.at[src], send_sem=send_sem.at[1 + src],
            recv_sem=recv_sem.at[1 + src], device_id=dev(src * 2 + core), device_id_type=MESH,
        ).wait_recv()
    for copy in sent:
        copy.wait_send()
    total = held[0].astype(jnp.float32)
    for c in range(1, chips):
        total = total + held[c].astype(jnp.float32)
    out_ref[...] = total.astype(out_ref.dtype)


def grp_rows_sum(x, chips):
    return pl.pallas_call(
        functools.partial(_rows_kernel, chips),
        out_shape=jax.ShapeDtypeStruct(x.shape, x.dtype),
        in_specs=[pl.BlockSpec(memory_space=pltpu.VMEM)],
        out_specs=pl.BlockSpec(memory_space=pltpu.VMEM),
        scratch_shapes=[
            pltpu.VMEM(x.shape, x.dtype),
            pltpu.VMEM((chips, *x.shape), x.dtype),
            pltpu.SemaphoreType.DMA((chips + 1,)),
            pltpu.SemaphoreType.DMA((chips + 1,)),
        ],
        compiler_params=pltpu.CompilerParams(collective_id=2, has_side_effects=True),
    )(x)


def _cross_kernel(zs, bands, scaling, x_ref, left_ref, sel_ref, cross_ref, bins_ref, held, stage, picked,
                  send_sem, recv_ring, recv_x, recv_sib, out_sem, recv_f):
    me = lax.axis_index("grp")
    band = lax.axis_index("freq")
    c = me % 2
    xl = (me // 2) % 2
    z = me // 4
    step = 1 - 2 * c
    width = x_ref.shape[0]
    half = width // 2

    def blk(zz, xx, cc):
        return (zz * 2 + xx) * 2 + cc

    def dev(g):
        return (g, band)

    sib = blk(z, xl, 1 - c)
    partner = blk(z, 1 - xl, c)
    nxt = blk((z + step + zs) % zs, xl, c)
    prv = blk((z - step + zs) % zs, xl, c)

    barrier = pltpu.get_barrier_semaphore()
    for g in (sib, partner, nxt, prv):
        pl.semaphore_signal(barrier, inc=1, device_id=dev(g), device_id_type=MESH)
    for k in range(1, bands):
        pl.semaphore_signal(barrier, inc=1, device_id=(me, (band + k) % bands), device_id_type=MESH)
    pl.semaphore_wait(barrier, 4 + bands - 1)

    sends = []
    outs = []

    def send(src, dst, recv, g):
        copy = pltpu.make_async_remote_copy(
            src_ref=src, dst_ref=dst, send_sem=send_sem.at[len(sends)], recv_sem=recv,
            device_id=dev(g), device_id_type=MESH,
        )
        copy.start()
        sends.append(copy)

    def wait(dst, recv, g):
        pltpu.make_async_remote_copy(
            src_ref=dst, dst_ref=dst, send_sem=send_sem.at[0], recv_sem=recv,
            device_id=dev(g), device_id_type=MESH,
        ).wait_recv()

    def rows(b, h):
        return held.at[b, pl.ds(pl.multiple_of(h * half, half), half)]

    def compute(b):
        block = held[b]
        prod = lax.dot_general(
            left_ref[...], block, (((1,), (1,)), ((), ())), preferred_element_type=jnp.float32
        )
        slot = len(outs) % 2
        if len(outs) >= 2:
            outs[-2].wait()
        stage[slot] = (prod * scaling).astype(stage.dtype).reshape(stage.shape[1:])
        copy = pltpu.make_async_copy(
            stage.at[slot], cross_ref.at[:, :, pl.ds(pl.multiple_of(b * width, width), width)], out_sem.at[slot]
        )
        copy.start()
        outs.append(copy)
        picked[...] += jnp.dot(
            sel_ref[:, pl.ds(pl.multiple_of(b * width, width), width)], block,
            preferred_element_type=jnp.float32,
        )

    picked[...] = jnp.zeros_like(picked)
    own = blk(z, xl, c)
    held[own] = x_ref[...]
    send(x_ref, held.at[own], recv_x.at[0], partner)
    send(x_ref, held.at[own], recv_sib.at[0], sib)
    send(x_ref.at[pl.ds(0, half)], rows(own, 0), recv_ring.at[0, 0], nxt)
    send(x_ref.at[pl.ds(half, half)], rows(own, 1), recv_ring.at[0, 1], nxt)
    compute(own)
    across = blk(z, 1 - xl, c)
    wait(held.at[across], recv_x.at[0], partner)
    send(rows(across, xl), rows(across, xl), recv_ring.at[0, 2], nxt)
    send(held.at[across], held.at[across], recv_sib.at[1], sib)
    compute(across)

    def finish(t):
        zo = (z - step * (t + 1) + 2 * zs) % zs
        part = blk(zo, 1 - xl, c)
        wait(rows(part, 1 - xl), recv_x.at[1 + t], partner)
        send(rows(part, 1 - xl), rows(part, 1 - xl), recv_sib.at[2 + 3 * (zs - 1) + t], sib)
        compute(part)
        zt = (z + step * (t + 1) + 2 * zs) % zs
        sfull = blk(zt, xl, 1 - c)
        spart = blk(zt, 1 - xl, 1 - c)
        for k, (b, h) in enumerate(((sfull, 0), (sfull, 1), (spart, xl))):
            wait(rows(b, h), recv_sib.at[2 + 3 * t + k], sib)
        compute(sfull)
        wait(rows(spart, 1 - xl), recv_sib.at[2 + 3 * (zs - 1) + t], sib)
        compute(spart)

    for s in range(zs - 1):
        zo = (z - step * (s + 1) + 2 * zs) % zs
        full = blk(zo, xl, c)
        part = blk(zo, 1 - xl, c)
        pieces = ((full, 0), (full, 1), (part, xl))
        for k, (b, h) in enumerate(pieces):
            wait(rows(b, h), recv_ring.at[s, k], prv)
            if s < zs - 2:
                send(rows(b, h), rows(b, h), recv_ring.at[s + 1, k], nxt)
            send(rows(b, h), rows(b, h), recv_sib.at[2 + 3 * s + k], sib)
        send(rows(full, xl), rows(full, xl), recv_x.at[1 + s], partner)
        compute(full)
        if s == 0:
            wait(held.at[sib], recv_sib.at[0], sib)
            compute(sib)
            sib_across = blk(z, 1 - xl, 1 - c)
            wait(held.at[sib_across], recv_sib.at[1], sib)
            compute(sib_across)
        else:
            finish(s - 1)
    finish(zs - 2)
    station = picked[...]
    wide = station.shape[1] // 2
    swapped = jnp.concatenate([station[:, wide:], -station[:, :wide]], axis=1)
    left = jnp.concatenate([station, swapped], axis=0).astype(x_ref.dtype)
    values = lax.dot_general(
        left, x_ref[...], (((1,), (1,)), ((), ())), preferred_element_type=jnp.float32
    ) * scaling
    bins_ref[band] = values.reshape(bins_ref.shape[1:])
    for k in range(1, bands):
        peer = (band + k) % bands
        copy = pltpu.make_async_remote_copy(
            src_ref=bins_ref.at[band], dst_ref=bins_ref.at[band], send_sem=send_sem.at[len(sends)],
            recv_sem=recv_f.at[band], device_id=(me, peer), device_id_type=MESH,
        )
        copy.start()
        sends.append(copy)
    for k in range(1, bands):
        src = (band + bands - k) % bands
        pltpu.make_async_remote_copy(
            src_ref=bins_ref.at[src], dst_ref=bins_ref.at[src], send_sem=send_sem.at[0],
            recv_sem=recv_f.at[src], device_id=(me, src), device_id_type=MESH,
        ).wait_recv()
    for copy in outs[-2:]:
        copy.wait()
    for copy in sends:
        copy.wait_send()


def grp_cross(whitened, left, selector, scaling, zs):
    groups = lax.axis_size("grp")
    bands = lax.axis_size("freq")
    width, cols = whitened.shape
    return pl.pallas_call(
        functools.partial(_cross_kernel, zs, bands, scaling),
        out_shape=(
            jax.ShapeDtypeStruct((2, width, groups * width), whitened.dtype),
            jax.ShapeDtypeStruct((bands, 2, selector.shape[0], width), jnp.float32),
        ),
        in_specs=[pl.BlockSpec(memory_space=pltpu.VMEM)] * 3,
        out_specs=(pl.BlockSpec(memory_space=pl.ANY), pl.BlockSpec(memory_space=pltpu.VMEM)),
        scratch_shapes=[
            pltpu.VMEM((groups, width, cols), whitened.dtype),
            pltpu.VMEM((2, 2, width, width), whitened.dtype),
            pltpu.VMEM((selector.shape[0], cols), jnp.float32),
            pltpu.SemaphoreType.DMA((8 * zs + 16,)),
            pltpu.SemaphoreType.DMA((zs - 1, 3)),
            pltpu.SemaphoreType.DMA((zs,)),
            pltpu.SemaphoreType.DMA((2 + 4 * (zs - 1),)),
            pltpu.SemaphoreType.DMA((2,)),
            pltpu.SemaphoreType.DMA((bands,)),
        ],
        compiler_params=pltpu.CompilerParams(
            collective_id=3, has_side_effects=True, vmem_limit_bytes=56 * 1024 * 1024
        ),
    )(whitened, left, selector)


def on_device(spectra, valid, station_index):
    bin_count, chan_count, double_width = spectra.shape
    window_count = double_width // 2
    freq_count = lax.axis_size("freq")
    spectrum_f32 = spectra.astype(jnp.float32)
    real_part = spectrum_f32[..., :window_count]
    imag_part = spectrum_f32[..., window_count:]
    local_power = jnp.sum(real_part * real_part + imag_part * imag_part, axis=0)
    band_power = freq_psum(local_power, freq_count)
    total_bins = bin_count * freq_count
    factor = lax.rsqrt(band_power / total_bins + 1e-05) * valid.astype(jnp.float32)
    whitened = (spectrum_f32 * jnp.concatenate([factor, factor], axis=1)[None]).astype(jnp.bfloat16)
    swapped = jnp.concatenate([whitened[..., window_count:], -whitened[..., :window_count]], axis=2)
    stacked = jnp.concatenate([whitened, swapped], axis=1)
    scaling = 1.0 / math.sqrt(window_count)
    station_count = station_index.shape[0]
    total_chans = lax.axis_size("grp") * chan_count
    selector = (station_index[:, None] == jnp.arange(total_chans, dtype=jnp.int32)[None, :]).astype(
        jnp.bfloat16
    )
    cross, all_bins = grp_cross(
        whitened[0], stacked[0], selector, scaling, lax.axis_size("grp") // 4
    )
    cross = cross[None]

    lag_share = LAGS // freq_count
    freq_index = lax.axis_index("freq")
    bin_values = jnp.arange(total_bins, dtype=jnp.float32) + 1.0
    lag_values = (freq_index * lag_share + jnp.arange(lag_share, dtype=jnp.int32)).astype(jnp.float32)
    phase = math.pi * bin_values[:, None] * lag_values[None, :] / LAGS
    lag_table = jnp.stack([jnp.cos(phase), -jnp.sin(phase)], axis=1)
    station_gather = jnp.einsum(
        "frsc,frl->scl", all_bins, lag_table, precision=lax.Precision.HIGHEST
    ) / math.sqrt(total_bins)
    return (cross, station_gather)


def solution(mesh):
    placed = (P("freq", "grp", None), P("grp", None), P())
    return jax.shard_map(
        on_device,
        mesh=mesh,
        in_specs=placed,
        out_specs=(P("freq", None, "grp", None), P(None, "grp", "freq")),
        check_vma=False,
    )
```

```python
import functools
import math

import jax
import jax.numpy as jnp
from jax import lax
from jax.experimental import pallas as pl
from jax.experimental.pallas import tpu as pltpu
from jax.sharding import PartitionSpec as P

LAGS = 256
SPLIT = 4
MESH = pl.DeviceIdType.MESH


def _greet(peers, here):
    barrier = pltpu.get_barrier_semaphore()
    for k in range(1, peers):
        pl.semaphore_signal(barrier, inc=1, device_id=here((lax.axis_index("freq") + k) % peers), device_id_type=MESH)
    pl.semaphore_wait(barrier, peers - 1)


def _psum_kernel(peers, x_ref, out_ref, parts, send_a, recv_a, send_b, recv_b):
    me = lax.axis_index("freq")
    grp = lax.axis_index("grp")
    rows = x_ref.shape[0] // peers

    def here(peer):
        return (grp, peer)

    _greet(peers, here)
    scatter = []
    for k in range(1, peers):
        peer = (me + k) % peers
        copy = pltpu.make_async_remote_copy(
            src_ref=x_ref.at[pl.ds(pl.multiple_of(peer * rows, rows), rows)],
            dst_ref=parts.at[me],
            send_sem=send_a.at[peer],
            recv_sem=recv_a.at[me],
            device_id=here(peer),
            device_id_type=MESH,
        )
        copy.start()
        scatter.append(copy)
    own = x_ref[pl.ds(pl.multiple_of(me * rows, rows), rows), :]
    for k in range(1, peers):
        src = (me + peers - k) % peers
        pltpu.make_async_remote_copy(
            src_ref=x_ref.at[pl.ds(0, rows)],
            dst_ref=parts.at[src],
            send_sem=send_a.at[src],
            recv_sem=recv_a.at[src],
            device_id=here(src),
            device_id_type=MESH,
        ).wait_recv()
    for copy in scatter:
        copy.wait_send()
    parts[me] = own
    total = parts[0]
    for src in range(1, peers):
        total = total + parts[src]
    out_ref[pl.ds(pl.multiple_of(me * rows, rows), rows), :] = total
    gather = []
    for k in range(1, peers):
        peer = (me + k) % peers
        copy = pltpu.make_async_remote_copy(
            src_ref=out_ref.at[pl.ds(pl.multiple_of(me * rows, rows), rows)],
            dst_ref=out_ref.at[pl.ds(pl.multiple_of(me * rows, rows), rows)],
            send_sem=send_b.at[peer],
            recv_sem=recv_b.at[me],
            device_id=here(peer),
            device_id_type=MESH,
        )
        copy.start()
        gather.append(copy)
    for k in range(1, peers):
        src = (me + peers - k) % peers
        pltpu.make_async_remote_copy(
            src_ref=out_ref.at[pl.ds(pl.multiple_of(src * rows, rows), rows)],
            dst_ref=out_ref.at[pl.ds(pl.multiple_of(src * rows, rows), rows)],
            send_sem=send_b.at[src],
            recv_sem=recv_b.at[src],
            device_id=here(src),
            device_id_type=MESH,
        ).wait_recv()
    for copy in gather:
        copy.wait_send()


def freq_psum(x, peers):
    rows, cols = x.shape
    return pl.pallas_call(
        functools.partial(_psum_kernel, peers),
        out_shape=jax.ShapeDtypeStruct((rows, cols), x.dtype),
        in_specs=[pl.BlockSpec(memory_space=pltpu.VMEM)],
        out_specs=pl.BlockSpec(memory_space=pltpu.VMEM),
        scratch_shapes=[
            pltpu.VMEM((peers, rows // peers, cols), x.dtype),
            pltpu.SemaphoreType.DMA((peers,)),
            pltpu.SemaphoreType.DMA((peers,)),
            pltpu.SemaphoreType.DMA((peers,)),
            pltpu.SemaphoreType.DMA((peers,)),
        ],
        compiler_params=pltpu.CompilerParams(collective_id=0, has_side_effects=True),
    )(x)


def _gather_kernel(peers, x_ref, out_ref, send_sem, recv_sem):
    me = lax.axis_index("freq")
    grp = lax.axis_index("grp")

    def here(peer):
        return (grp, peer)

    _greet(peers, here)
    sent = []
    for k in range(1, peers):
        peer = (me + k) % peers
        copy = pltpu.make_async_remote_copy(
            src_ref=x_ref,
            dst_ref=out_ref.at[me],
            send_sem=send_sem.at[peer],
            recv_sem=recv_sem.at[me],
            device_id=here(peer),
            device_id_type=MESH,
        )
        copy.start()
        sent.append(copy)
    out_ref[me] = x_ref[...]
    for k in range(1, peers):
        src = (me + peers - k) % peers
        pltpu.make_async_remote_copy(
            src_ref=x_ref,
            dst_ref=out_ref.at[src],
            send_sem=send_sem.at[src],
            recv_sem=recv_sem.at[src],
            device_id=here(src),
            device_id_type=MESH,
        ).wait_recv()
    for copy in sent:
        copy.wait_send()


def freq_gather(x, peers):
    return pl.pallas_call(
        functools.partial(_gather_kernel, peers),
        out_shape=jax.ShapeDtypeStruct((peers, *x.shape), x.dtype),
        in_specs=[pl.BlockSpec(memory_space=pltpu.VMEM)],
        out_specs=pl.BlockSpec(memory_space=pltpu.VMEM),
        scratch_shapes=[
            pltpu.SemaphoreType.DMA((peers,)),
            pltpu.SemaphoreType.DMA((peers,)),
        ],
        compiler_params=pltpu.CompilerParams(collective_id=1, has_side_effects=True),
    )(x)


def _rows_kernel(chips, x_ref, out_ref, pair, held, send_sem, recv_sem):
    me = lax.axis_index("grp")
    band = lax.axis_index("freq")
    core = me % 2
    chip = me // 2
    partner = me + 1 - 2 * core

    def dev(g):
        return (g, band)

    barrier = pltpu.get_barrier_semaphore()
    pl.semaphore_signal(barrier, inc=1, device_id=dev(partner), device_id_type=MESH)
    for k in range(1, chips):
        pl.semaphore_signal(barrier, inc=1, device_id=dev(((chip + k) % chips) * 2 + core), device_id_type=MESH)
    pl.semaphore_wait(barrier, chips)

    first = pltpu.make_async_remote_copy(
        src_ref=x_ref, dst_ref=pair, send_sem=send_sem.at[0], recv_sem=recv_sem.at[0],
        device_id=dev(partner), device_id_type=MESH,
    )
    first.start()
    first.wait_recv()
    first.wait_send()
    held[chip] = (x_ref[...].astype(jnp.float32) + pair[...].astype(jnp.float32)).astype(held.dtype)
    sent = []
    for k in range(1, chips):
        peer = (chip + k) % chips
        copy = pltpu.make_async_remote_copy(
            src_ref=held.at[chip], dst_ref=held.at[chip], send_sem=send_sem.at[1 + peer],
            recv_sem=recv_sem.at[1 + chip], device_id=dev(peer * 2 + core), device_id_type=MESH,
        )
        copy.start()
        sent.append(copy)
    for k in range(1, chips):
        src = (chip + chips - k) % chips
        pltpu.make_async_remote_copy(
            src_ref=held.at[src], dst_ref=held.at[src], send_sem=send_sem.at[1 + src],
            recv_sem=recv_sem.at[1 + src], device_id=dev(src * 2 + core), device_id_type=MESH,
        ).wait_recv()
    for copy in sent:
        copy.wait_send()
    total = held[0].astype(jnp.float32)
    for c in range(1, chips):
        total = total + held[c].astype(jnp.float32)
    out_ref[...] = total.astype(out_ref.dtype)


def grp_rows_sum(x, chips):
    return pl.pallas_call(
        functools.partial(_rows_kernel, chips),
        out_shape=jax.ShapeDtypeStruct(x.shape, x.dtype),
        in_specs=[pl.BlockSpec(memory_space=pltpu.VMEM)],
        out_specs=pl.BlockSpec(memory_space=pltpu.VMEM),
        scratch_shapes=[
            pltpu.VMEM(x.shape, x.dtype),
            pltpu.VMEM((chips, *x.shape), x.dtype),
            pltpu.SemaphoreType.DMA((chips + 1,)),
            pltpu.SemaphoreType.DMA((chips + 1,)),
        ],
        compiler_params=pltpu.CompilerParams(collective_id=2, has_side_effects=True),
    )(x)


def _cross_kernel(zs, split, bands, scaling, x_ref, left_ref, sel_ref, cross_ref, bins_ref, held, stage, picked,
                  send_sem, recv_ring, recv_x, recv_sib, out_sem, recv_f):
    me = lax.axis_index("grp")
    band = lax.axis_index("freq")
    c = me % 2
    xl = (me // 2) % 2
    z = me // 4
    step = 1 - 2 * c
    width = x_ref.shape[0]
    half = width // 2

    def blk(zz, xx, cc):
        return (zz * 2 + xx) * 2 + cc

    def dev(g):
        return (g, band)

    sib = blk(z, xl, 1 - c)
    partner = blk(z, 1 - xl, c)
    nxt = blk((z + step + zs) % zs, xl, c)
    prv = blk((z - step + zs) % zs, xl, c)

    barrier = pltpu.get_barrier_semaphore()
    for g in (sib, partner, nxt, prv):
        pl.semaphore_signal(barrier, inc=1, device_id=dev(g), device_id_type=MESH)
    for k in range(1, bands):
        pl.semaphore_signal(barrier, inc=1, device_id=(me, (band + k) % bands), device_id_type=MESH)
    pl.semaphore_wait(barrier, 4 + bands - 1)

    sends = []
    outs = []

    def send(src, dst, recv, g):
        copy = pltpu.make_async_remote_copy(
            src_ref=src, dst_ref=dst, send_sem=send_sem.at[len(sends)], recv_sem=recv,
            device_id=dev(g), device_id_type=MESH,
        )
        copy.start()
        sends.append(copy)

    def wait(dst, recv, g):
        pltpu.make_async_remote_copy(
            src_ref=dst, dst_ref=dst, send_sem=send_sem.at[0], recv_sem=recv,
            device_id=dev(g), device_id_type=MESH,
        ).wait_recv()

    def rows(b, h):
        return held.at[b, pl.ds(pl.multiple_of(h * half, half), half)]

    piece = width // split

    def bit(b, i):
        return held.at[b, pl.ds(pl.multiple_of(i * piece, piece), piece)]

    def ring_pieces(full, part, x_of):
        return [(full, i) for i in range(split)] + [(part, x_of * (split // 2) + j) for j in range(split // 2)]

    count = split + split // 2

    def compute(b):
        block = held[b]
        prod = lax.dot_general(
            left_ref[...], block, (((1,), (1,)), ((), ())), preferred_element_type=jnp.float32
        )
        slot = len(outs) % 2
        if len(outs) >= 2:
            outs[-2].wait()
        stage[slot] = (prod * scaling).astype(stage.dtype).reshape(stage.shape[1:])
        copy = pltpu.make_async_copy(
            stage.at[slot], cross_ref.at[:, :, pl.ds(pl.multiple_of(b * width, width), width)], out_sem.at[slot]
        )
        copy.start()
        outs.append(copy)
        picked[...] += jnp.dot(
            sel_ref[:, pl.ds(pl.multiple_of(b * width, width), width)], block,
            preferred_element_type=jnp.float32,
        )

    picked[...] = jnp.zeros_like(picked)
    own = blk(z, xl, c)
    held[own] = x_ref[...]
    send(x_ref, held.at[own], recv_x.at[0], partner)
    send(x_ref, held.at[own], recv_sib.at[0], sib)
    for i in range(split):
        send(x_ref.at[pl.ds(i * piece, piece)], bit(own, i), recv_ring.at[0, i], nxt)
    compute(own)
    across = blk(z, 1 - xl, c)
    wait(held.at[across], recv_x.at[0], partner)
    for j in range(split // 2):
        b, i = across, xl * (split // 2) + j
        send(bit(b, i), bit(b, i), recv_ring.at[0, split + j], nxt)
    send(held.at[across], held.at[across], recv_sib.at[1], sib)
    compute(across)

    def finish(t):
        zo = (z - step * (t + 1) + 2 * zs) % zs
        part = blk(zo, 1 - xl, c)
        wait(rows(part, 1 - xl), recv_x.at[1 + t], partner)
        send(rows(part, 1 - xl), rows(part, 1 - xl), recv_sib.at[2 + count * (zs - 1) + t], sib)
        compute(part)
        zt = (z + step * (t + 1) + 2 * zs) % zs
        sfull = blk(zt, xl, 1 - c)
        spart = blk(zt, 1 - xl, 1 - c)
        for k, (b, i) in enumerate(ring_pieces(sfull, spart, xl)):
            wait(bit(b, i), recv_sib.at[2 + count * t + k], sib)
        compute(sfull)
        wait(rows(spart, 1 - xl), recv_sib.at[2 + count * (zs - 1) + t], sib)
        compute(spart)

    for s in range(zs - 1):
        zo = (z - step * (s + 1) + 2 * zs) % zs
        full = blk(zo, xl, c)
        part = blk(zo, 1 - xl, c)
        for k, (b, i) in enumerate(ring_pieces(full, part, xl)):
            wait(bit(b, i), recv_ring.at[s, k], prv)
            if s < zs - 2:
                send(bit(b, i), bit(b, i), recv_ring.at[s + 1, k], nxt)
            send(bit(b, i), bit(b, i), recv_sib.at[2 + count * s + k], sib)
        send(rows(full, xl), rows(full, xl), recv_x.at[1 + s], partner)
        compute(full)
        if s == 0:
            wait(held.at[sib], recv_sib.at[0], sib)
            compute(sib)
            sib_across = blk(z, 1 - xl, 1 - c)
            wait(held.at[sib_across], recv_sib.at[1], sib)
            compute(sib_across)
        else:
            finish(s - 1)
    finish(zs - 2)
    station = picked[...]
    wide = station.shape[1] // 2
    swapped = jnp.concatenate([station[:, wide:], -station[:, :wide]], axis=1)
    left = jnp.concatenate([station, swapped], axis=0).astype(x_ref.dtype)
    values = lax.dot_general(
        left, x_ref[...], (((1,), (1,)), ((), ())), preferred_element_type=jnp.float32
    ) * scaling
    bins_ref[band] = values.reshape(bins_ref.shape[1:])
    for k in range(1, bands):
        peer = (band + k) % bands
        copy = pltpu.make_async_remote_copy(
            src_ref=bins_ref.at[band], dst_ref=bins_ref.at[band], send_sem=send_sem.at[len(sends)],
            recv_sem=recv_f.at[band], device_id=(me, peer), device_id_type=MESH,
        )
        copy.start()
        sends.append(copy)
    for k in range(1, bands):
        src = (band + bands - k) % bands
        pltpu.make_async_remote_copy(
            src_ref=bins_ref.at[src], dst_ref=bins_ref.at[src], send_sem=send_sem.at[0],
            recv_sem=recv_f.at[src], device_id=(me, src), device_id_type=MESH,
        ).wait_recv()
    for copy in outs[-2:]:
        copy.wait()
    for copy in sends:
        copy.wait_send()


def grp_cross(whitened, left, selector, scaling, zs):
    groups = lax.axis_size("grp")
    bands = lax.axis_size("freq")
    width, cols = whitened.shape
    return pl.pallas_call(
        functools.partial(_cross_kernel, zs, SPLIT, bands, scaling),
        out_shape=(
            jax.ShapeDtypeStruct((2, width, groups * width), whitened.dtype),
            jax.ShapeDtypeStruct((bands, 2, selector.shape[0], width), jnp.float32),
        ),
        in_specs=[pl.BlockSpec(memory_space=pltpu.VMEM)] * 3,
        out_specs=(pl.BlockSpec(memory_space=pl.ANY), pl.BlockSpec(memory_space=pltpu.VMEM)),
        scratch_shapes=[
            pltpu.VMEM((groups, width, cols), whitened.dtype),
            pltpu.VMEM((2, 2, width, width), whitened.dtype),
            pltpu.VMEM((selector.shape[0], cols), jnp.float32),
            pltpu.SemaphoreType.DMA((4 * SPLIT * zs + 16,)),
            pltpu.SemaphoreType.DMA((zs - 1, SPLIT + SPLIT // 2)),
            pltpu.SemaphoreType.DMA((zs,)),
            pltpu.SemaphoreType.DMA((2 + (SPLIT + SPLIT // 2 + 1) * (zs - 1),)),
            pltpu.SemaphoreType.DMA((2,)),
            pltpu.SemaphoreType.DMA((bands,)),
        ],
        compiler_params=pltpu.CompilerParams(
            collective_id=3, has_side_effects=True, vmem_limit_bytes=56 * 1024 * 1024
        ),
    )(whitened, left, selector)


def on_device(spectra, valid, station_index):
    bin_count, chan_count, double_width = spectra.shape
    window_count = double_width // 2
    freq_count = lax.axis_size("freq")
    spectrum_f32 = spectra.astype(jnp.float32)
    real_part = spectrum_f32[..., :window_count]
    imag_part = spectrum_f32[..., window_count:]
    local_power = jnp.sum(real_part * real_part + imag_part * imag_part, axis=0)
    band_power = freq_psum(local_power, freq_count)
    total_bins = bin_count * freq_count
    factor = lax.rsqrt(band_power / total_bins + 1e-05) * valid.astype(jnp.float32)
    whitened = (spectrum_f32 * jnp.concatenate([factor, factor], axis=1)[None]).astype(jnp.bfloat16)
    swapped = jnp.concatenate([whitened[..., window_count:], -whitened[..., :window_count]], axis=2)
    stacked = jnp.concatenate([whitened, swapped], axis=1)
    scaling = 1.0 / math.sqrt(window_count)
    station_count = station_index.shape[0]
    total_chans = lax.axis_size("grp") * chan_count
    selector = (station_index[:, None] == jnp.arange(total_chans, dtype=jnp.int32)[None, :]).astype(
        jnp.bfloat16
    )
    cross, all_bins = grp_cross(
        whitened[0], stacked[0], selector, scaling, lax.axis_size("grp") // 4
    )
    cross = cross[None]

    lag_share = LAGS // freq_count
    freq_index = lax.axis_index("freq")
    bin_values = jnp.arange(total_bins, dtype=jnp.float32) + 1.0
    lag_values = (freq_index * lag_share + jnp.arange(lag_share, dtype=jnp.int32)).astype(jnp.float32)
    phase = math.pi * bin_values[:, None] * lag_values[None, :] / LAGS
    lag_table = jnp.stack([jnp.cos(phase), -jnp.sin(phase)], axis=1)
    station_gather = jnp.einsum(
        "frsc,frl->scl", all_bins, lag_table, precision=lax.Precision.HIGHEST
    ) / math.sqrt(total_bins)
    return (cross, station_gather)


def solution(mesh):
    placed = (P("freq", "grp", None), P("grp", None), P())
    return jax.shard_map(
        on_device,
        mesh=mesh,
        in_specs=placed,
        out_specs=(P("freq", None, "grp", None), P(None, "grp", "freq")),
        check_vma=False,
    )
```

```python
import functools
import math

import jax
import jax.numpy as jnp
from jax import lax
from jax.experimental import pallas as pl
from jax.experimental.pallas import tpu as pltpu
from jax.sharding import PartitionSpec as P

LAGS = 256
MESH = pl.DeviceIdType.MESH


def _greet(peers, here):
    barrier = pltpu.get_barrier_semaphore()
    for k in range(1, peers):
        pl.semaphore_signal(barrier, inc=1, device_id=here((lax.axis_index("freq") + k) % peers), device_id_type=MESH)
    pl.semaphore_wait(barrier, peers - 1)


def _psum_kernel(peers, x_ref, out_ref, parts, send_a, recv_a, send_b, recv_b):
    me = lax.axis_index("freq")
    grp = lax.axis_index("grp")
    rows = x_ref.shape[0] // peers

    def here(peer):
        return (grp, peer)

    _greet(peers, here)
    scatter = []
    for k in range(1, peers):
        peer = (me + k) % peers
        copy = pltpu.make_async_remote_copy(
            src_ref=x_ref.at[pl.ds(pl.multiple_of(peer * rows, rows), rows)],
            dst_ref=parts.at[me],
            send_sem=send_a.at[peer],
            recv_sem=recv_a.at[me],
            device_id=here(peer),
            device_id_type=MESH,
        )
        copy.start()
        scatter.append(copy)
    own = x_ref[pl.ds(pl.multiple_of(me * rows, rows), rows), :]
    for k in range(1, peers):
        src = (me + peers - k) % peers
        pltpu.make_async_remote_copy(
            src_ref=x_ref.at[pl.ds(0, rows)],
            dst_ref=parts.at[src],
            send_sem=send_a.at[src],
            recv_sem=recv_a.at[src],
            device_id=here(src),
            device_id_type=MESH,
        ).wait_recv()
    for copy in scatter:
        copy.wait_send()
    parts[me] = own
    total = parts[0]
    for src in range(1, peers):
        total = total + parts[src]
    out_ref[pl.ds(pl.multiple_of(me * rows, rows), rows), :] = total
    gather = []
    for k in range(1, peers):
        peer = (me + k) % peers
        copy = pltpu.make_async_remote_copy(
            src_ref=out_ref.at[pl.ds(pl.multiple_of(me * rows, rows), rows)],
            dst_ref=out_ref.at[pl.ds(pl.multiple_of(me * rows, rows), rows)],
            send_sem=send_b.at[peer],
            recv_sem=recv_b.at[me],
            device_id=here(peer),
            device_id_type=MESH,
        )
        copy.start()
        gather.append(copy)
    for k in range(1, peers):
        src = (me + peers - k) % peers
        pltpu.make_async_remote_copy(
            src_ref=out_ref.at[pl.ds(pl.multiple_of(src * rows, rows), rows)],
            dst_ref=out_ref.at[pl.ds(pl.multiple_of(src * rows, rows), rows)],
            send_sem=send_b.at[src],
            recv_sem=recv_b.at[src],
            device_id=here(src),
            device_id_type=MESH,
        ).wait_recv()
    for copy in gather:
        copy.wait_send()


def freq_psum(x, peers):
    rows, cols = x.shape
    return pl.pallas_call(
        functools.partial(_psum_kernel, peers),
        out_shape=jax.ShapeDtypeStruct((rows, cols), x.dtype),
        in_specs=[pl.BlockSpec(memory_space=pltpu.VMEM)],
        out_specs=pl.BlockSpec(memory_space=pltpu.VMEM),
        scratch_shapes=[
            pltpu.VMEM((peers, rows // peers, cols), x.dtype),
            pltpu.SemaphoreType.DMA((peers,)),
            pltpu.SemaphoreType.DMA((peers,)),
            pltpu.SemaphoreType.DMA((peers,)),
            pltpu.SemaphoreType.DMA((peers,)),
        ],
        compiler_params=pltpu.CompilerParams(collective_id=0, has_side_effects=True),
    )(x)


def _gather_kernel(peers, x_ref, out_ref, send_sem, recv_sem):
    me = lax.axis_index("freq")
    grp = lax.axis_index("grp")

    def here(peer):
        return (grp, peer)

    _greet(peers, here)
    sent = []
    for k in range(1, peers):
        peer = (me + k) % peers
        copy = pltpu.make_async_remote_copy(
            src_ref=x_ref,
            dst_ref=out_ref.at[me],
            send_sem=send_sem.at[peer],
            recv_sem=recv_sem.at[me],
            device_id=here(peer),
            device_id_type=MESH,
        )
        copy.start()
        sent.append(copy)
    out_ref[me] = x_ref[...]
    for k in range(1, peers):
        src = (me + peers - k) % peers
        pltpu.make_async_remote_copy(
            src_ref=x_ref,
            dst_ref=out_ref.at[src],
            send_sem=send_sem.at[src],
            recv_sem=recv_sem.at[src],
            device_id=here(src),
            device_id_type=MESH,
        ).wait_recv()
    for copy in sent:
        copy.wait_send()


def freq_gather(x, peers):
    return pl.pallas_call(
        functools.partial(_gather_kernel, peers),
        out_shape=jax.ShapeDtypeStruct((peers, *x.shape), x.dtype),
        in_specs=[pl.BlockSpec(memory_space=pltpu.VMEM)],
        out_specs=pl.BlockSpec(memory_space=pltpu.VMEM),
        scratch_shapes=[
            pltpu.SemaphoreType.DMA((peers,)),
            pltpu.SemaphoreType.DMA((peers,)),
        ],
        compiler_params=pltpu.CompilerParams(collective_id=1, has_side_effects=True),
    )(x)


def _rows_kernel(chips, x_ref, out_ref, pair, held, send_sem, recv_sem):
    me = lax.axis_index("grp")
    band = lax.axis_index("freq")
    core = me % 2
    chip = me // 2
    partner = me + 1 - 2 * core

    def dev(g):
        return (g, band)

    barrier = pltpu.get_barrier_semaphore()
    pl.semaphore_signal(barrier, inc=1, device_id=dev(partner), device_id_type=MESH)
    for k in range(1, chips):
        pl.semaphore_signal(barrier, inc=1, device_id=dev(((chip + k) % chips) * 2 + core), device_id_type=MESH)
    pl.semaphore_wait(barrier, chips)

    first = pltpu.make_async_remote_copy(
        src_ref=x_ref, dst_ref=pair, send_sem=send_sem.at[0], recv_sem=recv_sem.at[0],
        device_id=dev(partner), device_id_type=MESH,
    )
    first.start()
    first.wait_recv()
    first.wait_send()
    held[chip] = (x_ref[...].astype(jnp.float32) + pair[...].astype(jnp.float32)).astype(held.dtype)
    sent = []
    for k in range(1, chips):
        peer = (chip + k) % chips
        copy = pltpu.make_async_remote_copy(
            src_ref=held.at[chip], dst_ref=held.at[chip], send_sem=send_sem.at[1 + peer],
            recv_sem=recv_sem.at[1 + chip], device_id=dev(peer * 2 + core), device_id_type=MESH,
        )
        copy.start()
        sent.append(copy)
    for k in range(1, chips):
        src = (chip + chips - k) % chips
        pltpu.make_async_remote_copy(
            src_ref=held.at[src], dst_ref=held.at[src], send_sem=send_sem.at[1 + src],
            recv_sem=recv_sem.at[1 + src], device_id=dev(src * 2 + core), device_id_type=MESH,
        ).wait_recv()
    for copy in sent:
        copy.wait_send()
    total = held[0].astype(jnp.float32)
    for c in range(1, chips):
        total = total + held[c].astype(jnp.float32)
    out_ref[...] = total.astype(out_ref.dtype)


def grp_rows_sum(x, chips):
    return pl.pallas_call(
        functools.partial(_rows_kernel, chips),
        out_shape=jax.ShapeDtypeStruct(x.shape, x.dtype),
        in_specs=[pl.BlockSpec(memory_space=pltpu.VMEM)],
        out_specs=pl.BlockSpec(memory_space=pltpu.VMEM),
        scratch_shapes=[
            pltpu.VMEM(x.shape, x.dtype),
            pltpu.VMEM((chips, *x.shape), x.dtype),
            pltpu.SemaphoreType.DMA((chips + 1,)),
            pltpu.SemaphoreType.DMA((chips + 1,)),
        ],
        compiler_params=pltpu.CompilerParams(collective_id=2, has_side_effects=True),
    )(x)


def _cross_kernel(zs, bands, scaling, x_ref, left_ref, sel_ref, cross_ref, bins_ref, held, picked,
                  send_sem, recv_ring, recv_x, recv_sib, recv_f):
    me = lax.axis_index("grp")
    band = lax.axis_index("freq")
    c = me % 2
    xl = (me // 2) % 2
    z = me // 4
    step = 1 - 2 * c
    width = x_ref.shape[0]
    half = width // 2

    def blk(zz, xx, cc):
        return (zz * 2 + xx) * 2 + cc

    def dev(g):
        return (g, band)

    sib = blk(z, xl, 1 - c)
    partner = blk(z, 1 - xl, c)
    nxt = blk((z + step + zs) % zs, xl, c)
    prv = blk((z - step + zs) % zs, xl, c)

    barrier = pltpu.get_barrier_semaphore()
    for g in (sib, partner, nxt, prv):
        pl.semaphore_signal(barrier, inc=1, device_id=dev(g), device_id_type=MESH)
    for k in range(1, bands):
        pl.semaphore_signal(barrier, inc=1, device_id=(me, (band + k) % bands), device_id_type=MESH)
    pl.semaphore_wait(barrier, 4 + bands - 1)

    sends = []

    def send(src, dst, recv, g):
        copy = pltpu.make_async_remote_copy(
            src_ref=src, dst_ref=dst, send_sem=send_sem.at[len(sends)], recv_sem=recv,
            device_id=dev(g), device_id_type=MESH,
        )
        copy.start()
        sends.append(copy)

    def wait(dst, recv, g):
        pltpu.make_async_remote_copy(
            src_ref=dst, dst_ref=dst, send_sem=send_sem.at[0], recv_sem=recv,
            device_id=dev(g), device_id_type=MESH,
        ).wait_recv()

    def rows(b, h):
        return held.at[b, pl.ds(pl.multiple_of(h * half, half), half)]

    def compute(b):
        block = held[b]
        prod = lax.dot_general(
            left_ref[...], block, (((1,), (1,)), ((), ())), preferred_element_type=jnp.float32
        )
        cross_ref[:, :, pl.ds(pl.multiple_of(b * width, width), width)] = (
            (prod * scaling).astype(cross_ref.dtype).reshape(2, width, width)
        )
        picked[...] += jnp.dot(
            sel_ref[:, pl.ds(pl.multiple_of(b * width, width), width)], block,
            preferred_element_type=jnp.float32,
        )

    picked[...] = jnp.zeros_like(picked)
    own = blk(z, xl, c)
    held[own] = x_ref[...]
    send(x_ref, held.at[own], recv_x.at[0], partner)
    send(x_ref, held.at[own], recv_sib.at[0], sib)
    send(x_ref.at[pl.ds(0, half)], rows(own, 0), recv_ring.at[0, 0], nxt)
    send(x_ref.at[pl.ds(half, half)], rows(own, 1), recv_ring.at[0, 1], nxt)
    compute(own)
    across = blk(z, 1 - xl, c)
    wait(held.at[across], recv_x.at[0], partner)
    send(rows(across, xl), rows(across, xl), recv_ring.at[0, 2], nxt)
    send(held.at[across], held.at[across], recv_sib.at[1], sib)
    compute(across)

    def finish(t):
        zo = (z - step * (t + 1) + 2 * zs) % zs
        part = blk(zo, 1 - xl, c)
        wait(rows(part, 1 - xl), recv_x.at[1 + t], partner)
        send(rows(part, 1 - xl), rows(part, 1 - xl), recv_sib.at[2 + 3 * (zs - 1) + t], sib)
        compute(part)
        zt = (z + step * (t + 1) + 2 * zs) % zs
        sfull = blk(zt, xl, 1 - c)
        spart = blk(zt, 1 - xl, 1 - c)
        for k, (b, h) in enumerate(((sfull, 0), (sfull, 1), (spart, xl))):
            wait(rows(b, h), recv_sib.at[2 + 3 * t + k], sib)
        compute(sfull)
        wait(rows(spart, 1 - xl), recv_sib.at[2 + 3 * (zs - 1) + t], sib)
        compute(spart)

    for s in range(zs - 1):
        zo = (z - step * (s + 1) + 2 * zs) % zs
        full = blk(zo, xl, c)
        part = blk(zo, 1 - xl, c)
        pieces = ((full, 0), (full, 1), (part, xl))
        for k, (b, h) in enumerate(pieces):
            wait(rows(b, h), recv_ring.at[s, k], prv)
            if s < zs - 2:
                send(rows(b, h), rows(b, h), recv_ring.at[s + 1, k], nxt)
            send(rows(b, h), rows(b, h), recv_sib.at[2 + 3 * s + k], sib)
        send(rows(full, xl), rows(full, xl), recv_x.at[1 + s], partner)
        compute(full)
        if s == 0:
            wait(held.at[sib], recv_sib.at[0], sib)
            compute(sib)
            sib_across = blk(z, 1 - xl, 1 - c)
            wait(held.at[sib_across], recv_sib.at[1], sib)
            compute(sib_across)
        else:
            finish(s - 1)
    finish(zs - 2)
    station = picked[...]
    wide = station.shape[1] // 2
    swapped = jnp.concatenate([station[:, wide:], -station[:, :wide]], axis=1)
    left = jnp.concatenate([station, swapped], axis=0).astype(x_ref.dtype)
    values = lax.dot_general(
        left, x_ref[...], (((1,), (1,)), ((), ())), preferred_element_type=jnp.float32
    ) * scaling
    bins_ref[band] = values.reshape(bins_ref.shape[1:])
    for k in range(1, bands):
        peer = (band + k) % bands
        copy = pltpu.make_async_remote_copy(
            src_ref=bins_ref.at[band], dst_ref=bins_ref.at[band], send_sem=send_sem.at[len(sends)],
            recv_sem=recv_f.at[band], device_id=(me, peer), device_id_type=MESH,
        )
        copy.start()
        sends.append(copy)
    for k in range(1, bands):
        src = (band + bands - k) % bands
        pltpu.make_async_remote_copy(
            src_ref=bins_ref.at[src], dst_ref=bins_ref.at[src], send_sem=send_sem.at[0],
            recv_sem=recv_f.at[src], device_id=(me, src), device_id_type=MESH,
        ).wait_recv()
    for copy in sends:
        copy.wait_send()


def grp_cross(whitened, left, selector, scaling, zs):
    groups = lax.axis_size("grp")
    bands = lax.axis_size("freq")
    width, cols = whitened.shape
    return pl.pallas_call(
        functools.partial(_cross_kernel, zs, bands, scaling),
        out_shape=(
            jax.ShapeDtypeStruct((2, width, groups * width), whitened.dtype),
            jax.ShapeDtypeStruct((bands, 2, selector.shape[0], width), jnp.float32),
        ),
        in_specs=[pl.BlockSpec(memory_space=pltpu.VMEM)] * 3,
        out_specs=(pl.BlockSpec(memory_space=pltpu.VMEM), pl.BlockSpec(memory_space=pltpu.VMEM)),
        scratch_shapes=[
            pltpu.VMEM((groups, width, cols), whitened.dtype),
            pltpu.VMEM((selector.shape[0], cols), jnp.float32),
            pltpu.SemaphoreType.DMA((8 * zs + 16,)),
            pltpu.SemaphoreType.DMA((zs - 1, 3)),
            pltpu.SemaphoreType.DMA((zs,)),
            pltpu.SemaphoreType.DMA((2 + 4 * (zs - 1),)),
            pltpu.SemaphoreType.DMA((bands,)),
        ],
        compiler_params=pltpu.CompilerParams(
            collective_id=3, has_side_effects=True, vmem_limit_bytes=56 * 1024 * 1024
        ),
    )(whitened, left, selector)


def on_device(spectra, valid, station_index):
    bin_count, chan_count, double_width = spectra.shape
    window_count = double_width // 2
    freq_count = lax.axis_size("freq")
    spectrum_f32 = spectra.astype(jnp.float32)
    real_part = spectrum_f32[..., :window_count]
    imag_part = spectrum_f32[..., window_count:]
    local_power = jnp.sum(real_part * real_part + imag_part * imag_part, axis=0)
    band_power = freq_psum(local_power, freq_count)
    total_bins = bin_count * freq_count
    factor = lax.rsqrt(band_power / total_bins + 1e-05) * valid.astype(jnp.float32)
    whitened = (spectrum_f32 * jnp.concatenate([factor, factor], axis=1)[None]).astype(jnp.bfloat16)
    swapped = jnp.concatenate([whitened[..., window_count:], -whitened[..., :window_count]], axis=2)
    stacked = jnp.concatenate([whitened, swapped], axis=1)
    scaling = 1.0 / math.sqrt(window_count)
    station_count = station_index.shape[0]
    total_chans = lax.axis_size("grp") * chan_count
    selector = (station_index[:, None] == jnp.arange(total_chans, dtype=jnp.int32)[None, :]).astype(
        jnp.bfloat16
    )
    cross, all_bins = grp_cross(
        whitened[0], stacked[0], selector, scaling, lax.axis_size("grp") // 4
    )
    cross = cross[None]

    lag_share = LAGS // freq_count
    freq_index = lax.axis_index("freq")
    bin_values = jnp.arange(total_bins, dtype=jnp.float32) + 1.0
    lag_values = (freq_index * lag_share + jnp.arange(lag_share, dtype=jnp.int32)).astype(jnp.float32)
    phase = math.pi * bin_values[:, None] * lag_values[None, :] / LAGS
    lag_table = jnp.stack([jnp.cos(phase), -jnp.sin(phase)], axis=1)
    station_gather = jnp.einsum(
        "frsc,frl->scl", all_bins, lag_table, precision=lax.Precision.HIGHEST
    ) / math.sqrt(total_bins)
    return (cross, station_gather)


def solution(mesh):
    placed = (P("freq", "grp", None), P("grp", None), P())
    return jax.shard_map(
        on_device,
        mesh=mesh,
        in_specs=placed,
        out_specs=(P("freq", None, "grp", None), P(None, "grp", "freq")),
        check_vma=False,
    )
```

```python
import functools
import math

import jax
import jax.numpy as jnp
from jax import lax
from jax.experimental import pallas as pl
from jax.experimental.pallas import tpu as pltpu
from jax.sharding import PartitionSpec as P

LAGS = 256
MESH = pl.DeviceIdType.MESH


def _greet(peers, here):
    barrier = pltpu.get_barrier_semaphore()
    for k in range(1, peers):
        pl.semaphore_signal(barrier, inc=1, device_id=here((lax.axis_index("freq") + k) % peers), device_id_type=MESH)
    pl.semaphore_wait(barrier, peers - 1)


def _whiten_kernel(peers, spec_ref, valid_ref, white_ref, left_ref, x_ref, out_ref, parts,
                   send_a, recv_a, send_b, recv_b):
    me = lax.axis_index("freq")
    grp = lax.axis_index("grp")
    rows = x_ref.shape[0] // peers
    wide = x_ref.shape[1]

    def here(peer):
        return (grp, peer)

    spectrum = spec_ref[...].astype(jnp.float32)
    real_part = spectrum[:, :wide]
    imag_part = spectrum[:, wide:]
    x_ref[...] = real_part * real_part + imag_part * imag_part
    _greet(peers, here)
    scatter = []
    for k in range(1, peers):
        peer = (me + k) % peers
        copy = pltpu.make_async_remote_copy(
            src_ref=x_ref.at[pl.ds(pl.multiple_of(peer * rows, rows), rows)],
            dst_ref=parts.at[me],
            send_sem=send_a.at[peer],
            recv_sem=recv_a.at[me],
            device_id=here(peer),
            device_id_type=MESH,
        )
        copy.start()
        scatter.append(copy)
    own = x_ref[pl.ds(pl.multiple_of(me * rows, rows), rows), :]
    for k in range(1, peers):
        src = (me + peers - k) % peers
        pltpu.make_async_remote_copy(
            src_ref=x_ref.at[pl.ds(0, rows)],
            dst_ref=parts.at[src],
            send_sem=send_a.at[src],
            recv_sem=recv_a.at[src],
            device_id=here(src),
            device_id_type=MESH,
        ).wait_recv()
    for copy in scatter:
        copy.wait_send()
    parts[me] = own
    total = parts[0]
    for src in range(1, peers):
        total = total + parts[src]
    out_ref[pl.ds(pl.multiple_of(me * rows, rows), rows), :] = total
    gather = []
    for k in range(1, peers):
        peer = (me + k) % peers
        copy = pltpu.make_async_remote_copy(
            src_ref=out_ref.at[pl.ds(pl.multiple_of(me * rows, rows), rows)],
            dst_ref=out_ref.at[pl.ds(pl.multiple_of(me * rows, rows), rows)],
            send_sem=send_b.at[peer],
            recv_sem=recv_b.at[me],
            device_id=here(peer),
            device_id_type=MESH,
        )
        copy.start()
        gather.append(copy)
    for k in range(1, peers):
        src = (me + peers - k) % peers
        pltpu.make_async_remote_copy(
            src_ref=out_ref.at[pl.ds(pl.multiple_of(src * rows, rows), rows)],
            dst_ref=out_ref.at[pl.ds(pl.multiple_of(src * rows, rows), rows)],
            send_sem=send_b.at[src],
            recv_sem=recv_b.at[src],
            device_id=here(src),
            device_id_type=MESH,
        ).wait_recv()
    for copy in gather:
        copy.wait_send()
    factor = lax.rsqrt(out_ref[...] / peers + 1e-05)
    factor = factor * valid_ref[...].astype(jnp.float32)
    white = (spectrum * jnp.concatenate([factor, factor], axis=1)).astype(white_ref.dtype)
    white_ref[...] = white
    count = white.shape[0]
    left_ref[pl.ds(0, count), :] = white
    left_ref[pl.ds(count, count), :] = jnp.concatenate([white[:, wide:], -white[:, :wide]], axis=1)


def freq_whiten(spectra, valid, peers):
    chans, double_width = spectra.shape
    wide = double_width // 2
    return pl.pallas_call(
        functools.partial(_whiten_kernel, peers),
        out_shape=(
            jax.ShapeDtypeStruct((chans, double_width), spectra.dtype),
            jax.ShapeDtypeStruct((2 * chans, double_width), spectra.dtype),
        ),
        in_specs=[pl.BlockSpec(memory_space=pltpu.VMEM)] * 2,
        out_specs=(pl.BlockSpec(memory_space=pltpu.VMEM), pl.BlockSpec(memory_space=pltpu.VMEM)),
        scratch_shapes=[
            pltpu.VMEM((chans, wide), jnp.float32),
            pltpu.VMEM((chans, wide), jnp.float32),
            pltpu.VMEM((peers, chans // peers, wide), jnp.float32),
            pltpu.SemaphoreType.DMA((peers,)),
            pltpu.SemaphoreType.DMA((peers,)),
            pltpu.SemaphoreType.DMA((peers,)),
            pltpu.SemaphoreType.DMA((peers,)),
        ],
        compiler_params=pltpu.CompilerParams(collective_id=0, has_side_effects=True),
    )(spectra, valid)


def _gather_kernel(peers, x_ref, out_ref, send_sem, recv_sem):
    me = lax.axis_index("freq")
    grp = lax.axis_index("grp")

    def here(peer):
        return (grp, peer)

    _greet(peers, here)
    sent = []
    for k in range(1, peers):
        peer = (me + k) % peers
        copy = pltpu.make_async_remote_copy(
            src_ref=x_ref,
            dst_ref=out_ref.at[me],
            send_sem=send_sem.at[peer],
            recv_sem=recv_sem.at[me],
            device_id=here(peer),
            device_id_type=MESH,
        )
        copy.start()
        sent.append(copy)
    out_ref[me] = x_ref[...]
    for k in range(1, peers):
        src = (me + peers - k) % peers
        pltpu.make_async_remote_copy(
            src_ref=x_ref,
            dst_ref=out_ref.at[src],
            send_sem=send_sem.at[src],
            recv_sem=recv_sem.at[src],
            device_id=here(src),
            device_id_type=MESH,
        ).wait_recv()
    for copy in sent:
        copy.wait_send()


def freq_gather(x, peers):
    return pl.pallas_call(
        functools.partial(_gather_kernel, peers),
        out_shape=jax.ShapeDtypeStruct((peers, *x.shape), x.dtype),
        in_specs=[pl.BlockSpec(memory_space=pltpu.VMEM)],
        out_specs=pl.BlockSpec(memory_space=pltpu.VMEM),
        scratch_shapes=[
            pltpu.SemaphoreType.DMA((peers,)),
            pltpu.SemaphoreType.DMA((peers,)),
        ],
        compiler_params=pltpu.CompilerParams(collective_id=1, has_side_effects=True),
    )(x)


def _rows_kernel(chips, x_ref, out_ref, pair, held, send_sem, recv_sem):
    me = lax.axis_index("grp")
    band = lax.axis_index("freq")
    core = me % 2
    chip = me // 2
    partner = me + 1 - 2 * core

    def dev(g):
        return (g, band)

    barrier = pltpu.get_barrier_semaphore()
    pl.semaphore_signal(barrier, inc=1, device_id=dev(partner), device_id_type=MESH)
    for k in range(1, chips):
        pl.semaphore_signal(barrier, inc=1, device_id=dev(((chip + k) % chips) * 2 + core), device_id_type=MESH)
    pl.semaphore_wait(barrier, chips)

    first = pltpu.make_async_remote_copy(
        src_ref=x_ref, dst_ref=pair, send_sem=send_sem.at[0], recv_sem=recv_sem.at[0],
        device_id=dev(partner), device_id_type=MESH,
    )
    first.start()
    first.wait_recv()
    first.wait_send()
    held[chip] = (x_ref[...].astype(jnp.float32) + pair[...].astype(jnp.float32)).astype(held.dtype)
    sent = []
    for k in range(1, chips):
        peer = (chip + k) % chips
        copy = pltpu.make_async_remote_copy(
            src_ref=held.at[chip], dst_ref=held.at[chip], send_sem=send_sem.at[1 + peer],
            recv_sem=recv_sem.at[1 + chip], device_id=dev(peer * 2 + core), device_id_type=MESH,
        )
        copy.start()
        sent.append(copy)
    for k in range(1, chips):
        src = (chip + chips - k) % chips
        pltpu.make_async_remote_copy(
            src_ref=held.at[src], dst_ref=held.at[src], send_sem=send_sem.at[1 + src],
            recv_sem=recv_sem.at[1 + src], device_id=dev(src * 2 + core), device_id_type=MESH,
        ).wait_recv()
    for copy in sent:
        copy.wait_send()
    total = held[0].astype(jnp.float32)
    for c in range(1, chips):
        total = total + held[c].astype(jnp.float32)
    out_ref[...] = total.astype(out_ref.dtype)


def grp_rows_sum(x, chips):
    return pl.pallas_call(
        functools.partial(_rows_kernel, chips),
        out_shape=jax.ShapeDtypeStruct(x.shape, x.dtype),
        in_specs=[pl.BlockSpec(memory_space=pltpu.VMEM)],
        out_specs=pl.BlockSpec(memory_space=pltpu.VMEM),
        scratch_shapes=[
            pltpu.VMEM(x.shape, x.dtype),
            pltpu.VMEM((chips, *x.shape), x.dtype),
            pltpu.SemaphoreType.DMA((chips + 1,)),
            pltpu.SemaphoreType.DMA((chips + 1,)),
        ],
        compiler_params=pltpu.CompilerParams(collective_id=2, has_side_effects=True),
    )(x)


def _cross_kernel(zs, bands, scaling, x_ref, left_ref, sel_ref, cross_ref, bins_ref, held, stage, picked,
                  send_sem, recv_ring, recv_x, recv_sib, out_sem, recv_f):
    me = lax.axis_index("grp")
    band = lax.axis_index("freq")
    c = me % 2
    xl = (me // 2) % 2
    z = me // 4
    step = 1 - 2 * c
    width = x_ref.shape[0]
    half = width // 2

    def blk(zz, xx, cc):
        return (zz * 2 + xx) * 2 + cc

    def dev(g):
        return (g, band)

    sib = blk(z, xl, 1 - c)
    partner = blk(z, 1 - xl, c)
    nxt = blk((z + step + zs) % zs, xl, c)
    prv = blk((z - step + zs) % zs, xl, c)

    barrier = pltpu.get_barrier_semaphore()
    for g in (sib, partner, nxt, prv):
        pl.semaphore_signal(barrier, inc=1, device_id=dev(g), device_id_type=MESH)
    for k in range(1, bands):
        pl.semaphore_signal(barrier, inc=1, device_id=(me, (band + k) % bands), device_id_type=MESH)
    pl.semaphore_wait(barrier, 4 + bands - 1)

    sends = []
    outs = []

    def send(src, dst, recv, g):
        copy = pltpu.make_async_remote_copy(
            src_ref=src, dst_ref=dst, send_sem=send_sem.at[len(sends)], recv_sem=recv,
            device_id=dev(g), device_id_type=MESH,
        )
        copy.start()
        sends.append(copy)

    def wait(dst, recv, g):
        pltpu.make_async_remote_copy(
            src_ref=dst, dst_ref=dst, send_sem=send_sem.at[0], recv_sem=recv,
            device_id=dev(g), device_id_type=MESH,
        ).wait_recv()

    def rows(b, h):
        return held.at[b, pl.ds(pl.multiple_of(h * half, half), half)]

    def compute(b):
        block = held[b]
        prod = lax.dot_general(
            left_ref[...], block, (((1,), (1,)), ((), ())), preferred_element_type=jnp.float32
        )
        slot = len(outs) % 2
        if len(outs) >= 2:
            outs[-2].wait()
        stage[slot] = (prod * scaling).astype(stage.dtype).reshape(stage.shape[1:])
        copy = pltpu.make_async_copy(
            stage.at[slot], cross_ref.at[:, :, pl.ds(pl.multiple_of(b * width, width), width)], out_sem.at[slot]
        )
        copy.start()
        outs.append(copy)
        picked[...] += jnp.dot(
            sel_ref[:, pl.ds(pl.multiple_of(b * width, width), width)], block,
            preferred_element_type=jnp.float32,
        )

    picked[...] = jnp.zeros_like(picked)
    own = blk(z, xl, c)
    held[own] = x_ref[...]
    send(x_ref, held.at[own], recv_x.at[0], partner)
    send(x_ref, held.at[own], recv_sib.at[0], sib)
    send(x_ref.at[pl.ds(0, half)], rows(own, 0), recv_ring.at[0, 0], nxt)
    send(x_ref.at[pl.ds(half, half)], rows(own, 1), recv_ring.at[0, 1], nxt)
    compute(own)
    across = blk(z, 1 - xl, c)
    wait(held.at[across], recv_x.at[0], partner)
    send(rows(across, xl), rows(across, xl), recv_ring.at[0, 2], nxt)
    send(held.at[across], held.at[across], recv_sib.at[1], sib)
    compute(across)

    def finish(t):
        zo = (z - step * (t + 1) + 2 * zs) % zs
        part = blk(zo, 1 - xl, c)
        wait(rows(part, 1 - xl), recv_x.at[1 + t], partner)
        send(rows(part, 1 - xl), rows(part, 1 - xl), recv_sib.at[2 + 3 * (zs - 1) + t], sib)
        compute(part)
        zt = (z + step * (t + 1) + 2 * zs) % zs
        sfull = blk(zt, xl, 1 - c)
        spart = blk(zt, 1 - xl, 1 - c)
        for k, (b, h) in enumerate(((sfull, 0), (sfull, 1), (spart, xl))):
            wait(rows(b, h), recv_sib.at[2 + 3 * t + k], sib)
        compute(sfull)
        wait(rows(spart, 1 - xl), recv_sib.at[2 + 3 * (zs - 1) + t], sib)
        compute(spart)

    for s in range(zs - 1):
        zo = (z - step * (s + 1) + 2 * zs) % zs
        full = blk(zo, xl, c)
        part = blk(zo, 1 - xl, c)
        pieces = ((full, 0), (full, 1), (part, xl))
        for k, (b, h) in enumerate(pieces):
            wait(rows(b, h), recv_ring.at[s, k], prv)
            if s < zs - 2:
                send(rows(b, h), rows(b, h), recv_ring.at[s + 1, k], nxt)
            send(rows(b, h), rows(b, h), recv_sib.at[2 + 3 * s + k], sib)
        send(rows(full, xl), rows(full, xl), recv_x.at[1 + s], partner)
        compute(full)
        if s == 0:
            wait(held.at[sib], recv_sib.at[0], sib)
            compute(sib)
            sib_across = blk(z, 1 - xl, 1 - c)
            wait(held.at[sib_across], recv_sib.at[1], sib)
            compute(sib_across)
        else:
            finish(s - 1)
    finish(zs - 2)
    station = picked[...]
    wide = station.shape[1] // 2
    swapped = jnp.concatenate([station[:, wide:], -station[:, :wide]], axis=1)
    left = jnp.concatenate([station, swapped], axis=0).astype(x_ref.dtype)
    values = lax.dot_general(
        left, x_ref[...], (((1,), (1,)), ((), ())), preferred_element_type=jnp.float32
    ) * scaling
    bins_ref[band] = values.reshape(bins_ref.shape[1:])
    for k in range(1, bands):
        peer = (band + k) % bands
        copy = pltpu.make_async_remote_copy(
            src_ref=bins_ref.at[band], dst_ref=bins_ref.at[band], send_sem=send_sem.at[len(sends)],
            recv_sem=recv_f.at[band], device_id=(me, peer), device_id_type=MESH,
        )
        copy.start()
        sends.append(copy)
    for k in range(1, bands):
        src = (band + bands - k) % bands
        pltpu.make_async_remote_copy(
            src_ref=bins_ref.at[src], dst_ref=bins_ref.at[src], send_sem=send_sem.at[0],
            recv_sem=recv_f.at[src], device_id=(me, src), device_id_type=MESH,
        ).wait_recv()
    for copy in outs[-2:]:
        copy.wait()
    for copy in sends:
        copy.wait_send()


def grp_cross(whitened, left, selector, scaling, zs):
    groups = lax.axis_size("grp")
    bands = lax.axis_size("freq")
    width, cols = whitened.shape
    return pl.pallas_call(
        functools.partial(_cross_kernel, zs, bands, scaling),
        out_shape=(
            jax.ShapeDtypeStruct((2, width, groups * width), whitened.dtype),
            jax.ShapeDtypeStruct((bands, 2, selector.shape[0], width), jnp.float32),
        ),
        in_specs=[pl.BlockSpec(memory_space=pltpu.VMEM)] * 3,
        out_specs=(pl.BlockSpec(memory_space=pl.ANY), pl.BlockSpec(memory_space=pltpu.VMEM)),
        scratch_shapes=[
            pltpu.VMEM((groups, width, cols), whitened.dtype),
            pltpu.VMEM((2, 2, width, width), whitened.dtype),
            pltpu.VMEM((selector.shape[0], cols), jnp.float32),
            pltpu.SemaphoreType.DMA((8 * zs + 16,)),
            pltpu.SemaphoreType.DMA((zs - 1, 3)),
            pltpu.SemaphoreType.DMA((zs,)),
            pltpu.SemaphoreType.DMA((2 + 4 * (zs - 1),)),
            pltpu.SemaphoreType.DMA((2,)),
            pltpu.SemaphoreType.DMA((bands,)),
        ],
        compiler_params=pltpu.CompilerParams(
            collective_id=3, has_side_effects=True, vmem_limit_bytes=56 * 1024 * 1024
        ),
    )(whitened, left, selector)


def on_device(spectra, valid, station_index):
    bin_count, chan_count, double_width = spectra.shape
    window_count = double_width // 2
    freq_count = lax.axis_size("freq")
    total_bins = bin_count * freq_count
    white, left = freq_whiten(spectra[0], valid, freq_count)
    scaling = 1.0 / math.sqrt(window_count)
    station_count = station_index.shape[0]
    total_chans = lax.axis_size("grp") * chan_count
    selector = (station_index[:, None] == jnp.arange(total_chans, dtype=jnp.int32)[None, :]).astype(
        jnp.bfloat16
    )
    cross, all_bins = grp_cross(
        white, left, selector, scaling, lax.axis_size("grp") // 4
    )
    cross = cross[None]

    lag_share = LAGS // freq_count
    freq_index = lax.axis_index("freq")
    bin_values = jnp.arange(total_bins, dtype=jnp.float32) + 1.0
    lag_values = (freq_index * lag_share + jnp.arange(lag_share, dtype=jnp.int32)).astype(jnp.float32)
    phase = math.pi * bin_values[:, None] * lag_values[None, :] / LAGS
    lag_table = jnp.stack([jnp.cos(phase), -jnp.sin(phase)], axis=1)
    station_gather = jnp.einsum(
        "frsc,frl->scl", all_bins, lag_table, precision=lax.Precision.HIGHEST
    ) / math.sqrt(total_bins)
    return (cross, station_gather)


def solution(mesh):
    placed = (P("freq", "grp", None), P("grp", None), P())
    return jax.shard_map(
        on_device,
        mesh=mesh,
        in_specs=placed,
        out_specs=(P("freq", None, "grp", None), P(None, "grp", "freq")),
        check_vma=False,
    )
```

```python
import functools
import math

import jax
import jax.numpy as jnp
from jax import lax
from jax.experimental import pallas as pl
from jax.experimental.pallas import tpu as pltpu
from jax.sharding import PartitionSpec as P

LAGS = 256
MESH = pl.DeviceIdType.MESH


def _greet(peers, here):
    barrier = pltpu.get_barrier_semaphore()
    for k in range(1, peers):
        pl.semaphore_signal(barrier, inc=1, device_id=here((lax.axis_index("freq") + k) % peers), device_id_type=MESH)
    pl.semaphore_wait(barrier, peers - 1)


def _whiten_kernel(peers, spec_ref, valid_ref, white_ref, left_ref, x_ref, out_ref, parts,
                   send_a, recv_a, send_b, recv_b):
    me = lax.axis_index("freq")
    grp = lax.axis_index("grp")
    rows = x_ref.shape[0] // peers
    wide = x_ref.shape[1]

    def here(peer):
        return (grp, peer)

    spectrum = spec_ref[...].astype(jnp.float32)
    real_part = spectrum[:, :wide]
    imag_part = spectrum[:, wide:]
    x_ref[...] = real_part * real_part + imag_part * imag_part
    _greet(peers, here)
    scatter = []
    for k in range(1, peers):
        peer = (me + k) % peers
        copy = pltpu.make_async_remote_copy(
            src_ref=x_ref.at[pl.ds(pl.multiple_of(peer * rows, rows), rows)],
            dst_ref=parts.at[me],
            send_sem=send_a.at[peer],
            recv_sem=recv_a.at[me],
            device_id=here(peer),
            device_id_type=MESH,
        )
        copy.start()
        scatter.append(copy)
    own = x_ref[pl.ds(pl.multiple_of(me * rows, rows), rows), :]
    for k in range(1, peers):
        src = (me + peers - k) % peers
        pltpu.make_async_remote_copy(
            src_ref=x_ref.at[pl.ds(0, rows)],
            dst_ref=parts.at[src],
            send_sem=send_a.at[src],
            recv_sem=recv_a.at[src],
            device_id=here(src),
            device_id_type=MESH,
        ).wait_recv()
    for copy in scatter:
        copy.wait_send()
    parts[me] = own
    total = parts[0]
    for src in range(1, peers):
        total = total + parts[src]
    out_ref[pl.ds(pl.multiple_of(me * rows, rows), rows), :] = total
    gather = []
    for k in range(1, peers):
        peer = (me + k) % peers
        copy = pltpu.make_async_remote_copy(
            src_ref=out_ref.at[pl.ds(pl.multiple_of(me * rows, rows), rows)],
            dst_ref=out_ref.at[pl.ds(pl.multiple_of(me * rows, rows), rows)],
            send_sem=send_b.at[peer],
            recv_sem=recv_b.at[me],
            device_id=here(peer),
            device_id_type=MESH,
        )
        copy.start()
        gather.append(copy)
    for k in range(1, peers):
        src = (me + peers - k) % peers
        pltpu.make_async_remote_copy(
            src_ref=out_ref.at[pl.ds(pl.multiple_of(src * rows, rows), rows)],
            dst_ref=out_ref.at[pl.ds(pl.multiple_of(src * rows, rows), rows)],
            send_sem=send_b.at[src],
            recv_sem=recv_b.at[src],
            device_id=here(src),
            device_id_type=MESH,
        ).wait_recv()
    for copy in gather:
        copy.wait_send()
    factor = lax.rsqrt(out_ref[...] / peers + 1e-05)
    factor = factor * valid_ref[...].astype(jnp.float32)
    white = (spectrum * jnp.concatenate([factor, factor], axis=1)).astype(white_ref.dtype)
    white_ref[...] = white
    count = white.shape[0]
    left_ref[pl.ds(0, count), :] = white
    left_ref[pl.ds(count, count), :] = jnp.concatenate([white[:, wide:], -white[:, :wide]], axis=1)


def freq_whiten(spectra, valid, peers):
    chans, double_width = spectra.shape
    wide = double_width // 2
    return pl.pallas_call(
        functools.partial(_whiten_kernel, peers),
        out_shape=(
            jax.ShapeDtypeStruct((chans, double_width), spectra.dtype),
            jax.ShapeDtypeStruct((2 * chans, double_width), spectra.dtype),
        ),
        in_specs=[pl.BlockSpec(memory_space=pltpu.VMEM)] * 2,
        out_specs=(pl.BlockSpec(memory_space=pltpu.VMEM), pl.BlockSpec(memory_space=pltpu.VMEM)),
        scratch_shapes=[
            pltpu.VMEM((chans, wide), jnp.float32),
            pltpu.VMEM((chans, wide), jnp.float32),
            pltpu.VMEM((peers, chans // peers, wide), jnp.float32),
            pltpu.SemaphoreType.DMA((peers,)),
            pltpu.SemaphoreType.DMA((peers,)),
            pltpu.SemaphoreType.DMA((peers,)),
            pltpu.SemaphoreType.DMA((peers,)),
        ],
        compiler_params=pltpu.CompilerParams(collective_id=0, has_side_effects=True),
    )(spectra, valid)


def _gather_kernel(peers, x_ref, out_ref, send_sem, recv_sem):
    me = lax.axis_index("freq")
    grp = lax.axis_index("grp")

    def here(peer):
        return (grp, peer)

    _greet(peers, here)
    sent = []
    for k in range(1, peers):
        peer = (me + k) % peers
        copy = pltpu.make_async_remote_copy(
            src_ref=x_ref,
            dst_ref=out_ref.at[me],
            send_sem=send_sem.at[peer],
            recv_sem=recv_sem.at[me],
            device_id=here(peer),
            device_id_type=MESH,
        )
        copy.start()
        sent.append(copy)
    out_ref[me] = x_ref[...]
    for k in range(1, peers):
        src = (me + peers - k) % peers
        pltpu.make_async_remote_copy(
            src_ref=x_ref,
            dst_ref=out_ref.at[src],
            send_sem=send_sem.at[src],
            recv_sem=recv_sem.at[src],
            device_id=here(src),
            device_id_type=MESH,
        ).wait_recv()
    for copy in sent:
        copy.wait_send()


def freq_gather(x, peers):
    return pl.pallas_call(
        functools.partial(_gather_kernel, peers),
        out_shape=jax.ShapeDtypeStruct((peers, *x.shape), x.dtype),
        in_specs=[pl.BlockSpec(memory_space=pltpu.VMEM)],
        out_specs=pl.BlockSpec(memory_space=pltpu.VMEM),
        scratch_shapes=[
            pltpu.SemaphoreType.DMA((peers,)),
            pltpu.SemaphoreType.DMA((peers,)),
        ],
        compiler_params=pltpu.CompilerParams(collective_id=1, has_side_effects=True),
    )(x)


def _rows_kernel(chips, x_ref, out_ref, pair, held, send_sem, recv_sem):
    me = lax.axis_index("grp")
    band = lax.axis_index("freq")
    core = me % 2
    chip = me // 2
    partner = me + 1 - 2 * core

    def dev(g):
        return (g, band)

    barrier = pltpu.get_barrier_semaphore()
    pl.semaphore_signal(barrier, inc=1, device_id=dev(partner), device_id_type=MESH)
    for k in range(1, chips):
        pl.semaphore_signal(barrier, inc=1, device_id=dev(((chip + k) % chips) * 2 + core), device_id_type=MESH)
    pl.semaphore_wait(barrier, chips)

    first = pltpu.make_async_remote_copy(
        src_ref=x_ref, dst_ref=pair, send_sem=send_sem.at[0], recv_sem=recv_sem.at[0],
        device_id=dev(partner), device_id_type=MESH,
    )
    first.start()
    first.wait_recv()
    first.wait_send()
    held[chip] = (x_ref[...].astype(jnp.float32) + pair[...].astype(jnp.float32)).astype(held.dtype)
    sent = []
    for k in range(1, chips):
        peer = (chip + k) % chips
        copy = pltpu.make_async_remote_copy(
            src_ref=held.at[chip], dst_ref=held.at[chip], send_sem=send_sem.at[1 + peer],
            recv_sem=recv_sem.at[1 + chip], device_id=dev(peer * 2 + core), device_id_type=MESH,
        )
        copy.start()
        sent.append(copy)
    for k in range(1, chips):
        src = (chip + chips - k) % chips
        pltpu.make_async_remote_copy(
            src_ref=held.at[src], dst_ref=held.at[src], send_sem=send_sem.at[1 + src],
            recv_sem=recv_sem.at[1 + src], device_id=dev(src * 2 + core), device_id_type=MESH,
        ).wait_recv()
    for copy in sent:
        copy.wait_send()
    total = held[0].astype(jnp.float32)
    for c in range(1, chips):
        total = total + held[c].astype(jnp.float32)
    out_ref[...] = total.astype(out_ref.dtype)


def grp_rows_sum(x, chips):
    return pl.pallas_call(
        functools.partial(_rows_kernel, chips),
        out_shape=jax.ShapeDtypeStruct(x.shape, x.dtype),
        in_specs=[pl.BlockSpec(memory_space=pltpu.VMEM)],
        out_specs=pl.BlockSpec(memory_space=pltpu.VMEM),
        scratch_shapes=[
            pltpu.VMEM(x.shape, x.dtype),
            pltpu.VMEM((chips, *x.shape), x.dtype),
            pltpu.SemaphoreType.DMA((chips + 1,)),
            pltpu.SemaphoreType.DMA((chips + 1,)),
        ],
        compiler_params=pltpu.CompilerParams(collective_id=2, has_side_effects=True),
    )(x)


def _cross_kernel(zs, bands, scaling, x_ref, left_ref, sel_ref, cross_ref, bins_ref, held, stage, picked,
                  send_sem, recv_ring, recv_x, recv_sib, out_sem, recv_f):
    me = lax.axis_index("grp")
    band = lax.axis_index("freq")
    c = me % 2
    xl = (me // 2) % 2
    z = me // 4
    step = 1 - 2 * c
    width = x_ref.shape[0]
    half = width // 2

    def blk(zz, xx, cc):
        return (zz * 2 + xx) * 2 + cc

    def dev(g):
        return (g, band)

    sib = blk(z, xl, 1 - c)
    partner = blk(z, 1 - xl, c)
    nxt = blk((z + step + zs) % zs, xl, c)
    prv = blk((z - step + zs) % zs, xl, c)

    barrier = pltpu.get_barrier_semaphore()
    for g in (sib, partner, nxt, prv):
        pl.semaphore_signal(barrier, inc=1, device_id=dev(g), device_id_type=MESH)
    for k in range(1, bands):
        pl.semaphore_signal(barrier, inc=1, device_id=(me, (band + k) % bands), device_id_type=MESH)
    pl.semaphore_wait(barrier, 4 + bands - 1)

    sends = []
    outs = []

    def send(src, dst, recv, g):
        copy = pltpu.make_async_remote_copy(
            src_ref=src, dst_ref=dst, send_sem=send_sem.at[len(sends)], recv_sem=recv,
            device_id=dev(g), device_id_type=MESH,
        )
        copy.start()
        sends.append(copy)

    def wait(dst, recv, g):
        pltpu.make_async_remote_copy(
            src_ref=dst, dst_ref=dst, send_sem=send_sem.at[0], recv_sem=recv,
            device_id=dev(g), device_id_type=MESH,
        ).wait_recv()

    def rows(b, h):
        return held.at[b, pl.ds(pl.multiple_of(h * half, half), half)]

    def compute(b):
        block = held[b]
        prod = lax.dot_general(
            left_ref[...], block, (((1,), (1,)), ((), ())), preferred_element_type=jnp.float32
        )
        slot = len(outs) % 2
        if len(outs) >= 2:
            outs[-2].wait()
        stage[slot] = (prod * scaling).astype(stage.dtype).reshape(stage.shape[1:])
        copy = pltpu.make_async_copy(
            stage.at[slot], cross_ref.at[:, :, pl.ds(pl.multiple_of(b * width, width), width)], out_sem.at[slot]
        )
        copy.start()
        outs.append(copy)
        columns = b * width + lax.broadcasted_iota(jnp.int32, (sel_ref.shape[0], width), 1)
        chosen = (sel_ref[...] == columns).astype(block.dtype)
        picked[...] += jnp.dot(chosen, block, preferred_element_type=jnp.float32)

    picked[...] = jnp.zeros_like(picked)
    own = blk(z, xl, c)
    held[own] = x_ref[...]
    send(x_ref, held.at[own], recv_x.at[0], partner)
    send(x_ref, held.at[own], recv_sib.at[0], sib)
    send(x_ref.at[pl.ds(0, half)], rows(own, 0), recv_ring.at[0, 0], nxt)
    send(x_ref.at[pl.ds(half, half)], rows(own, 1), recv_ring.at[0, 1], nxt)
    compute(own)
    across = blk(z, 1 - xl, c)
    wait(held.at[across], recv_x.at[0], partner)
    send(rows(across, xl), rows(across, xl), recv_ring.at[0, 2], nxt)
    send(held.at[across], held.at[across], recv_sib.at[1], sib)
    compute(across)

    def finish(t):
        zo = (z - step * (t + 1) + 2 * zs) % zs
        part = blk(zo, 1 - xl, c)
        wait(rows(part, 1 - xl), recv_x.at[1 + t], partner)
        send(rows(part, 1 - xl), rows(part, 1 - xl), recv_sib.at[2 + 3 * (zs - 1) + t], sib)
        compute(part)
        zt = (z + step * (t + 1) + 2 * zs) % zs
        sfull = blk(zt, xl, 1 - c)
        spart = blk(zt, 1 - xl, 1 - c)
        for k, (b, h) in enumerate(((sfull, 0), (sfull, 1), (spart, xl))):
            wait(rows(b, h), recv_sib.at[2 + 3 * t + k], sib)
        compute(sfull)
        wait(rows(spart, 1 - xl), recv_sib.at[2 + 3 * (zs - 1) + t], sib)
        compute(spart)

    for s in range(zs - 1):
        zo = (z - step * (s + 1) + 2 * zs) % zs
        full = blk(zo, xl, c)
        part = blk(zo, 1 - xl, c)
        pieces = ((full, 0), (full, 1), (part, xl))
        for k, (b, h) in enumerate(pieces):
            wait(rows(b, h), recv_ring.at[s, k], prv)
            if s < zs - 2:
                send(rows(b, h), rows(b, h), recv_ring.at[s + 1, k], nxt)
            send(rows(b, h), rows(b, h), recv_sib.at[2 + 3 * s + k], sib)
        send(rows(full, xl), rows(full, xl), recv_x.at[1 + s], partner)
        compute(full)
        if s == 0:
            wait(held.at[sib], recv_sib.at[0], sib)
            compute(sib)
            sib_across = blk(z, 1 - xl, 1 - c)
            wait(held.at[sib_across], recv_sib.at[1], sib)
            compute(sib_across)
        else:
            finish(s - 1)
    finish(zs - 2)
    station = picked[...]
    wide = station.shape[1] // 2
    swapped = jnp.concatenate([station[:, wide:], -station[:, :wide]], axis=1)
    left = jnp.concatenate([station, swapped], axis=0).astype(x_ref.dtype)
    values = lax.dot_general(
        left, x_ref[...], (((1,), (1,)), ((), ())), preferred_element_type=jnp.float32
    ) * scaling
    bins_ref[band] = values.reshape(bins_ref.shape[1:])
    for k in range(1, bands):
        peer = (band + k) % bands
        copy = pltpu.make_async_remote_copy(
            src_ref=bins_ref.at[band], dst_ref=bins_ref.at[band], send_sem=send_sem.at[len(sends)],
            recv_sem=recv_f.at[band], device_id=(me, peer), device_id_type=MESH,
        )
        copy.start()
        sends.append(copy)
    for k in range(1, bands):
        src = (band + bands - k) % bands
        pltpu.make_async_remote_copy(
            src_ref=bins_ref.at[src], dst_ref=bins_ref.at[src], send_sem=send_sem.at[0],
            recv_sem=recv_f.at[src], device_id=(me, src), device_id_type=MESH,
        ).wait_recv()
    for copy in outs[-2:]:
        copy.wait()
    for copy in sends:
        copy.wait_send()


def grp_cross(whitened, left, selector, scaling, zs):
    groups = lax.axis_size("grp")
    bands = lax.axis_size("freq")
    width, cols = whitened.shape
    return pl.pallas_call(
        functools.partial(_cross_kernel, zs, bands, scaling),
        out_shape=(
            jax.ShapeDtypeStruct((2, width, groups * width), whitened.dtype),
            jax.ShapeDtypeStruct((bands, 2, selector.shape[0], width), jnp.float32),
        ),
        in_specs=[pl.BlockSpec(memory_space=pltpu.VMEM)] * 3,
        out_specs=(pl.BlockSpec(memory_space=pl.ANY), pl.BlockSpec(memory_space=pltpu.VMEM)),
        scratch_shapes=[
            pltpu.VMEM((groups, width, cols), whitened.dtype),
            pltpu.VMEM((2, 2, width, width), whitened.dtype),
            pltpu.VMEM((selector.shape[0], cols), jnp.float32),
            pltpu.SemaphoreType.DMA((8 * zs + 16,)),
            pltpu.SemaphoreType.DMA((zs - 1, 3)),
            pltpu.SemaphoreType.DMA((zs,)),
            pltpu.SemaphoreType.DMA((2 + 4 * (zs - 1),)),
            pltpu.SemaphoreType.DMA((2,)),
            pltpu.SemaphoreType.DMA((bands,)),
        ],
        compiler_params=pltpu.CompilerParams(
            collective_id=3, has_side_effects=True, vmem_limit_bytes=56 * 1024 * 1024
        ),
    )(whitened, left, selector)


def on_device(spectra, valid, station_index):
    bin_count, chan_count, double_width = spectra.shape
    window_count = double_width // 2
    freq_count = lax.axis_size("freq")
    total_bins = bin_count * freq_count
    white, left = freq_whiten(spectra[0], valid, freq_count)
    scaling = 1.0 / math.sqrt(window_count)
    station_count = station_index.shape[0]
    selector = station_index[:, None]
    cross, all_bins = grp_cross(
        white, left, selector, scaling, lax.axis_size("grp") // 4
    )
    cross = cross[None]

    lag_share = LAGS // freq_count
    freq_index = lax.axis_index("freq")
    bin_values = jnp.arange(total_bins, dtype=jnp.float32) + 1.0
    lag_values = (freq_index * lag_share + jnp.arange(lag_share, dtype=jnp.int32)).astype(jnp.float32)
    phase = math.pi * bin_values[:, None] * lag_values[None, :] / LAGS
    lag_table = jnp.stack([jnp.cos(phase), -jnp.sin(phase)], axis=1)
    station_gather = jnp.einsum(
        "frsc,frl->scl", all_bins, lag_table, precision=lax.Precision.HIGHEST
    ) / math.sqrt(total_bins)
    return (cross, station_gather)


def solution(mesh):
    placed = (P("freq", "grp", None), P("grp", None), P())
    return jax.shard_map(
        on_device,
        mesh=mesh,
        in_specs=placed,
        out_specs=(P("freq", None, "grp", None), P(None, "grp", "freq")),
        check_vma=False,
    )
```

```python
import functools
import math

import jax
import jax.numpy as jnp
from jax import lax
from jax.experimental import pallas as pl
from jax.experimental.pallas import tpu as pltpu
from jax.sharding import PartitionSpec as P

LAGS = 256
MESH = pl.DeviceIdType.MESH


def _greet(peers, here):
    barrier = pltpu.get_barrier_semaphore()
    for k in range(1, peers):
        pl.semaphore_signal(barrier, inc=1, device_id=here((lax.axis_index("freq") + k) % peers), device_id_type=MESH)
    pl.semaphore_wait(barrier, peers - 1)


def _whiten_kernel(peers, spec_ref, valid_ref, white_ref, left_ref, x_ref, out_ref, parts,
                   send_a, recv_a, send_b, recv_b):
    me = lax.axis_index("freq")
    grp = lax.axis_index("grp")
    rows = x_ref.shape[0] // peers
    wide = x_ref.shape[1]

    def here(peer):
        return (grp, peer)

    spectrum = spec_ref[...].astype(jnp.float32)
    real_part = spectrum[:, :wide]
    imag_part = spectrum[:, wide:]
    x_ref[...] = real_part * real_part + imag_part * imag_part
    _greet(peers, here)
    scatter = []
    for k in range(1, peers):
        peer = (me + k) % peers
        copy = pltpu.make_async_remote_copy(
            src_ref=x_ref.at[pl.ds(pl.multiple_of(peer * rows, rows), rows)],
            dst_ref=parts.at[me],
            send_sem=send_a.at[peer],
            recv_sem=recv_a.at[me],
            device_id=here(peer),
            device_id_type=MESH,
        )
        copy.start()
        scatter.append(copy)
    own = x_ref[pl.ds(pl.multiple_of(me * rows, rows), rows), :]
    for k in range(1, peers):
        src = (me + peers - k) % peers
        pltpu.make_async_remote_copy(
            src_ref=x_ref.at[pl.ds(0, rows)],
            dst_ref=parts.at[src],
            send_sem=send_a.at[src],
            recv_sem=recv_a.at[src],
            device_id=here(src),
            device_id_type=MESH,
        ).wait_recv()
    for copy in scatter:
        copy.wait_send()
    parts[me] = own
    total = parts[0]
    for src in range(1, peers):
        total = total + parts[src]
    out_ref[pl.ds(pl.multiple_of(me * rows, rows), rows), :] = total
    gather = []
    for k in range(1, peers):
        peer = (me + k) % peers
        copy = pltpu.make_async_remote_copy(
            src_ref=out_ref.at[pl.ds(pl.multiple_of(me * rows, rows), rows)],
            dst_ref=out_ref.at[pl.ds(pl.multiple_of(me * rows, rows), rows)],
            send_sem=send_b.at[peer],
            recv_sem=recv_b.at[me],
            device_id=here(peer),
            device_id_type=MESH,
        )
        copy.start()
        gather.append(copy)
    for k in range(1, peers):
        src = (me + peers - k) % peers
        pltpu.make_async_remote_copy(
            src_ref=out_ref.at[pl.ds(pl.multiple_of(src * rows, rows), rows)],
            dst_ref=out_ref.at[pl.ds(pl.multiple_of(src * rows, rows), rows)],
            send_sem=send_b.at[src],
            recv_sem=recv_b.at[src],
            device_id=here(src),
            device_id_type=MESH,
        ).wait_recv()
    for copy in gather:
        copy.wait_send()
    factor = lax.rsqrt(out_ref[...] / peers + 1e-05)
    factor = factor * valid_ref[...].astype(jnp.float32)
    white = (spectrum * jnp.concatenate([factor, factor], axis=1)).astype(white_ref.dtype)
    white_ref[...] = white
    count = white.shape[0]
    left_ref[pl.ds(0, count), :] = white
    left_ref[pl.ds(count, count), :] = jnp.concatenate([white[:, wide:], -white[:, :wide]], axis=1)


def freq_whiten(spectra, valid, peers):
    chans, double_width = spectra.shape
    wide = double_width // 2
    return pl.pallas_call(
        functools.partial(_whiten_kernel, peers),
        out_shape=(
            jax.ShapeDtypeStruct((chans, double_width), spectra.dtype),
            jax.ShapeDtypeStruct((2 * chans, double_width), spectra.dtype),
        ),
        in_specs=[pl.BlockSpec(memory_space=pltpu.VMEM)] * 2,
        out_specs=(pl.BlockSpec(memory_space=pltpu.VMEM), pl.BlockSpec(memory_space=pltpu.VMEM)),
        scratch_shapes=[
            pltpu.VMEM((chans, wide), jnp.float32),
            pltpu.VMEM((chans, wide), jnp.float32),
            pltpu.VMEM((peers, chans // peers, wide), jnp.float32),
            pltpu.SemaphoreType.DMA((peers,)),
            pltpu.SemaphoreType.DMA((peers,)),
            pltpu.SemaphoreType.DMA((peers,)),
            pltpu.SemaphoreType.DMA((peers,)),
        ],
        compiler_params=pltpu.CompilerParams(collective_id=0, has_side_effects=True),
    )(spectra, valid)


def _gather_kernel(peers, x_ref, out_ref, send_sem, recv_sem):
    me = lax.axis_index("freq")
    grp = lax.axis_index("grp")

    def here(peer):
        return (grp, peer)

    _greet(peers, here)
    sent = []
    for k in range(1, peers):
        peer = (me + k) % peers
        copy = pltpu.make_async_remote_copy(
            src_ref=x_ref,
            dst_ref=out_ref.at[me],
            send_sem=send_sem.at[peer],
            recv_sem=recv_sem.at[me],
            device_id=here(peer),
            device_id_type=MESH,
        )
        copy.start()
        sent.append(copy)
    out_ref[me] = x_ref[...]
    for k in range(1, peers):
        src = (me + peers - k) % peers
        pltpu.make_async_remote_copy(
            src_ref=x_ref,
            dst_ref=out_ref.at[src],
            send_sem=send_sem.at[src],
            recv_sem=recv_sem.at[src],
            device_id=here(src),
            device_id_type=MESH,
        ).wait_recv()
    for copy in sent:
        copy.wait_send()


def freq_gather(x, peers):
    return pl.pallas_call(
        functools.partial(_gather_kernel, peers),
        out_shape=jax.ShapeDtypeStruct((peers, *x.shape), x.dtype),
        in_specs=[pl.BlockSpec(memory_space=pltpu.VMEM)],
        out_specs=pl.BlockSpec(memory_space=pltpu.VMEM),
        scratch_shapes=[
            pltpu.SemaphoreType.DMA((peers,)),
            pltpu.SemaphoreType.DMA((peers,)),
        ],
        compiler_params=pltpu.CompilerParams(collective_id=1, has_side_effects=True),
    )(x)


def _rows_kernel(chips, x_ref, out_ref, pair, held, send_sem, recv_sem):
    me = lax.axis_index("grp")
    band = lax.axis_index("freq")
    core = me % 2
    chip = me // 2
    partner = me + 1 - 2 * core

    def dev(g):
        return (g, band)

    barrier = pltpu.get_barrier_semaphore()
    pl.semaphore_signal(barrier, inc=1, device_id=dev(partner), device_id_type=MESH)
    for k in range(1, chips):
        pl.semaphore_signal(barrier, inc=1, device_id=dev(((chip + k) % chips) * 2 + core), device_id_type=MESH)
    pl.semaphore_wait(barrier, chips)

    first = pltpu.make_async_remote_copy(
        src_ref=x_ref, dst_ref=pair, send_sem=send_sem.at[0], recv_sem=recv_sem.at[0],
        device_id=dev(partner), device_id_type=MESH,
    )
    first.start()
    first.wait_recv()
    first.wait_send()
    held[chip] = (x_ref[...].astype(jnp.float32) + pair[...].astype(jnp.float32)).astype(held.dtype)
    sent = []
    for k in range(1, chips):
        peer = (chip + k) % chips
        copy = pltpu.make_async_remote_copy(
            src_ref=held.at[chip], dst_ref=held.at[chip], send_sem=send_sem.at[1 + peer],
            recv_sem=recv_sem.at[1 + chip], device_id=dev(peer * 2 + core), device_id_type=MESH,
        )
        copy.start()
        sent.append(copy)
    for k in range(1, chips):
        src = (chip + chips - k) % chips
        pltpu.make_async_remote_copy(
            src_ref=held.at[src], dst_ref=held.at[src], send_sem=send_sem.at[1 + src],
            recv_sem=recv_sem.at[1 + src], device_id=dev(src * 2 + core), device_id_type=MESH,
        ).wait_recv()
    for copy in sent:
        copy.wait_send()
    total = held[0].astype(jnp.float32)
    for c in range(1, chips):
        total = total + held[c].astype(jnp.float32)
    out_ref[...] = total.astype(out_ref.dtype)


def grp_rows_sum(x, chips):
    return pl.pallas_call(
        functools.partial(_rows_kernel, chips),
        out_shape=jax.ShapeDtypeStruct(x.shape, x.dtype),
        in_specs=[pl.BlockSpec(memory_space=pltpu.VMEM)],
        out_specs=pl.BlockSpec(memory_space=pltpu.VMEM),
        scratch_shapes=[
            pltpu.VMEM(x.shape, x.dtype),
            pltpu.VMEM((chips, *x.shape), x.dtype),
            pltpu.SemaphoreType.DMA((chips + 1,)),
            pltpu.SemaphoreType.DMA((chips + 1,)),
        ],
        compiler_params=pltpu.CompilerParams(collective_id=2, has_side_effects=True),
    )(x)


def _cross_kernel(zs, bands, scaling, x_ref, left_ref, sel_ref, cross_ref, bins_ref, held, stage, picked,
                  send_sem, recv_ring, recv_x, recv_sib, out_sem, recv_f):
    me = lax.axis_index("grp")
    band = lax.axis_index("freq")
    c = me % 2
    xl = (me // 2) % 2
    z = me // 4
    step = 1 - 2 * c
    width = x_ref.shape[0]
    half = width // 2

    def blk(zz, xx, cc):
        return (zz * 2 + xx) * 2 + cc

    def dev(g):
        return (g, band)

    sib = blk(z, xl, 1 - c)
    partner = blk(z, 1 - xl, c)
    nxt = blk((z + step + zs) % zs, xl, c)
    prv = blk((z - step + zs) % zs, xl, c)

    barrier = pltpu.get_barrier_semaphore()
    for g in (sib, partner, nxt, prv):
        pl.semaphore_signal(barrier, inc=1, device_id=dev(g), device_id_type=MESH)
    for k in range(1, bands):
        pl.semaphore_signal(barrier, inc=1, device_id=(me, (band + k) % bands), device_id_type=MESH)
    pl.semaphore_wait(barrier, 4 + bands - 1)

    sends = []
    outs = []

    def send(src, dst, recv, g):
        copy = pltpu.make_async_remote_copy(
            src_ref=src, dst_ref=dst, send_sem=send_sem.at[len(sends)], recv_sem=recv,
            device_id=dev(g), device_id_type=MESH,
        )
        copy.start()
        sends.append(copy)

    def wait(dst, recv, g):
        pltpu.make_async_remote_copy(
            src_ref=dst, dst_ref=dst, send_sem=send_sem.at[0], recv_sem=recv,
            device_id=dev(g), device_id_type=MESH,
        ).wait_recv()

    def rows(b, h):
        return held.at[b, pl.ds(pl.multiple_of(h * half, half), half)]

    def compute(b):
        block = held[b]
        prod = lax.dot_general(
            left_ref[...], block, (((1,), (1,)), ((), ())), preferred_element_type=jnp.float32
        )
        slot = len(outs) % 2
        if len(outs) >= 2:
            outs[-2].wait()
        stage[slot] = (prod * scaling).astype(stage.dtype).reshape(stage.shape[1:])
        copy = pltpu.make_async_copy(
            stage.at[slot], cross_ref.at[:, :, pl.ds(pl.multiple_of(b * width, width), width)], out_sem.at[slot]
        )
        copy.start()
        outs.append(copy)
        columns = b * width + lax.broadcasted_iota(jnp.int32, (stations, width), 1)
        chosen = (station_ids == columns).astype(block.dtype)
        picked[...] += jnp.dot(chosen, block, preferred_element_type=jnp.float32)

    picked[...] = jnp.zeros_like(picked)
    stations = picked.shape[0]
    place = lax.broadcasted_iota(jnp.int32, (stations, width), 0)
    station_ids = jnp.zeros((stations, width), jnp.int32)
    for k in range(stations):
        station_ids = jnp.where(place == k, sel_ref[k], station_ids)
    own = blk(z, xl, c)
    held[own] = x_ref[...]
    send(x_ref, held.at[own], recv_x.at[0], partner)
    send(x_ref, held.at[own], recv_sib.at[0], sib)
    send(x_ref.at[pl.ds(0, half)], rows(own, 0), recv_ring.at[0, 0], nxt)
    send(x_ref.at[pl.ds(half, half)], rows(own, 1), recv_ring.at[0, 1], nxt)
    compute(own)
    across = blk(z, 1 - xl, c)
    wait(held.at[across], recv_x.at[0], partner)
    send(rows(across, xl), rows(across, xl), recv_ring.at[0, 2], nxt)
    send(held.at[across], held.at[across], recv_sib.at[1], sib)
    compute(across)

    def finish(t):
        zo = (z - step * (t + 1) + 2 * zs) % zs
        part = blk(zo, 1 - xl, c)
        wait(rows(part, 1 - xl), recv_x.at[1 + t], partner)
        send(rows(part, 1 - xl), rows(part, 1 - xl), recv_sib.at[2 + 3 * (zs - 1) + t], sib)
        compute(part)
        zt = (z + step * (t + 1) + 2 * zs) % zs
        sfull = blk(zt, xl, 1 - c)
        spart = blk(zt, 1 - xl, 1 - c)
        for k, (b, h) in enumerate(((sfull, 0), (sfull, 1), (spart, xl))):
            wait(rows(b, h), recv_sib.at[2 + 3 * t + k], sib)
        compute(sfull)
        wait(rows(spart, 1 - xl), recv_sib.at[2 + 3 * (zs - 1) + t], sib)
        compute(spart)

    for s in range(zs - 1):
        zo = (z - step * (s + 1) + 2 * zs) % zs
        full = blk(zo, xl, c)
        part = blk(zo, 1 - xl, c)
        pieces = ((full, 0), (full, 1), (part, xl))
        for k, (b, h) in enumerate(pieces):
            wait(rows(b, h), recv_ring.at[s, k], prv)
            if s < zs - 2:
                send(rows(b, h), rows(b, h), recv_ring.at[s + 1, k], nxt)
            send(rows(b, h), rows(b, h), recv_sib.at[2 + 3 * s + k], sib)
        send(rows(full, xl), rows(full, xl), recv_x.at[1 + s], partner)
        compute(full)
        if s == 0:
            wait(held.at[sib], recv_sib.at[0], sib)
            compute(sib)
            sib_across = blk(z, 1 - xl, 1 - c)
            wait(held.at[sib_across], recv_sib.at[1], sib)
            compute(sib_across)
        else:
            finish(s - 1)
    finish(zs - 2)
    station = picked[...]
    wide = station.shape[1] // 2
    swapped = jnp.concatenate([station[:, wide:], -station[:, :wide]], axis=1)
    left = jnp.concatenate([station, swapped], axis=0).astype(x_ref.dtype)
    values = lax.dot_general(
        left, x_ref[...], (((1,), (1,)), ((), ())), preferred_element_type=jnp.float32
    ) * scaling
    bins_ref[band] = values.reshape(bins_ref.shape[1:])
    for k in range(1, bands):
        peer = (band + k) % bands
        copy = pltpu.make_async_remote_copy(
            src_ref=bins_ref.at[band], dst_ref=bins_ref.at[band], send_sem=send_sem.at[len(sends)],
            recv_sem=recv_f.at[band], device_id=(me, peer), device_id_type=MESH,
        )
        copy.start()
        sends.append(copy)
    for k in range(1, bands):
        src = (band + bands - k) % bands
        pltpu.make_async_remote_copy(
            src_ref=bins_ref.at[src], dst_ref=bins_ref.at[src], send_sem=send_sem.at[0],
            recv_sem=recv_f.at[src], device_id=(me, src), device_id_type=MESH,
        ).wait_recv()
    for copy in outs[-2:]:
        copy.wait()
    for copy in sends:
        copy.wait_send()


def grp_cross(whitened, left, selector, scaling, zs):
    groups = lax.axis_size("grp")
    bands = lax.axis_size("freq")
    width, cols = whitened.shape
    return pl.pallas_call(
        functools.partial(_cross_kernel, zs, bands, scaling),
        out_shape=(
            jax.ShapeDtypeStruct((2, width, groups * width), whitened.dtype),
            jax.ShapeDtypeStruct((bands, 2, selector.shape[0], width), jnp.float32),
        ),
        in_specs=[pl.BlockSpec(memory_space=pltpu.VMEM)] * 2 + [pl.BlockSpec(memory_space=pltpu.SMEM)],
        out_specs=(pl.BlockSpec(memory_space=pl.ANY), pl.BlockSpec(memory_space=pltpu.VMEM)),
        scratch_shapes=[
            pltpu.VMEM((groups, width, cols), whitened.dtype),
            pltpu.VMEM((2, 2, width, width), whitened.dtype),
            pltpu.VMEM((selector.shape[0], cols), jnp.float32),
            pltpu.SemaphoreType.DMA((8 * zs + 16,)),
            pltpu.SemaphoreType.DMA((zs - 1, 3)),
            pltpu.SemaphoreType.DMA((zs,)),
            pltpu.SemaphoreType.DMA((2 + 4 * (zs - 1),)),
            pltpu.SemaphoreType.DMA((2,)),
            pltpu.SemaphoreType.DMA((bands,)),
        ],
        compiler_params=pltpu.CompilerParams(
            collective_id=3, has_side_effects=True, vmem_limit_bytes=56 * 1024 * 1024
        ),
    )(whitened, left, selector)


def on_device(spectra, valid, station_index):
    bin_count, chan_count, double_width = spectra.shape
    window_count = double_width // 2
    freq_count = lax.axis_size("freq")
    total_bins = bin_count * freq_count
    white, left = freq_whiten(spectra[0], valid, freq_count)
    scaling = 1.0 / math.sqrt(window_count)
    station_count = station_index.shape[0]
    selector = station_index
    cross, all_bins = grp_cross(
        white, left, selector, scaling, lax.axis_size("grp") // 4
    )
    cross = cross[None]

    lag_share = LAGS // freq_count
    freq_index = lax.axis_index("freq")
    bin_values = jnp.arange(total_bins, dtype=jnp.float32) + 1.0
    lag_values = (freq_index * lag_share + jnp.arange(lag_share, dtype=jnp.int32)).astype(jnp.float32)
    phase = math.pi * bin_values[:, None] * lag_values[None, :] / LAGS
    lag_table = jnp.stack([jnp.cos(phase), -jnp.sin(phase)], axis=1)
    station_gather = jnp.einsum(
        "frsc,frl->scl", all_bins, lag_table, precision=lax.Precision.HIGHEST
    ) / math.sqrt(total_bins)
    return (cross, station_gather)


def solution(mesh):
    placed = (P("freq", "grp", None), P("grp", None), P())
    return jax.shard_map(
        on_device,
        mesh=mesh,
        in_specs=placed,
        out_specs=(P("freq", None, "grp", None), P(None, "grp", "freq")),
        check_vma=False,
    )
```

```python
import functools
import math

import jax
import jax.numpy as jnp
from jax import lax
from jax.experimental import pallas as pl
from jax.experimental.pallas import tpu as pltpu
from jax.sharding import PartitionSpec as P

LAGS = 256
MESH = pl.DeviceIdType.MESH


def _greet(peers, here):
    barrier = pltpu.get_barrier_semaphore()
    for k in range(1, peers):
        pl.semaphore_signal(barrier, inc=1, device_id=here((lax.axis_index("freq") + k) % peers), device_id_type=MESH)
    pl.semaphore_wait(barrier, peers - 1)


def _whiten_kernel(peers, greet, spec_ref, valid_ref, white_ref, left_ref, x_ref, out_ref, parts,
                   send_a, recv_a, send_b, recv_b):
    me = lax.axis_index("freq")
    grp = lax.axis_index("grp")
    rows = x_ref.shape[0] // peers
    wide = x_ref.shape[1]

    def here(peer):
        return (grp, peer)

    spectrum = spec_ref[...].astype(jnp.float32)
    real_part = spectrum[:, :wide]
    imag_part = spectrum[:, wide:]
    x_ref[...] = real_part * real_part + imag_part * imag_part
    if greet:
        _greet(peers, here)
    scatter = []
    for k in range(1, peers):
        peer = (me + k) % peers
        copy = pltpu.make_async_remote_copy(
            src_ref=x_ref.at[pl.ds(pl.multiple_of(peer * rows, rows), rows)],
            dst_ref=parts.at[me],
            send_sem=send_a.at[peer],
            recv_sem=recv_a.at[me],
            device_id=here(peer),
            device_id_type=MESH,
        )
        copy.start()
        scatter.append(copy)
    own = x_ref[pl.ds(pl.multiple_of(me * rows, rows), rows), :]
    for k in range(1, peers):
        src = (me + peers - k) % peers
        pltpu.make_async_remote_copy(
            src_ref=x_ref.at[pl.ds(0, rows)],
            dst_ref=parts.at[src],
            send_sem=send_a.at[src],
            recv_sem=recv_a.at[src],
            device_id=here(src),
            device_id_type=MESH,
        ).wait_recv()
    for copy in scatter:
        copy.wait_send()
    parts[me] = own
    total = parts[0]
    for src in range(1, peers):
        total = total + parts[src]
    out_ref[pl.ds(pl.multiple_of(me * rows, rows), rows), :] = total
    gather = []
    for k in range(1, peers):
        peer = (me + k) % peers
        copy = pltpu.make_async_remote_copy(
            src_ref=out_ref.at[pl.ds(pl.multiple_of(me * rows, rows), rows)],
            dst_ref=out_ref.at[pl.ds(pl.multiple_of(me * rows, rows), rows)],
            send_sem=send_b.at[peer],
            recv_sem=recv_b.at[me],
            device_id=here(peer),
            device_id_type=MESH,
        )
        copy.start()
        gather.append(copy)
    for k in range(1, peers):
        src = (me + peers - k) % peers
        pltpu.make_async_remote_copy(
            src_ref=out_ref.at[pl.ds(pl.multiple_of(src * rows, rows), rows)],
            dst_ref=out_ref.at[pl.ds(pl.multiple_of(src * rows, rows), rows)],
            send_sem=send_b.at[src],
            recv_sem=recv_b.at[src],
            device_id=here(src),
            device_id_type=MESH,
        ).wait_recv()
    for copy in gather:
        copy.wait_send()
    factor = lax.rsqrt(out_ref[...] / peers + 1e-05)
    factor = factor * valid_ref[...].astype(jnp.float32)
    white = (spectrum * jnp.concatenate([factor, factor], axis=1)).astype(white_ref.dtype)
    white_ref[...] = white
    count = white.shape[0]
    left_ref[pl.ds(0, count), :] = white
    left_ref[pl.ds(count, count), :] = jnp.concatenate([white[:, wide:], -white[:, :wide]], axis=1)


def freq_whiten(spectra, valid, peers):
    chans, double_width = spectra.shape
    wide = double_width // 2
    return pl.pallas_call(
        functools.partial(_whiten_kernel, peers, True),
        out_shape=(
            jax.ShapeDtypeStruct((chans, double_width), spectra.dtype),
            jax.ShapeDtypeStruct((2 * chans, double_width), spectra.dtype),
        ),
        in_specs=[pl.BlockSpec(memory_space=pltpu.VMEM)] * 2,
        out_specs=(pl.BlockSpec(memory_space=pltpu.VMEM), pl.BlockSpec(memory_space=pltpu.VMEM)),
        scratch_shapes=[
            pltpu.VMEM((chans, wide), jnp.float32),
            pltpu.VMEM((chans, wide), jnp.float32),
            pltpu.VMEM((peers, chans // peers, wide), jnp.float32),
            pltpu.SemaphoreType.DMA((peers,)),
            pltpu.SemaphoreType.DMA((peers,)),
            pltpu.SemaphoreType.DMA((peers,)),
            pltpu.SemaphoreType.DMA((peers,)),
        ],
        compiler_params=pltpu.CompilerParams(collective_id=0, has_side_effects=True),
    )(spectra, valid)


def _gather_kernel(peers, x_ref, out_ref, send_sem, recv_sem):
    me = lax.axis_index("freq")
    grp = lax.axis_index("grp")

    def here(peer):
        return (grp, peer)

    _greet(peers, here)
    sent = []
    for k in range(1, peers):
        peer = (me + k) % peers
        copy = pltpu.make_async_remote_copy(
            src_ref=x_ref,
            dst_ref=out_ref.at[me],
            send_sem=send_sem.at[peer],
            recv_sem=recv_sem.at[me],
            device_id=here(peer),
            device_id_type=MESH,
        )
        copy.start()
        sent.append(copy)
    out_ref[me] = x_ref[...]
    for k in range(1, peers):
        src = (me + peers - k) % peers
        pltpu.make_async_remote_copy(
            src_ref=x_ref,
            dst_ref=out_ref.at[src],
            send_sem=send_sem.at[src],
            recv_sem=recv_sem.at[src],
            device_id=here(src),
            device_id_type=MESH,
        ).wait_recv()
    for copy in sent:
        copy.wait_send()


def freq_gather(x, peers):
    return pl.pallas_call(
        functools.partial(_gather_kernel, peers),
        out_shape=jax.ShapeDtypeStruct((peers, *x.shape), x.dtype),
        in_specs=[pl.BlockSpec(memory_space=pltpu.VMEM)],
        out_specs=pl.BlockSpec(memory_space=pltpu.VMEM),
        scratch_shapes=[
            pltpu.SemaphoreType.DMA((peers,)),
            pltpu.SemaphoreType.DMA((peers,)),
        ],
        compiler_params=pltpu.CompilerParams(collective_id=1, has_side_effects=True),
    )(x)


def _rows_kernel(chips, x_ref, out_ref, pair, held, send_sem, recv_sem):
    me = lax.axis_index("grp")
    band = lax.axis_index("freq")
    core = me % 2
    chip = me // 2
    partner = me + 1 - 2 * core

    def dev(g):
        return (g, band)

    barrier = pltpu.get_barrier_semaphore()
    pl.semaphore_signal(barrier, inc=1, device_id=dev(partner), device_id_type=MESH)
    for k in range(1, chips):
        pl.semaphore_signal(barrier, inc=1, device_id=dev(((chip + k) % chips) * 2 + core), device_id_type=MESH)
    pl.semaphore_wait(barrier, chips)

    first = pltpu.make_async_remote_copy(
        src_ref=x_ref, dst_ref=pair, send_sem=send_sem.at[0], recv_sem=recv_sem.at[0],
        device_id=dev(partner), device_id_type=MESH,
    )
    first.start()
    first.wait_recv()
    first.wait_send()
    held[chip] = (x_ref[...].astype(jnp.float32) + pair[...].astype(jnp.float32)).astype(held.dtype)
    sent = []
    for k in range(1, chips):
        peer = (chip + k) % chips
        copy = pltpu.make_async_remote_copy(
            src_ref=held.at[chip], dst_ref=held.at[chip], send_sem=send_sem.at[1 + peer],
            recv_sem=recv_sem.at[1 + chip], device_id=dev(peer * 2 + core), device_id_type=MESH,
        )
        copy.start()
        sent.append(copy)
    for k in range(1, chips):
        src = (chip + chips - k) % chips
        pltpu.make_async_remote_copy(
            src_ref=held.at[src], dst_ref=held.at[src], send_sem=send_sem.at[1 + src],
            recv_sem=recv_sem.at[1 + src], device_id=dev(src * 2 + core), device_id_type=MESH,
        ).wait_recv()
    for copy in sent:
        copy.wait_send()
    total = held[0].astype(jnp.float32)
    for c in range(1, chips):
        total = total + held[c].astype(jnp.float32)
    out_ref[...] = total.astype(out_ref.dtype)


def grp_rows_sum(x, chips):
    return pl.pallas_call(
        functools.partial(_rows_kernel, chips),
        out_shape=jax.ShapeDtypeStruct(x.shape, x.dtype),
        in_specs=[pl.BlockSpec(memory_space=pltpu.VMEM)],
        out_specs=pl.BlockSpec(memory_space=pltpu.VMEM),
        scratch_shapes=[
            pltpu.VMEM(x.shape, x.dtype),
            pltpu.VMEM((chips, *x.shape), x.dtype),
            pltpu.SemaphoreType.DMA((chips + 1,)),
            pltpu.SemaphoreType.DMA((chips + 1,)),
        ],
        compiler_params=pltpu.CompilerParams(collective_id=2, has_side_effects=True),
    )(x)


def _cross_kernel(zs, bands, scaling, spec_ref, valid_ref, sel_ref, cross_ref, bins_ref, held, stage, picked,
                  send_sem, recv_ring, recv_x, recv_sib, out_sem, recv_f, x_ref, left_ref, power, summed, parts,
                  send_a, recv_a, send_b, recv_b):
    me = lax.axis_index("grp")
    band = lax.axis_index("freq")
    c = me % 2
    xl = (me // 2) % 2
    z = me // 4
    step = 1 - 2 * c
    width = x_ref.shape[0]
    half = width // 2

    def blk(zz, xx, cc):
        return (zz * 2 + xx) * 2 + cc

    def dev(g):
        return (g, band)

    sib = blk(z, xl, 1 - c)
    partner = blk(z, 1 - xl, c)
    nxt = blk((z + step + zs) % zs, xl, c)
    prv = blk((z - step + zs) % zs, xl, c)

    barrier = pltpu.get_barrier_semaphore()
    for g in (sib, partner, nxt, prv):
        pl.semaphore_signal(barrier, inc=1, device_id=dev(g), device_id_type=MESH)
    for k in range(1, bands):
        pl.semaphore_signal(barrier, inc=1, device_id=(me, (band + k) % bands), device_id_type=MESH)
    pl.semaphore_wait(barrier, 4 + bands - 1)
    _whiten_kernel(bands, False, spec_ref, valid_ref, x_ref, left_ref, power, summed, parts,
                   send_a, recv_a, send_b, recv_b)

    sends = []
    outs = []

    def send(src, dst, recv, g):
        copy = pltpu.make_async_remote_copy(
            src_ref=src, dst_ref=dst, send_sem=send_sem.at[len(sends)], recv_sem=recv,
            device_id=dev(g), device_id_type=MESH,
        )
        copy.start()
        sends.append(copy)

    def wait(dst, recv, g):
        pltpu.make_async_remote_copy(
            src_ref=dst, dst_ref=dst, send_sem=send_sem.at[0], recv_sem=recv,
            device_id=dev(g), device_id_type=MESH,
        ).wait_recv()

    def rows(b, h):
        return held.at[b, pl.ds(pl.multiple_of(h * half, half), half)]

    def compute(b):
        block = held[b]
        prod = lax.dot_general(
            left_ref[...], block, (((1,), (1,)), ((), ())), preferred_element_type=jnp.float32
        )
        slot = len(outs) % 2
        if len(outs) >= 2:
            outs[-2].wait()
        stage[slot] = (prod * scaling).astype(stage.dtype).reshape(stage.shape[1:])
        copy = pltpu.make_async_copy(
            stage.at[slot], cross_ref.at[:, :, pl.ds(pl.multiple_of(b * width, width), width)], out_sem.at[slot]
        )
        copy.start()
        outs.append(copy)
        columns = b * width + lax.broadcasted_iota(jnp.int32, (stations, width), 1)
        chosen = (station_ids == columns).astype(block.dtype)
        picked[...] += jnp.dot(chosen, block, preferred_element_type=jnp.float32)

    picked[...] = jnp.zeros_like(picked)
    stations = picked.shape[0]
    place = lax.broadcasted_iota(jnp.int32, (stations, width), 0)
    station_ids = jnp.zeros((stations, width), jnp.int32)
    for k in range(stations):
        station_ids = jnp.where(place == k, sel_ref[k], station_ids)
    own = blk(z, xl, c)
    held[own] = x_ref[...]
    send(x_ref, held.at[own], recv_x.at[0], partner)
    send(x_ref, held.at[own], recv_sib.at[0], sib)
    send(x_ref.at[pl.ds(0, half)], rows(own, 0), recv_ring.at[0, 0], nxt)
    send(x_ref.at[pl.ds(half, half)], rows(own, 1), recv_ring.at[0, 1], nxt)
    compute(own)
    across = blk(z, 1 - xl, c)
    wait(held.at[across], recv_x.at[0], partner)
    send(rows(across, xl), rows(across, xl), recv_ring.at[0, 2], nxt)
    send(held.at[across], held.at[across], recv_sib.at[1], sib)
    compute(across)

    def finish(t):
        zo = (z - step * (t + 1) + 2 * zs) % zs
        part = blk(zo, 1 - xl, c)
        wait(rows(part, 1 - xl), recv_x.at[1 + t], partner)
        send(rows(part, 1 - xl), rows(part, 1 - xl), recv_sib.at[2 + 3 * (zs - 1) + t], sib)
        compute(part)
        zt = (z + step * (t + 1) + 2 * zs) % zs
        sfull = blk(zt, xl, 1 - c)
        spart = blk(zt, 1 - xl, 1 - c)
        for k, (b, h) in enumerate(((sfull, 0), (sfull, 1), (spart, xl))):
            wait(rows(b, h), recv_sib.at[2 + 3 * t + k], sib)
        compute(sfull)
        wait(rows(spart, 1 - xl), recv_sib.at[2 + 3 * (zs - 1) + t], sib)
        compute(spart)

    for s in range(zs - 1):
        zo = (z - step * (s + 1) + 2 * zs) % zs
        full = blk(zo, xl, c)
        part = blk(zo, 1 - xl, c)
        pieces = ((full, 0), (full, 1), (part, xl))
        for k, (b, h) in enumerate(pieces):
            wait(rows(b, h), recv_ring.at[s, k], prv)
            if s < zs - 2:
                send(rows(b, h), rows(b, h), recv_ring.at[s + 1, k], nxt)
            send(rows(b, h), rows(b, h), recv_sib.at[2 + 3 * s + k], sib)
        send(rows(full, xl), rows(full, xl), recv_x.at[1 + s], partner)
        compute(full)
        if s == 0:
            wait(held.at[sib], recv_sib.at[0], sib)
            compute(sib)
            sib_across = blk(z, 1 - xl, 1 - c)
            wait(held.at[sib_across], recv_sib.at[1], sib)
            compute(sib_across)
        else:
            finish(s - 1)
    finish(zs - 2)
    station = picked[...]
    wide = station.shape[1] // 2
    swapped = jnp.concatenate([station[:, wide:], -station[:, :wide]], axis=1)
    left = jnp.concatenate([station, swapped], axis=0).astype(x_ref.dtype)
    values = lax.dot_general(
        left, x_ref[...], (((1,), (1,)), ((), ())), preferred_element_type=jnp.float32
    ) * scaling
    bins_ref[band] = values.reshape(bins_ref.shape[1:])
    for k in range(1, bands):
        peer = (band + k) % bands
        copy = pltpu.make_async_remote_copy(
            src_ref=bins_ref.at[band], dst_ref=bins_ref.at[band], send_sem=send_sem.at[len(sends)],
            recv_sem=recv_f.at[band], device_id=(me, peer), device_id_type=MESH,
        )
        copy.start()
        sends.append(copy)
    for k in range(1, bands):
        src = (band + bands - k) % bands
        pltpu.make_async_remote_copy(
            src_ref=bins_ref.at[src], dst_ref=bins_ref.at[src], send_sem=send_sem.at[0],
            recv_sem=recv_f.at[src], device_id=(me, src), device_id_type=MESH,
        ).wait_recv()
    for copy in outs[-2:]:
        copy.wait()
    for copy in sends:
        copy.wait_send()


def grp_cross(spectra, valid, selector, scaling, zs):
    groups = lax.axis_size("grp")
    bands = lax.axis_size("freq")
    width, cols = spectra.shape
    whitened = spectra
    wide = cols // 2
    return pl.pallas_call(
        functools.partial(_cross_kernel, zs, bands, scaling),
        out_shape=(
            jax.ShapeDtypeStruct((2, width, groups * width), whitened.dtype),
            jax.ShapeDtypeStruct((bands, 2, selector.shape[0], width), jnp.float32),
        ),
        in_specs=[pl.BlockSpec(memory_space=pltpu.VMEM)] * 2 + [pl.BlockSpec(memory_space=pltpu.SMEM)],
        out_specs=(pl.BlockSpec(memory_space=pl.ANY), pl.BlockSpec(memory_space=pltpu.VMEM)),
        scratch_shapes=[
            pltpu.VMEM((groups, width, cols), whitened.dtype),
            pltpu.VMEM((2, 2, width, width), whitened.dtype),
            pltpu.VMEM((selector.shape[0], cols), jnp.float32),
            pltpu.SemaphoreType.DMA((8 * zs + 16,)),
            pltpu.SemaphoreType.DMA((zs - 1, 3)),
            pltpu.SemaphoreType.DMA((zs,)),
            pltpu.SemaphoreType.DMA((2 + 4 * (zs - 1),)),
            pltpu.SemaphoreType.DMA((2,)),
            pltpu.SemaphoreType.DMA((bands,)),
            pltpu.VMEM((width, cols), spectra.dtype),
            pltpu.VMEM((2 * width, cols), spectra.dtype),
            pltpu.VMEM((width, wide), jnp.float32),
            pltpu.VMEM((width, wide), jnp.float32),
            pltpu.VMEM((bands, width // bands, wide), jnp.float32),
            pltpu.SemaphoreType.DMA((bands,)),
            pltpu.SemaphoreType.DMA((bands,)),
            pltpu.SemaphoreType.DMA((bands,)),
            pltpu.SemaphoreType.DMA((bands,)),
        ],
        compiler_params=pltpu.CompilerParams(
            collective_id=3, has_side_effects=True, vmem_limit_bytes=56 * 1024 * 1024
        ),
    )(spectra, valid, selector)


def on_device(spectra, valid, station_index):
    bin_count, chan_count, double_width = spectra.shape
    window_count = double_width // 2
    freq_count = lax.axis_size("freq")
    total_bins = bin_count * freq_count
    scaling = 1.0 / math.sqrt(window_count)
    station_count = station_index.shape[0]
    selector = station_index
    cross, all_bins = grp_cross(
        spectra[0], valid, selector, scaling, lax.axis_size("grp") // 4
    )
    cross = cross[None]

    lag_share = LAGS // freq_count
    freq_index = lax.axis_index("freq")
    bin_values = jnp.arange(total_bins, dtype=jnp.float32) + 1.0
    lag_values = (freq_index * lag_share + jnp.arange(lag_share, dtype=jnp.int32)).astype(jnp.float32)
    phase = math.pi * bin_values[:, None] * lag_values[None, :] / LAGS
    lag_table = jnp.stack([jnp.cos(phase), -jnp.sin(phase)], axis=1)
    station_gather = jnp.einsum(
        "frsc,frl->scl", all_bins, lag_table, precision=lax.Precision.HIGHEST
    ) / math.sqrt(total_bins)
    return (cross, station_gather)


def solution(mesh):
    placed = (P("freq", "grp", None), P("grp", None), P())
    return jax.shard_map(
        on_device,
        mesh=mesh,
        in_specs=placed,
        out_specs=(P("freq", None, "grp", None), P(None, "grp", "freq")),
        check_vma=False,
    )
```

```python
import functools
import math

import jax
import jax.numpy as jnp
from jax import lax
from jax.experimental import pallas as pl
from jax.experimental.pallas import tpu as pltpu
from jax.sharding import PartitionSpec as P

LAGS = 256
MESH = pl.DeviceIdType.MESH


def _greet(peers, here):
    barrier = pltpu.get_barrier_semaphore()
    for k in range(1, peers):
        pl.semaphore_signal(barrier, inc=1, device_id=here((lax.axis_index("freq") + k) % peers), device_id_type=MESH)
    pl.semaphore_wait(barrier, peers - 1)


def _whiten_kernel(peers, greet, spec_ref, valid_ref, white_ref, left_ref, x_ref, out_ref, parts,
                   send_a, recv_a, send_b, recv_b):
    me = lax.axis_index("freq")
    grp = lax.axis_index("grp")
    rows = x_ref.shape[0] // peers
    wide = x_ref.shape[1]

    def here(peer):
        return (grp, peer)

    spectrum = spec_ref[...].astype(jnp.float32)
    real_part = spectrum[:, :wide]
    imag_part = spectrum[:, wide:]
    x_ref[...] = real_part * real_part + imag_part * imag_part
    if greet:
        _greet(peers, here)
    scatter = []
    for k in range(1, peers):
        peer = (me + k) % peers
        copy = pltpu.make_async_remote_copy(
            src_ref=x_ref.at[pl.ds(pl.multiple_of(peer * rows, rows), rows)],
            dst_ref=parts.at[me],
            send_sem=send_a.at[peer],
            recv_sem=recv_a.at[me],
            device_id=here(peer),
            device_id_type=MESH,
        )
        copy.start()
        scatter.append(copy)
    own = x_ref[pl.ds(pl.multiple_of(me * rows, rows), rows), :]
    for k in range(1, peers):
        src = (me + peers - k) % peers
        pltpu.make_async_remote_copy(
            src_ref=x_ref.at[pl.ds(0, rows)],
            dst_ref=parts.at[src],
            send_sem=send_a.at[src],
            recv_sem=recv_a.at[src],
            device_id=here(src),
            device_id_type=MESH,
        ).wait_recv()
    for copy in scatter:
        copy.wait_send()
    parts[me] = own
    total = parts[0]
    for src in range(1, peers):
        total = total + parts[src]
    out_ref[pl.ds(pl.multiple_of(me * rows, rows), rows), :] = total
    gather = []
    for k in range(1, peers):
        peer = (me + k) % peers
        copy = pltpu.make_async_remote_copy(
            src_ref=out_ref.at[pl.ds(pl.multiple_of(me * rows, rows), rows)],
            dst_ref=out_ref.at[pl.ds(pl.multiple_of(me * rows, rows), rows)],
            send_sem=send_b.at[peer],
            recv_sem=recv_b.at[me],
            device_id=here(peer),
            device_id_type=MESH,
        )
        copy.start()
        gather.append(copy)
    for k in range(1, peers):
        src = (me + peers - k) % peers
        pltpu.make_async_remote_copy(
            src_ref=out_ref.at[pl.ds(pl.multiple_of(src * rows, rows), rows)],
            dst_ref=out_ref.at[pl.ds(pl.multiple_of(src * rows, rows), rows)],
            send_sem=send_b.at[src],
            recv_sem=recv_b.at[src],
            device_id=here(src),
            device_id_type=MESH,
        ).wait_recv()
    for copy in gather:
        copy.wait_send()
    factor = lax.rsqrt(out_ref[...] / peers + 1e-05)
    factor = factor * valid_ref[...].astype(jnp.float32)
    white = (spectrum * jnp.concatenate([factor, factor], axis=1)).astype(white_ref.dtype)
    white_ref[...] = white
    count = white.shape[0]
    left_ref[pl.ds(0, count), :] = white
    left_ref[pl.ds(count, count), :] = jnp.concatenate([white[:, wide:], -white[:, :wide]], axis=1)


def freq_whiten(spectra, valid, peers):
    chans, double_width = spectra.shape
    wide = double_width // 2
    return pl.pallas_call(
        functools.partial(_whiten_kernel, peers, True),
        out_shape=(
            jax.ShapeDtypeStruct((chans, double_width), spectra.dtype),
            jax.ShapeDtypeStruct((2 * chans, double_width), spectra.dtype),
        ),
        in_specs=[pl.BlockSpec(memory_space=pltpu.VMEM)] * 2,
        out_specs=(pl.BlockSpec(memory_space=pltpu.VMEM), pl.BlockSpec(memory_space=pltpu.VMEM)),
        scratch_shapes=[
            pltpu.VMEM((chans, wide), jnp.float32),
            pltpu.VMEM((chans, wide), jnp.float32),
            pltpu.VMEM((peers, chans // peers, wide), jnp.float32),
            pltpu.SemaphoreType.DMA((peers,)),
            pltpu.SemaphoreType.DMA((peers,)),
            pltpu.SemaphoreType.DMA((peers,)),
            pltpu.SemaphoreType.DMA((peers,)),
        ],
        compiler_params=pltpu.CompilerParams(collective_id=0, has_side_effects=True),
    )(spectra, valid)


def _gather_kernel(peers, x_ref, out_ref, send_sem, recv_sem):
    me = lax.axis_index("freq")
    grp = lax.axis_index("grp")

    def here(peer):
        return (grp, peer)

    _greet(peers, here)
    sent = []
    for k in range(1, peers):
        peer = (me + k) % peers
        copy = pltpu.make_async_remote_copy(
            src_ref=x_ref,
            dst_ref=out_ref.at[me],
            send_sem=send_sem.at[peer],
            recv_sem=recv_sem.at[me],
            device_id=here(peer),
            device_id_type=MESH,
        )
        copy.start()
        sent.append(copy)
    out_ref[me] = x_ref[...]
    for k in range(1, peers):
        src = (me + peers - k) % peers
        pltpu.make_async_remote_copy(
            src_ref=x_ref,
            dst_ref=out_ref.at[src],
            send_sem=send_sem.at[src],
            recv_sem=recv_sem.at[src],
            device_id=here(src),
            device_id_type=MESH,
        ).wait_recv()
    for copy in sent:
        copy.wait_send()


def freq_gather(x, peers):
    return pl.pallas_call(
        functools.partial(_gather_kernel, peers),
        out_shape=jax.ShapeDtypeStruct((peers, *x.shape), x.dtype),
        in_specs=[pl.BlockSpec(memory_space=pltpu.VMEM)],
        out_specs=pl.BlockSpec(memory_space=pltpu.VMEM),
        scratch_shapes=[
            pltpu.SemaphoreType.DMA((peers,)),
            pltpu.SemaphoreType.DMA((peers,)),
        ],
        compiler_params=pltpu.CompilerParams(collective_id=1, has_side_effects=True),
    )(x)


def _rows_kernel(chips, x_ref, out_ref, pair, held, send_sem, recv_sem):
    me = lax.axis_index("grp")
    band = lax.axis_index("freq")
    core = me % 2
    chip = me // 2
    partner = me + 1 - 2 * core

    def dev(g):
        return (g, band)

    barrier = pltpu.get_barrier_semaphore()
    pl.semaphore_signal(barrier, inc=1, device_id=dev(partner), device_id_type=MESH)
    for k in range(1, chips):
        pl.semaphore_signal(barrier, inc=1, device_id=dev(((chip + k) % chips) * 2 + core), device_id_type=MESH)
    pl.semaphore_wait(barrier, chips)

    first = pltpu.make_async_remote_copy(
        src_ref=x_ref, dst_ref=pair, send_sem=send_sem.at[0], recv_sem=recv_sem.at[0],
        device_id=dev(partner), device_id_type=MESH,
    )
    first.start()
    first.wait_recv()
    first.wait_send()
    held[chip] = (x_ref[...].astype(jnp.float32) + pair[...].astype(jnp.float32)).astype(held.dtype)
    sent = []
    for k in range(1, chips):
        peer = (chip + k) % chips
        copy = pltpu.make_async_remote_copy(
            src_ref=held.at[chip], dst_ref=held.at[chip], send_sem=send_sem.at[1 + peer],
            recv_sem=recv_sem.at[1 + chip], device_id=dev(peer * 2 + core), device_id_type=MESH,
        )
        copy.start()
        sent.append(copy)
    for k in range(1, chips):
        src = (chip + chips - k) % chips
        pltpu.make_async_remote_copy(
            src_ref=held.at[src], dst_ref=held.at[src], send_sem=send_sem.at[1 + src],
            recv_sem=recv_sem.at[1 + src], device_id=dev(src * 2 + core), device_id_type=MESH,
        ).wait_recv()
    for copy in sent:
        copy.wait_send()
    total = held[0].astype(jnp.float32)
    for c in range(1, chips):
        total = total + held[c].astype(jnp.float32)
    out_ref[...] = total.astype(out_ref.dtype)


def grp_rows_sum(x, chips):
    return pl.pallas_call(
        functools.partial(_rows_kernel, chips),
        out_shape=jax.ShapeDtypeStruct(x.shape, x.dtype),
        in_specs=[pl.BlockSpec(memory_space=pltpu.VMEM)],
        out_specs=pl.BlockSpec(memory_space=pltpu.VMEM),
        scratch_shapes=[
            pltpu.VMEM(x.shape, x.dtype),
            pltpu.VMEM((chips, *x.shape), x.dtype),
            pltpu.SemaphoreType.DMA((chips + 1,)),
            pltpu.SemaphoreType.DMA((chips + 1,)),
        ],
        compiler_params=pltpu.CompilerParams(collective_id=2, has_side_effects=True),
    )(x)


def _cross_kernel(zs, bands, scaling, spec_ref, valid_ref, sel_ref, cross_ref, bins_ref, held, stage, picked,
                  send_sem, recv_ring, recv_x, recv_sib, out_sem, recv_f, x_ref, left_ref, power, summed, parts,
                  send_a, recv_a, send_b, recv_b):
    me = lax.axis_index("grp")
    band = lax.axis_index("freq")
    c = me % 2
    xl = (me // 2) % 2
    z = me // 4
    step = 1 - 2 * c
    width = x_ref.shape[0]
    half = width // 2

    def blk(zz, xx, cc):
        return (zz * 2 + xx) * 2 + cc

    def dev(g):
        return (g, band)

    sib = blk(z, xl, 1 - c)
    partner = blk(z, 1 - xl, c)
    nxt = blk((z + step + zs) % zs, xl, c)
    prv = blk((z - step + zs) % zs, xl, c)

    barrier = pltpu.get_barrier_semaphore()
    for g in (sib, partner, nxt, prv):
        pl.semaphore_signal(barrier, inc=1, device_id=dev(g), device_id_type=MESH)
    for k in range(1, bands):
        pl.semaphore_signal(barrier, inc=1, device_id=(me, (band + k) % bands), device_id_type=MESH)
    pl.semaphore_wait(barrier, 4 + bands - 1)
    _whiten_kernel(bands, False, spec_ref, valid_ref, x_ref, left_ref, power, summed, parts,
                   send_a, recv_a, send_b, recv_b)

    sends = []
    outs = []

    def send(src, dst, recv, g):
        copy = pltpu.make_async_remote_copy(
            src_ref=src, dst_ref=dst, send_sem=send_sem.at[len(sends)], recv_sem=recv,
            device_id=dev(g), device_id_type=MESH,
        )
        copy.start()
        sends.append(copy)

    def wait(dst, recv, g):
        pltpu.make_async_remote_copy(
            src_ref=dst, dst_ref=dst, send_sem=send_sem.at[0], recv_sem=recv,
            device_id=dev(g), device_id_type=MESH,
        ).wait_recv()

    def rows(b, h):
        return held.at[b, pl.ds(pl.multiple_of(h * half, half), half)]

    def compute(b):
        block = held[b]
        prod = lax.dot_general(
            left_ref[...], block, (((1,), (1,)), ((), ())), preferred_element_type=jnp.float32
        )
        slot = len(outs) % 2
        if len(outs) >= 2:
            outs[-2].wait()
        stage[slot] = (prod * scaling).astype(stage.dtype).reshape(stage.shape[1:])
        copy = pltpu.make_async_copy(
            stage.at[slot], cross_ref.at[:, :, pl.ds(pl.multiple_of(b * width, width), width)], out_sem.at[slot]
        )
        copy.start()
        outs.append(copy)
        columns = b * width + lax.broadcasted_iota(jnp.int32, (stations, width), 1)
        chosen = (station_ids == columns).astype(block.dtype)
        picked[...] += jnp.dot(chosen, block, preferred_element_type=jnp.float32)

    picked[...] = jnp.zeros_like(picked)
    stations = picked.shape[0]
    place = lax.broadcasted_iota(jnp.int32, (stations, width), 0)
    station_ids = jnp.zeros((stations, width), jnp.int32)
    for k in range(stations):
        station_ids = jnp.where(place == k, sel_ref[k], station_ids)
    own = blk(z, xl, c)
    held[own] = x_ref[...]
    send(x_ref, held.at[own], recv_x.at[0], partner)
    send(x_ref, held.at[own], recv_sib.at[0], sib)
    send(x_ref.at[pl.ds(0, half)], rows(own, 0), recv_ring.at[0, 0], nxt)
    send(x_ref.at[pl.ds(half, half)], rows(own, 1), recv_ring.at[0, 1], nxt)
    compute(own)
    across = blk(z, 1 - xl, c)
    wait(held.at[across], recv_x.at[0], partner)
    send(rows(across, xl), rows(across, xl), recv_ring.at[0, 2], nxt)
    send(held.at[across], held.at[across], recv_sib.at[1], sib)
    compute(across)

    def finish(t):
        zo = (z - step * (t + 1) + 2 * zs) % zs
        part = blk(zo, 1 - xl, c)
        zt = (z + step * (t + 1) + 2 * zs) % zs
        sfull = blk(zt, xl, 1 - c)
        spart = blk(zt, 1 - xl, 1 - c)

        def first():
            wait(rows(part, 1 - xl), recv_x.at[1 + t], partner)
            send(rows(part, 1 - xl), rows(part, 1 - xl), recv_sib.at[2 + 3 * (zs - 1) + t], sib)
            compute(part)

        def second():
            for k, (b, h) in enumerate(((sfull, 0), (sfull, 1), (spart, xl))):
                wait(rows(b, h), recv_sib.at[2 + 3 * t + k], sib)
            compute(sfull)

        def third():
            wait(rows(spart, 1 - xl), recv_sib.at[2 + 3 * (zs - 1) + t], sib)
            compute(spart)

        return [first, second, third]

    def sibling_own():
        wait(held.at[sib], recv_sib.at[0], sib)
        compute(sib)

    def sibling_across():
        sib_across = blk(z, 1 - xl, 1 - c)
        wait(held.at[sib_across], recv_sib.at[1], sib)
        compute(sib_across)

    pending = []

    def one():
        if pending:
            pending.pop(0)()

    for s in range(zs - 1):
        zo = (z - step * (s + 1) + 2 * zs) % zs
        full = blk(zo, xl, c)
        part = blk(zo, 1 - xl, c)
        pieces = ((full, 0), (full, 1), (part, xl))
        for k, (b, h) in enumerate(pieces):
            wait(rows(b, h), recv_ring.at[s, k], prv)
            if s < zs - 2:
                send(rows(b, h), rows(b, h), recv_ring.at[s + 1, k], nxt)
            send(rows(b, h), rows(b, h), recv_sib.at[2 + 3 * s + k], sib)
            one()
        send(rows(full, xl), rows(full, xl), recv_x.at[1 + s], partner)
        pending.append(functools.partial(compute, full))
        if s == 0:
            pending.extend([sibling_own, sibling_across])
        else:
            pending.extend(finish(s - 1))
        one()
    pending.extend(finish(zs - 2))
    while pending:
        one()
    station = picked[...]
    wide = station.shape[1] // 2
    swapped = jnp.concatenate([station[:, wide:], -station[:, :wide]], axis=1)
    left = jnp.concatenate([station, swapped], axis=0).astype(x_ref.dtype)
    values = lax.dot_general(
        left, x_ref[...], (((1,), (1,)), ((), ())), preferred_element_type=jnp.float32
    ) * scaling
    bins_ref[band] = values.reshape(bins_ref.shape[1:])
    for k in range(1, bands):
        peer = (band + k) % bands
        copy = pltpu.make_async_remote_copy(
            src_ref=bins_ref.at[band], dst_ref=bins_ref.at[band], send_sem=send_sem.at[len(sends)],
            recv_sem=recv_f.at[band], device_id=(me, peer), device_id_type=MESH,
        )
        copy.start()
        sends.append(copy)
    for k in range(1, bands):
        src = (band + bands - k) % bands
        pltpu.make_async_remote_copy(
            src_ref=bins_ref.at[src], dst_ref=bins_ref.at[src], send_sem=send_sem.at[0],
            recv_sem=recv_f.at[src], device_id=(me, src), device_id_type=MESH,
        ).wait_recv()
    for copy in outs[-2:]:
        copy.wait()
    for copy in sends:
        copy.wait_send()


def grp_cross(spectra, valid, selector, scaling, zs):
    groups = lax.axis_size("grp")
    bands = lax.axis_size("freq")
    width, cols = spectra.shape
    whitened = spectra
    wide = cols // 2
    return pl.pallas_call(
        functools.partial(_cross_kernel, zs, bands, scaling),
        out_shape=(
            jax.ShapeDtypeStruct((2, width, groups * width), whitened.dtype),
            jax.ShapeDtypeStruct((bands, 2, selector.shape[0], width), jnp.float32),
        ),
        in_specs=[pl.BlockSpec(memory_space=pltpu.VMEM)] * 2 + [pl.BlockSpec(memory_space=pltpu.SMEM)],
        out_specs=(pl.BlockSpec(memory_space=pl.ANY), pl.BlockSpec(memory_space=pltpu.VMEM)),
        scratch_shapes=[
            pltpu.VMEM((groups, width, cols), whitened.dtype),
            pltpu.VMEM((2, 2, width, width), whitened.dtype),
            pltpu.VMEM((selector.shape[0], cols), jnp.float32),
            pltpu.SemaphoreType.DMA((8 * zs + 16,)),
            pltpu.SemaphoreType.DMA((zs - 1, 3)),
            pltpu.SemaphoreType.DMA((zs,)),
            pltpu.SemaphoreType.DMA((2 + 4 * (zs - 1),)),
            pltpu.SemaphoreType.DMA((2,)),
            pltpu.SemaphoreType.DMA((bands,)),
            pltpu.VMEM((width, cols), spectra.dtype),
            pltpu.VMEM((2 * width, cols), spectra.dtype),
            pltpu.VMEM((width, wide), jnp.float32),
            pltpu.VMEM((width, wide), jnp.float32),
            pltpu.VMEM((bands, width // bands, wide), jnp.float32),
            pltpu.SemaphoreType.DMA((bands,)),
            pltpu.SemaphoreType.DMA((bands,)),
            pltpu.SemaphoreType.DMA((bands,)),
            pltpu.SemaphoreType.DMA((bands,)),
        ],
        compiler_params=pltpu.CompilerParams(
            collective_id=3, has_side_effects=True, vmem_limit_bytes=56 * 1024 * 1024
        ),
    )(spectra, valid, selector)


def on_device(spectra, valid, station_index):
    bin_count, chan_count, double_width = spectra.shape
    window_count = double_width // 2
    freq_count = lax.axis_size("freq")
    total_bins = bin_count * freq_count
    scaling = 1.0 / math.sqrt(window_count)
    station_count = station_index.shape[0]
    selector = station_index
    cross, all_bins = grp_cross(
        spectra[0], valid, selector, scaling, lax.axis_size("grp") // 4
    )
    cross = cross[None]

    lag_share = LAGS // freq_count
    freq_index = lax.axis_index("freq")
    bin_values = jnp.arange(total_bins, dtype=jnp.float32) + 1.0
    lag_values = (freq_index * lag_share + jnp.arange(lag_share, dtype=jnp.int32)).astype(jnp.float32)
    phase = math.pi * bin_values[:, None] * lag_values[None, :] / LAGS
    lag_table = jnp.stack([jnp.cos(phase), -jnp.sin(phase)], axis=1)
    station_gather = jnp.einsum(
        "frsc,frl->scl", all_bins, lag_table, precision=lax.Precision.HIGHEST
    ) / math.sqrt(total_bins)
    return (cross, station_gather)


def solution(mesh):
    placed = (P("freq", "grp", None), P("grp", None), P())
    return jax.shard_map(
        on_device,
        mesh=mesh,
        in_specs=placed,
        out_specs=(P("freq", None, "grp", None), P(None, "grp", "freq")),
        check_vma=False,
    )
```

```python
import functools
import math

import jax
import jax.numpy as jnp
from jax import lax
from jax.experimental import pallas as pl
from jax.experimental.pallas import tpu as pltpu
from jax.sharding import PartitionSpec as P

LAGS = 256
MESH = pl.DeviceIdType.MESH


def _greet(peers, here):
    barrier = pltpu.get_barrier_semaphore()
    for k in range(1, peers):
        pl.semaphore_signal(barrier, inc=1, device_id=here((lax.axis_index("freq") + k) % peers), device_id_type=MESH)
    pl.semaphore_wait(barrier, peers - 1)


def _whiten_kernel(peers, greet, spec_ref, valid_ref, white_ref, left_ref, x_ref, out_ref, parts,
                   send_a, recv_a, send_b, recv_b):
    me = lax.axis_index("freq")
    grp = lax.axis_index("grp")
    rows = x_ref.shape[0] // peers
    wide = x_ref.shape[1]

    def here(peer):
        return (grp, peer)

    spectrum = spec_ref[...].astype(jnp.float32)
    real_part = spectrum[:, :wide]
    imag_part = spectrum[:, wide:]
    x_ref[...] = real_part * real_part + imag_part * imag_part
    if greet:
        _greet(peers, here)
    scatter = []
    for k in range(1, peers):
        peer = (me + k) % peers
        copy = pltpu.make_async_remote_copy(
            src_ref=x_ref.at[pl.ds(pl.multiple_of(peer * rows, rows), rows)],
            dst_ref=parts.at[me],
            send_sem=send_a.at[peer],
            recv_sem=recv_a.at[me],
            device_id=here(peer),
            device_id_type=MESH,
        )
        copy.start()
        scatter.append(copy)
    own = x_ref[pl.ds(pl.multiple_of(me * rows, rows), rows), :]
    for k in range(1, peers):
        src = (me + peers - k) % peers
        pltpu.make_async_remote_copy(
            src_ref=x_ref.at[pl.ds(0, rows)],
            dst_ref=parts.at[src],
            send_sem=send_a.at[src],
            recv_sem=recv_a.at[src],
            device_id=here(src),
            device_id_type=MESH,
        ).wait_recv()
    for copy in scatter:
        copy.wait_send()
    parts[me] = own
    total = parts[0]
    for src in range(1, peers):
        total = total + parts[src]
    out_ref[pl.ds(pl.multiple_of(me * rows, rows), rows), :] = total
    gather = []
    for k in range(1, peers):
        peer = (me + k) % peers
        copy = pltpu.make_async_remote_copy(
            src_ref=out_ref.at[pl.ds(pl.multiple_of(me * rows, rows), rows)],
            dst_ref=out_ref.at[pl.ds(pl.multiple_of(me * rows, rows), rows)],
            send_sem=send_b.at[peer],
            recv_sem=recv_b.at[me],
            device_id=here(peer),
            device_id_type=MESH,
        )
        copy.start()
        gather.append(copy)
    for k in range(1, peers):
        src = (me + peers - k) % peers
        pltpu.make_async_remote_copy(
            src_ref=out_ref.at[pl.ds(pl.multiple_of(src * rows, rows), rows)],
            dst_ref=out_ref.at[pl.ds(pl.multiple_of(src * rows, rows), rows)],
            send_sem=send_b.at[src],
            recv_sem=recv_b.at[src],
            device_id=here(src),
            device_id_type=MESH,
        ).wait_recv()
    for copy in gather:
        copy.wait_send()
    factor = lax.rsqrt(out_ref[...] / peers + 1e-05)
    factor = factor * valid_ref[...].astype(jnp.float32)
    white = (spectrum * jnp.concatenate([factor, factor], axis=1)).astype(white_ref.dtype)
    white_ref[...] = white
    count = white.shape[0]
    left_ref[pl.ds(0, count), :] = white
    left_ref[pl.ds(count, count), :] = jnp.concatenate([white[:, wide:], -white[:, :wide]], axis=1)


def freq_whiten(spectra, valid, peers):
    chans, double_width = spectra.shape
    wide = double_width // 2
    return pl.pallas_call(
        functools.partial(_whiten_kernel, peers, True),
        out_shape=(
            jax.ShapeDtypeStruct((chans, double_width), spectra.dtype),
            jax.ShapeDtypeStruct((2 * chans, double_width), spectra.dtype),
        ),
        in_specs=[pl.BlockSpec(memory_space=pltpu.VMEM)] * 2,
        out_specs=(pl.BlockSpec(memory_space=pltpu.VMEM), pl.BlockSpec(memory_space=pltpu.VMEM)),
        scratch_shapes=[
            pltpu.VMEM((chans, wide), jnp.float32),
            pltpu.VMEM((chans, wide), jnp.float32),
            pltpu.VMEM((peers, chans // peers, wide), jnp.float32),
            pltpu.SemaphoreType.DMA((peers,)),
            pltpu.SemaphoreType.DMA((peers,)),
            pltpu.SemaphoreType.DMA((peers,)),
            pltpu.SemaphoreType.DMA((peers,)),
        ],
        compiler_params=pltpu.CompilerParams(collective_id=0, has_side_effects=True),
    )(spectra, valid)


def _gather_kernel(peers, x_ref, out_ref, send_sem, recv_sem):
    me = lax.axis_index("freq")
    grp = lax.axis_index("grp")

    def here(peer):
        return (grp, peer)

    _greet(peers, here)
    sent = []
    for k in range(1, peers):
        peer = (me + k) % peers
        copy = pltpu.make_async_remote_copy(
            src_ref=x_ref,
            dst_ref=out_ref.at[me],
            send_sem=send_sem.at[peer],
            recv_sem=recv_sem.at[me],
            device_id=here(peer),
            device_id_type=MESH,
        )
        copy.start()
        sent.append(copy)
    out_ref[me] = x_ref[...]
    for k in range(1, peers):
        src = (me + peers - k) % peers
        pltpu.make_async_remote_copy(
            src_ref=x_ref,
            dst_ref=out_ref.at[src],
            send_sem=send_sem.at[src],
            recv_sem=recv_sem.at[src],
            device_id=here(src),
            device_id_type=MESH,
        ).wait_recv()
    for copy in sent:
        copy.wait_send()


def freq_gather(x, peers):
    return pl.pallas_call(
        functools.partial(_gather_kernel, peers),
        out_shape=jax.ShapeDtypeStruct((peers, *x.shape), x.dtype),
        in_specs=[pl.BlockSpec(memory_space=pltpu.VMEM)],
        out_specs=pl.BlockSpec(memory_space=pltpu.VMEM),
        scratch_shapes=[
            pltpu.SemaphoreType.DMA((peers,)),
            pltpu.SemaphoreType.DMA((peers,)),
        ],
        compiler_params=pltpu.CompilerParams(collective_id=1, has_side_effects=True),
    )(x)


def _rows_kernel(chips, x_ref, out_ref, pair, held, send_sem, recv_sem):
    me = lax.axis_index("grp")
    band = lax.axis_index("freq")
    core = me % 2
    chip = me // 2
    partner = me + 1 - 2 * core

    def dev(g):
        return (g, band)

    barrier = pltpu.get_barrier_semaphore()
    pl.semaphore_signal(barrier, inc=1, device_id=dev(partner), device_id_type=MESH)
    for k in range(1, chips):
        pl.semaphore_signal(barrier, inc=1, device_id=dev(((chip + k) % chips) * 2 + core), device_id_type=MESH)
    pl.semaphore_wait(barrier, chips)

    first = pltpu.make_async_remote_copy(
        src_ref=x_ref, dst_ref=pair, send_sem=send_sem.at[0], recv_sem=recv_sem.at[0],
        device_id=dev(partner), device_id_type=MESH,
    )
    first.start()
    first.wait_recv()
    first.wait_send()
    held[chip] = (x_ref[...].astype(jnp.float32) + pair[...].astype(jnp.float32)).astype(held.dtype)
    sent = []
    for k in range(1, chips):
        peer = (chip + k) % chips
        copy = pltpu.make_async_remote_copy(
            src_ref=held.at[chip], dst_ref=held.at[chip], send_sem=send_sem.at[1 + peer],
            recv_sem=recv_sem.at[1 + chip], device_id=dev(peer * 2 + core), device_id_type=MESH,
        )
        copy.start()
        sent.append(copy)
    for k in range(1, chips):
        src = (chip + chips - k) % chips
        pltpu.make_async_remote_copy(
            src_ref=held.at[src], dst_ref=held.at[src], send_sem=send_sem.at[1 + src],
            recv_sem=recv_sem.at[1 + src], device_id=dev(src * 2 + core), device_id_type=MESH,
        ).wait_recv()
    for copy in sent:
        copy.wait_send()
    total = held[0].astype(jnp.float32)
    for c in range(1, chips):
        total = total + held[c].astype(jnp.float32)
    out_ref[...] = total.astype(out_ref.dtype)


def grp_rows_sum(x, chips):
    return pl.pallas_call(
        functools.partial(_rows_kernel, chips),
        out_shape=jax.ShapeDtypeStruct(x.shape, x.dtype),
        in_specs=[pl.BlockSpec(memory_space=pltpu.VMEM)],
        out_specs=pl.BlockSpec(memory_space=pltpu.VMEM),
        scratch_shapes=[
            pltpu.VMEM(x.shape, x.dtype),
            pltpu.VMEM((chips, *x.shape), x.dtype),
            pltpu.SemaphoreType.DMA((chips + 1,)),
            pltpu.SemaphoreType.DMA((chips + 1,)),
        ],
        compiler_params=pltpu.CompilerParams(collective_id=2, has_side_effects=True),
    )(x)


def _cross_kernel(zs, bands, scaling, spec_ref, valid_ref, sel_ref, cross_ref, bins_ref, held, stage, picked,
                  send_sem, recv_ring, recv_x, recv_sib, out_sem, recv_f, x_ref, left_ref, power, summed, parts,
                  send_a, recv_a, send_b, recv_b):
    me = lax.axis_index("grp")
    band = lax.axis_index("freq")
    c = me % 2
    xl = (me // 2) % 2
    z = me // 4
    step = 1 - 2 * c
    width = x_ref.shape[0]
    half = width // 2

    def blk(zz, xx, cc):
        return (zz * 2 + xx) * 2 + cc

    def dev(g):
        return (g, band)

    sib = blk(z, xl, 1 - c)
    partner = blk(z, 1 - xl, c)
    nxt = blk((z + step + zs) % zs, xl, c)
    prv = blk((z - step + zs) % zs, xl, c)

    barrier = pltpu.get_barrier_semaphore()
    for g in (sib, partner, nxt, prv):
        pl.semaphore_signal(barrier, inc=1, device_id=dev(g), device_id_type=MESH)
    for k in range(1, bands):
        pl.semaphore_signal(barrier, inc=1, device_id=(me, (band + k) % bands), device_id_type=MESH)
    pl.semaphore_wait(barrier, 4 + bands - 1)
    _whiten_kernel(bands, False, spec_ref, valid_ref, x_ref, left_ref, power, summed, parts,
                   send_a, recv_a, send_b, recv_b)

    sends = []
    outs = []

    def send(src, dst, recv, g):
        copy = pltpu.make_async_remote_copy(
            src_ref=src, dst_ref=dst, send_sem=send_sem.at[len(sends)], recv_sem=recv,
            device_id=dev(g), device_id_type=MESH,
        )
        copy.start()
        sends.append(copy)

    def wait(dst, recv, g):
        pltpu.make_async_remote_copy(
            src_ref=dst, dst_ref=dst, send_sem=send_sem.at[0], recv_sem=recv,
            device_id=dev(g), device_id_type=MESH,
        ).wait_recv()

    def rows(b, h):
        return held.at[b, pl.ds(pl.multiple_of(h * half, half), half)]

    def compute(b):
        block = held[b]
        prod = lax.dot_general(
            left_ref[...], block, (((1,), (1,)), ((), ())), preferred_element_type=jnp.float32
        )
        slot = len(outs) % 2
        if len(outs) >= 2:
            outs[-2].wait()
        stage[slot] = (prod * scaling).astype(stage.dtype).reshape(stage.shape[1:])
        copy = pltpu.make_async_copy(
            stage.at[slot], cross_ref.at[:, :, pl.ds(pl.multiple_of(b * width, width), width)], out_sem.at[slot]
        )
        copy.start()
        outs.append(copy)
        columns = b * width + lax.broadcasted_iota(jnp.int32, (stations, width), 1)
        chosen = (station_ids == columns).astype(block.dtype)
        picked[...] += jnp.dot(chosen, block, preferred_element_type=jnp.float32)

    picked[...] = jnp.zeros_like(picked)
    stations = picked.shape[0]
    place = lax.broadcasted_iota(jnp.int32, (stations, width), 0)
    station_ids = jnp.zeros((stations, width), jnp.int32)
    for k in range(stations):
        station_ids = jnp.where(place == k, sel_ref[k], station_ids)
    own = blk(z, xl, c)
    held[own] = x_ref[...]
    send(x_ref, held.at[own], recv_x.at[0], partner)
    send(x_ref, held.at[own], recv_sib.at[0], sib)
    send(x_ref.at[pl.ds(0, half)], rows(own, 0), recv_ring.at[0, 0], nxt)
    send(x_ref.at[pl.ds(half, half)], rows(own, 1), recv_ring.at[0, 1], nxt)
    compute(own)
    across = blk(z, 1 - xl, c)
    wait(held.at[across], recv_x.at[0], partner)
    send(rows(across, xl), rows(across, xl), recv_ring.at[0, 2], nxt)
    send(held.at[across], held.at[across], recv_sib.at[1], sib)
    compute(across)

    def finish(t):
        zo = (z - step * (t + 1) + 2 * zs) % zs
        part = blk(zo, 1 - xl, c)
        wait(rows(part, 1 - xl), recv_x.at[1 + t], partner)
        send(rows(part, 1 - xl), rows(part, 1 - xl), recv_sib.at[2 + 3 * (zs - 1) + t], sib)
        compute(part)
        zt = (z + step * (t + 1) + 2 * zs) % zs
        sfull = blk(zt, xl, 1 - c)
        spart = blk(zt, 1 - xl, 1 - c)
        for k, (b, h) in enumerate(((sfull, 0), (sfull, 1), (spart, xl))):
            wait(rows(b, h), recv_sib.at[2 + 3 * t + k], sib)
        compute(sfull)
        wait(rows(spart, 1 - xl), recv_sib.at[2 + 3 * (zs - 1) + t], sib)
        compute(spart)

    for s in range(zs - 1):
        zo = (z - step * (s + 1) + 2 * zs) % zs
        full = blk(zo, xl, c)
        part = blk(zo, 1 - xl, c)
        pieces = ((full, 0), (full, 1), (part, xl))
        for k, (b, h) in enumerate(pieces):
            wait(rows(b, h), recv_ring.at[s, k], prv)
            if s < zs - 2:
                send(rows(b, h), rows(b, h), recv_ring.at[s + 1, k], nxt)
        send(rows(full, xl), rows(full, xl), recv_x.at[1 + s], partner)
        for k, (b, h) in enumerate(pieces):
            send(rows(b, h), rows(b, h), recv_sib.at[2 + 3 * s + k], sib)
        compute(full)
        if s == 0:
            wait(held.at[sib], recv_sib.at[0], sib)
            compute(sib)
            sib_across = blk(z, 1 - xl, 1 - c)
            wait(held.at[sib_across], recv_sib.at[1], sib)
            compute(sib_across)
        else:
            finish(s - 1)
    finish(zs - 2)
    station = picked[...]
    wide = station.shape[1] // 2
    swapped = jnp.concatenate([station[:, wide:], -station[:, :wide]], axis=1)
    left = jnp.concatenate([station, swapped], axis=0).astype(x_ref.dtype)
    values = lax.dot_general(
        left, x_ref[...], (((1,), (1,)), ((), ())), preferred_element_type=jnp.float32
    ) * scaling
    bins_ref[band] = values.reshape(bins_ref.shape[1:])
    for k in range(1, bands):
        peer = (band + k) % bands
        copy = pltpu.make_async_remote_copy(
            src_ref=bins_ref.at[band], dst_ref=bins_ref.at[band], send_sem=send_sem.at[len(sends)],
            recv_sem=recv_f.at[band], device_id=(me, peer), device_id_type=MESH,
        )
        copy.start()
        sends.append(copy)
    for k in range(1, bands):
        src = (band + bands - k) % bands
        pltpu.make_async_remote_copy(
            src_ref=bins_ref.at[src], dst_ref=bins_ref.at[src], send_sem=send_sem.at[0],
            recv_sem=recv_f.at[src], device_id=(me, src), device_id_type=MESH,
        ).wait_recv()
    for copy in outs[-2:]:
        copy.wait()
    for copy in sends:
        copy.wait_send()


def grp_cross(spectra, valid, selector, scaling, zs):
    groups = lax.axis_size("grp")
    bands = lax.axis_size("freq")
    width, cols = spectra.shape
    whitened = spectra
    wide = cols // 2
    return pl.pallas_call(
        functools.partial(_cross_kernel, zs, bands, scaling),
        out_shape=(
            jax.ShapeDtypeStruct((2, width, groups * width), whitened.dtype),
            jax.ShapeDtypeStruct((bands, 2, selector.shape[0], width), jnp.float32),
        ),
        in_specs=[pl.BlockSpec(memory_space=pltpu.VMEM)] * 2 + [pl.BlockSpec(memory_space=pltpu.SMEM)],
        out_specs=(pl.BlockSpec(memory_space=pl.ANY), pl.BlockSpec(memory_space=pltpu.VMEM)),
        scratch_shapes=[
            pltpu.VMEM((groups, width, cols), whitened.dtype),
            pltpu.VMEM((2, 2, width, width), whitened.dtype),
            pltpu.VMEM((selector.shape[0], cols), jnp.float32),
            pltpu.SemaphoreType.DMA((8 * zs + 16,)),
            pltpu.SemaphoreType.DMA((zs - 1, 3)),
            pltpu.SemaphoreType.DMA((zs,)),
            pltpu.SemaphoreType.DMA((2 + 4 * (zs - 1),)),
            pltpu.SemaphoreType.DMA((2,)),
            pltpu.SemaphoreType.DMA((bands,)),
            pltpu.VMEM((width, cols), spectra.dtype),
            pltpu.VMEM((2 * width, cols), spectra.dtype),
            pltpu.VMEM((width, wide), jnp.float32),
            pltpu.VMEM((width, wide), jnp.float32),
            pltpu.VMEM((bands, width // bands, wide), jnp.float32),
            pltpu.SemaphoreType.DMA((bands,)),
            pltpu.SemaphoreType.DMA((bands,)),
            pltpu.SemaphoreType.DMA((bands,)),
            pltpu.SemaphoreType.DMA((bands,)),
        ],
        compiler_params=pltpu.CompilerParams(
            collective_id=3, has_side_effects=True, vmem_limit_bytes=56 * 1024 * 1024
        ),
    )(spectra, valid, selector)


def on_device(spectra, valid, station_index):
    bin_count, chan_count, double_width = spectra.shape
    window_count = double_width // 2
    freq_count = lax.axis_size("freq")
    total_bins = bin_count * freq_count
    scaling = 1.0 / math.sqrt(window_count)
    station_count = station_index.shape[0]
    selector = station_index
    cross, all_bins = grp_cross(
        spectra[0], valid, selector, scaling, lax.axis_size("grp") // 4
    )
    cross = cross[None]

    lag_share = LAGS // freq_count
    freq_index = lax.axis_index("freq")
    bin_values = jnp.arange(total_bins, dtype=jnp.float32) + 1.0
    lag_values = (freq_index * lag_share + jnp.arange(lag_share, dtype=jnp.int32)).astype(jnp.float32)
    phase = math.pi * bin_values[:, None] * lag_values[None, :] / LAGS
    lag_table = jnp.stack([jnp.cos(phase), -jnp.sin(phase)], axis=1)
    station_gather = jnp.einsum(
        "frsc,frl->scl", all_bins, lag_table, precision=lax.Precision.HIGHEST
    ) / math.sqrt(total_bins)
    return (cross, station_gather)


def solution(mesh):
    placed = (P("freq", "grp", None), P("grp", None), P())
    return jax.shard_map(
        on_device,
        mesh=mesh,
        in_specs=placed,
        out_specs=(P("freq", None, "grp", None), P(None, "grp", "freq")),
        check_vma=False,
    )
```

```python
import functools
import math

import jax
import jax.numpy as jnp
from jax import lax
from jax.experimental import pallas as pl
from jax.experimental.pallas import tpu as pltpu
from jax.sharding import PartitionSpec as P

LAGS = 256
MESH = pl.DeviceIdType.MESH


def _greet(peers, here):
    barrier = pltpu.get_barrier_semaphore()
    for k in range(1, peers):
        pl.semaphore_signal(barrier, inc=1, device_id=here((lax.axis_index("freq") + k) % peers), device_id_type=MESH)
    pl.semaphore_wait(barrier, peers - 1)


def _whiten_kernel(peers, greet, spec_ref, valid_ref, white_ref, left_ref, x_ref, out_ref, parts,
                   send_a, recv_a, send_b, recv_b):
    me = lax.axis_index("freq")
    grp = lax.axis_index("grp")
    rows = x_ref.shape[0] // peers
    wide = x_ref.shape[1]

    def here(peer):
        return (grp, peer)

    spectrum = spec_ref[...].astype(jnp.float32)
    real_part = spectrum[:, :wide]
    imag_part = spectrum[:, wide:]
    x_ref[...] = real_part * real_part + imag_part * imag_part
    if greet:
        _greet(peers, here)
    scatter = []
    for k in range(1, peers):
        peer = (me + k) % peers
        copy = pltpu.make_async_remote_copy(
            src_ref=x_ref.at[pl.ds(pl.multiple_of(peer * rows, rows), rows)],
            dst_ref=parts.at[me],
            send_sem=send_a.at[peer],
            recv_sem=recv_a.at[me],
            device_id=here(peer),
            device_id_type=MESH,
        )
        copy.start()
        scatter.append(copy)
    own = x_ref[pl.ds(pl.multiple_of(me * rows, rows), rows), :]
    for k in range(1, peers):
        src = (me + peers - k) % peers
        pltpu.make_async_remote_copy(
            src_ref=x_ref.at[pl.ds(0, rows)],
            dst_ref=parts.at[src],
            send_sem=send_a.at[src],
            recv_sem=recv_a.at[src],
            device_id=here(src),
            device_id_type=MESH,
        ).wait_recv()
    for copy in scatter:
        copy.wait_send()
    parts[me] = own
    total = parts[0]
    for src in range(1, peers):
        total = total + parts[src]
    out_ref[pl.ds(pl.multiple_of(me * rows, rows), rows), :] = total
    gather = []
    for k in range(1, peers):
        peer = (me + k) % peers
        copy = pltpu.make_async_remote_copy(
            src_ref=out_ref.at[pl.ds(pl.multiple_of(me * rows, rows), rows)],
            dst_ref=out_ref.at[pl.ds(pl.multiple_of(me * rows, rows), rows)],
            send_sem=send_b.at[peer],
            recv_sem=recv_b.at[me],
            device_id=here(peer),
            device_id_type=MESH,
        )
        copy.start()
        gather.append(copy)
    for k in range(1, peers):
        src = (me + peers - k) % peers
        pltpu.make_async_remote_copy(
            src_ref=out_ref.at[pl.ds(pl.multiple_of(src * rows, rows), rows)],
            dst_ref=out_ref.at[pl.ds(pl.multiple_of(src * rows, rows), rows)],
            send_sem=send_b.at[src],
            recv_sem=recv_b.at[src],
            device_id=here(src),
            device_id_type=MESH,
        ).wait_recv()
    for copy in gather:
        copy.wait_send()
    factor = lax.rsqrt(out_ref[...] / peers + 1e-05)
    factor = factor * valid_ref[...].astype(jnp.float32)
    white = (spectrum * jnp.concatenate([factor, factor], axis=1)).astype(white_ref.dtype)
    white_ref[...] = white
    count = white.shape[0]
    left_ref[pl.ds(0, count), :] = white
    left_ref[pl.ds(count, count), :] = jnp.concatenate([white[:, wide:], -white[:, :wide]], axis=1)


def freq_whiten(spectra, valid, peers):
    chans, double_width = spectra.shape
    wide = double_width // 2
    return pl.pallas_call(
        functools.partial(_whiten_kernel, peers, True),
        out_shape=(
            jax.ShapeDtypeStruct((chans, double_width), spectra.dtype),
            jax.ShapeDtypeStruct((2 * chans, double_width), spectra.dtype),
        ),
        in_specs=[pl.BlockSpec(memory_space=pltpu.VMEM)] * 2,
        out_specs=(pl.BlockSpec(memory_space=pltpu.VMEM), pl.BlockSpec(memory_space=pltpu.VMEM)),
        scratch_shapes=[
            pltpu.VMEM((chans, wide), jnp.float32),
            pltpu.VMEM((chans, wide), jnp.float32),
            pltpu.VMEM((peers, chans // peers, wide), jnp.float32),
            pltpu.SemaphoreType.DMA((peers,)),
            pltpu.SemaphoreType.DMA((peers,)),
            pltpu.SemaphoreType.DMA((peers,)),
            pltpu.SemaphoreType.DMA((peers,)),
        ],
        compiler_params=pltpu.CompilerParams(collective_id=0, has_side_effects=True),
    )(spectra, valid)


def _gather_kernel(peers, x_ref, out_ref, send_sem, recv_sem):
    me = lax.axis_index("freq")
    grp = lax.axis_index("grp")

    def here(peer):
        return (grp, peer)

    _greet(peers, here)
    sent = []
    for k in range(1, peers):
        peer = (me + k) % peers
        copy = pltpu.make_async_remote_copy(
            src_ref=x_ref,
            dst_ref=out_ref.at[me],
            send_sem=send_sem.at[peer],
            recv_sem=recv_sem.at[me],
            device_id=here(peer),
            device_id_type=MESH,
        )
        copy.start()
        sent.append(copy)
    out_ref[me] = x_ref[...]
    for k in range(1, peers):
        src = (me + peers - k) % peers
        pltpu.make_async_remote_copy(
            src_ref=x_ref,
            dst_ref=out_ref.at[src],
            send_sem=send_sem.at[src],
            recv_sem=recv_sem.at[src],
            device_id=here(src),
            device_id_type=MESH,
        ).wait_recv()
    for copy in sent:
        copy.wait_send()


def freq_gather(x, peers):
    return pl.pallas_call(
        functools.partial(_gather_kernel, peers),
        out_shape=jax.ShapeDtypeStruct((peers, *x.shape), x.dtype),
        in_specs=[pl.BlockSpec(memory_space=pltpu.VMEM)],
        out_specs=pl.BlockSpec(memory_space=pltpu.VMEM),
        scratch_shapes=[
            pltpu.SemaphoreType.DMA((peers,)),
            pltpu.SemaphoreType.DMA((peers,)),
        ],
        compiler_params=pltpu.CompilerParams(collective_id=1, has_side_effects=True),
    )(x)


def _rows_kernel(chips, x_ref, out_ref, pair, held, send_sem, recv_sem):
    me = lax.axis_index("grp")
    band = lax.axis_index("freq")
    core = me % 2
    chip = me // 2
    partner = me + 1 - 2 * core

    def dev(g):
        return (g, band)

    barrier = pltpu.get_barrier_semaphore()
    pl.semaphore_signal(barrier, inc=1, device_id=dev(partner), device_id_type=MESH)
    for k in range(1, chips):
        pl.semaphore_signal(barrier, inc=1, device_id=dev(((chip + k) % chips) * 2 + core), device_id_type=MESH)
    pl.semaphore_wait(barrier, chips)

    first = pltpu.make_async_remote_copy(
        src_ref=x_ref, dst_ref=pair, send_sem=send_sem.at[0], recv_sem=recv_sem.at[0],
        device_id=dev(partner), device_id_type=MESH,
    )
    first.start()
    first.wait_recv()
    first.wait_send()
    held[chip] = (x_ref[...].astype(jnp.float32) + pair[...].astype(jnp.float32)).astype(held.dtype)
    sent = []
    for k in range(1, chips):
        peer = (chip + k) % chips
        copy = pltpu.make_async_remote_copy(
            src_ref=held.at[chip], dst_ref=held.at[chip], send_sem=send_sem.at[1 + peer],
            recv_sem=recv_sem.at[1 + chip], device_id=dev(peer * 2 + core), device_id_type=MESH,
        )
        copy.start()
        sent.append(copy)
    for k in range(1, chips):
        src = (chip + chips - k) % chips
        pltpu.make_async_remote_copy(
            src_ref=held.at[src], dst_ref=held.at[src], send_sem=send_sem.at[1 + src],
            recv_sem=recv_sem.at[1 + src], device_id=dev(src * 2 + core), device_id_type=MESH,
        ).wait_recv()
    for copy in sent:
        copy.wait_send()
    total = held[0].astype(jnp.float32)
    for c in range(1, chips):
        total = total + held[c].astype(jnp.float32)
    out_ref[...] = total.astype(out_ref.dtype)


def grp_rows_sum(x, chips):
    return pl.pallas_call(
        functools.partial(_rows_kernel, chips),
        out_shape=jax.ShapeDtypeStruct(x.shape, x.dtype),
        in_specs=[pl.BlockSpec(memory_space=pltpu.VMEM)],
        out_specs=pl.BlockSpec(memory_space=pltpu.VMEM),
        scratch_shapes=[
            pltpu.VMEM(x.shape, x.dtype),
            pltpu.VMEM((chips, *x.shape), x.dtype),
            pltpu.SemaphoreType.DMA((chips + 1,)),
            pltpu.SemaphoreType.DMA((chips + 1,)),
        ],
        compiler_params=pltpu.CompilerParams(collective_id=2, has_side_effects=True),
    )(x)


def _cross_kernel(zs, bands, scaling, spec_ref, valid_ref, sel_ref, cross_ref, bins_ref, held, stage, picked,
                  send_sem, recv_ring, recv_x, recv_sib, out_sem, recv_f, x_ref, left_ref, power, summed, parts,
                  send_a, recv_a, send_b, recv_b):
    me = lax.axis_index("grp")
    band = lax.axis_index("freq")
    c = me % 2
    xl = (me // 2) % 2
    z = me // 4
    step = 1 - 2 * c
    width = x_ref.shape[0]
    half = width // 2

    def blk(zz, xx, cc):
        return (zz * 2 + xx) * 2 + cc

    def dev(g):
        return (g, band)

    sib = blk(z, xl, 1 - c)
    partner = blk(z, 1 - xl, c)
    nxt = blk((z + step + zs) % zs, xl, c)
    prv = blk((z - step + zs) % zs, xl, c)

    barrier = pltpu.get_barrier_semaphore()
    for g in (sib, partner, nxt, prv):
        pl.semaphore_signal(barrier, inc=1, device_id=dev(g), device_id_type=MESH)
    for k in range(1, bands):
        pl.semaphore_signal(barrier, inc=1, device_id=(me, (band + k) % bands), device_id_type=MESH)
    pl.semaphore_wait(barrier, 4 + bands - 1)
    _whiten_kernel(bands, False, spec_ref, valid_ref, x_ref, left_ref, power, summed, parts,
                   send_a, recv_a, send_b, recv_b)

    sends = []
    outs = []

    def send(src, dst, recv, g):
        copy = pltpu.make_async_remote_copy(
            src_ref=src, dst_ref=dst, send_sem=send_sem.at[len(sends)], recv_sem=recv,
            device_id=dev(g), device_id_type=MESH,
        )
        copy.start()
        sends.append(copy)

    def wait(dst, recv, g):
        pltpu.make_async_remote_copy(
            src_ref=dst, dst_ref=dst, send_sem=send_sem.at[0], recv_sem=recv,
            device_id=dev(g), device_id_type=MESH,
        ).wait_recv()

    def rows(b, h):
        return held.at[b, pl.ds(pl.multiple_of(h * half, half), half)]

    def compute(b):
        block = held[b]
        prod = lax.dot_general(
            left_ref[...], block, (((1,), (1,)), ((), ())), preferred_element_type=jnp.float32
        )
        slot = len(outs) % 2
        if len(outs) >= 2:
            outs[-2].wait()
        stage[slot] = (prod * scaling).astype(stage.dtype).reshape(stage.shape[1:])
        copy = pltpu.make_async_copy(
            stage.at[slot], cross_ref.at[:, :, pl.ds(pl.multiple_of(b * width, width), width)], out_sem.at[slot]
        )
        copy.start()
        outs.append(copy)
        columns = b * width + lax.broadcasted_iota(jnp.int32, (stations, width), 1)
        chosen = (station_ids == columns).astype(block.dtype)
        picked[...] += jnp.dot(chosen, block, preferred_element_type=jnp.float32)

    picked[...] = jnp.zeros_like(picked)
    stations = picked.shape[0]
    place = lax.broadcasted_iota(jnp.int32, (stations, width), 0)
    station_ids = jnp.zeros((stations, width), jnp.int32)
    for k in range(stations):
        station_ids = jnp.where(place == k, sel_ref[k], station_ids)
    own = blk(z, xl, c)
    held[own] = x_ref[...]
    send(x_ref, held.at[own], recv_x.at[0], partner)
    send(x_ref, held.at[own], recv_sib.at[0], sib)
    send(x_ref.at[pl.ds(0, half)], rows(own, 0), recv_ring.at[0, 0], nxt)
    send(x_ref.at[pl.ds(half, half)], rows(own, 1), recv_ring.at[0, 1], nxt)
    compute(own)
    across = blk(z, 1 - xl, c)
    wait(held.at[across], recv_x.at[0], partner)
    send(rows(across, xl), rows(across, xl), recv_ring.at[0, 2], nxt)
    send(held.at[across], held.at[across], recv_sib.at[1], sib)
    compute(across)

    def finish(t):
        zo = (z - step * (t + 1) + 2 * zs) % zs
        part = blk(zo, 1 - xl, c)
        wait(rows(part, 1 - xl), recv_x.at[1 + t], partner)
        send(rows(part, 1 - xl), rows(part, 1 - xl), recv_sib.at[2 + 3 * (zs - 1) + t], sib)
        compute(part)
        zt = (z + step * (t + 1) + 2 * zs) % zs
        sfull = blk(zt, xl, 1 - c)
        spart = blk(zt, 1 - xl, 1 - c)
        for k, (b, h) in enumerate(((sfull, 0), (sfull, 1), (spart, xl))):
            wait(rows(b, h), recv_sib.at[2 + 3 * t + k], sib)
        compute(sfull)
        wait(rows(spart, 1 - xl), recv_sib.at[2 + 3 * (zs - 1) + t], sib)
        compute(spart)

    for s in range(zs - 1):
        zo = (z - step * (s + 1) + 2 * zs) % zs
        full = blk(zo, xl, c)
        part = blk(zo, 1 - xl, c)
        pieces = ((full, 0), (full, 1), (part, xl))
        for k, (b, h) in enumerate(pieces):
            wait(rows(b, h), recv_ring.at[s, k], prv)
            if s < zs - 2:
                send(rows(b, h), rows(b, h), recv_ring.at[s + 1, k], nxt)
        send(rows(full, xl), rows(full, xl), recv_x.at[1 + s], partner)
        for k, (b, h) in enumerate(pieces):
            send(rows(b, h), rows(b, h), recv_sib.at[2 + 3 * s + k], sib)
        compute(full)
        if s == 0:
            wait(held.at[sib], recv_sib.at[0], sib)
            compute(sib)
            sib_across = blk(z, 1 - xl, 1 - c)
            wait(held.at[sib_across], recv_sib.at[1], sib)
            compute(sib_across)
        else:
            finish(s - 1)
    finish(zs - 2)
    station = picked[...]
    wide = station.shape[1] // 2
    swapped = jnp.concatenate([station[:, wide:], -station[:, :wide]], axis=1)
    left = jnp.concatenate([station, swapped], axis=0).astype(x_ref.dtype)
    values = lax.dot_general(
        left, x_ref[...], (((1,), (1,)), ((), ())), preferred_element_type=jnp.float32
    ) * scaling
    bins_ref[band] = values.reshape(bins_ref.shape[1:])
    for k in range(1, bands):
        peer = (band + k) % bands
        copy = pltpu.make_async_remote_copy(
            src_ref=bins_ref.at[band], dst_ref=bins_ref.at[band], send_sem=send_sem.at[len(sends)],
            recv_sem=recv_f.at[band], device_id=(me, peer), device_id_type=MESH,
        )
        copy.start()
        sends.append(copy)
    for k in range(1, bands):
        src = (band + bands - k) % bands
        pltpu.make_async_remote_copy(
            src_ref=bins_ref.at[src], dst_ref=bins_ref.at[src], send_sem=send_sem.at[0],
            recv_sem=recv_f.at[src], device_id=(me, src), device_id_type=MESH,
        ).wait_recv()
    for copy in outs[-2:]:
        copy.wait()
    for copy in sends:
        copy.wait_send()


def grp_cross(spectra, valid, selector, scaling, zs):
    groups = lax.axis_size("grp")
    bands = lax.axis_size("freq")
    width, cols = spectra.shape
    whitened = spectra
    wide = cols // 2
    return pl.pallas_call(
        functools.partial(_cross_kernel, zs, bands, scaling),
        out_shape=(
            jax.ShapeDtypeStruct((2, width, groups * width), whitened.dtype),
            jax.ShapeDtypeStruct((bands, 2, selector.shape[0], width), jnp.float32),
        ),
        in_specs=[pl.BlockSpec(memory_space=pltpu.VMEM)] * 2 + [pl.BlockSpec(memory_space=pltpu.SMEM)],
        out_specs=(pl.BlockSpec(memory_space=pl.ANY), pl.BlockSpec(memory_space=pltpu.VMEM)),
        scratch_shapes=[
            pltpu.VMEM((groups, width, cols), whitened.dtype),
            pltpu.VMEM((2, 2, width, width), whitened.dtype),
            pltpu.VMEM((selector.shape[0], cols), jnp.float32),
            pltpu.SemaphoreType.DMA((8 * zs + 16,)),
            pltpu.SemaphoreType.DMA((zs - 1, 3)),
            pltpu.SemaphoreType.DMA((zs,)),
            pltpu.SemaphoreType.DMA((2 + 4 * (zs - 1),)),
            pltpu.SemaphoreType.DMA((2,)),
            pltpu.SemaphoreType.DMA((bands,)),
            pltpu.VMEM((width, cols), spectra.dtype),
            pltpu.VMEM((2 * width, cols), spectra.dtype),
            pltpu.VMEM((width, wide), jnp.float32),
            pltpu.VMEM((width, wide), jnp.float32),
            pltpu.VMEM((bands, width // bands, wide), jnp.float32),
            pltpu.SemaphoreType.DMA((bands,)),
            pltpu.SemaphoreType.DMA((bands,)),
            pltpu.SemaphoreType.DMA((bands,)),
            pltpu.SemaphoreType.DMA((bands,)),
        ],
        compiler_params=pltpu.CompilerParams(
            collective_id=3, has_side_effects=True, vmem_limit_bytes=56 * 1024 * 1024
        ),
    )(spectra, valid, selector)


def on_device(spectra, valid, station_index):
    bin_count, chan_count, double_width = spectra.shape
    window_count = double_width // 2
    freq_count = lax.axis_size("freq")
    total_bins = bin_count * freq_count
    scaling = 1.0 / math.sqrt(window_count)
    station_count = station_index.shape[0]
    selector = station_index
    cross, all_bins = grp_cross(
        spectra[0], valid, selector, scaling, lax.axis_size("grp") // 4
    )
    cross = cross[None]

    lag_share = LAGS // freq_count
    freq_index = lax.axis_index("freq")
    bin_values = jnp.arange(total_bins, dtype=jnp.float32) + 1.0
    lag_values = (freq_index * lag_share + jnp.arange(lag_share, dtype=jnp.int32)).astype(jnp.float32)
    phase = math.pi * bin_values[:, None] * lag_values[None, :] / LAGS
    lag_table = jnp.stack([jnp.cos(phase), -jnp.sin(phase)], axis=1)
    station_gather = jnp.einsum(
        "frsc,frl->scl", all_bins, lag_table, precision=lax.Precision.HIGH
    ) / math.sqrt(total_bins)
    return (cross, station_gather)


def solution(mesh):
    placed = (P("freq", "grp", None), P("grp", None), P())
    return jax.shard_map(
        on_device,
        mesh=mesh,
        in_specs=placed,
        out_specs=(P("freq", None, "grp", None), P(None, "grp", "freq")),
        check_vma=False,
    )
```

```python
import functools
import math

import jax
import jax.numpy as jnp
from jax import lax
from jax.experimental import pallas as pl
from jax.experimental.pallas import tpu as pltpu
from jax.sharding import PartitionSpec as P

LAGS = 256
MESH = pl.DeviceIdType.MESH


def _greet(peers, here):
    barrier = pltpu.get_barrier_semaphore()
    for k in range(1, peers):
        pl.semaphore_signal(barrier, inc=1, device_id=here((lax.axis_index("freq") + k) % peers), device_id_type=MESH)
    pl.semaphore_wait(barrier, peers - 1)


def _whiten_kernel(peers, greet, spec_ref, valid_ref, white_ref, left_ref, x_ref, out_ref, parts,
                   send_a, recv_a, send_b, recv_b):
    me = lax.axis_index("freq")
    grp = lax.axis_index("grp")
    rows = x_ref.shape[0] // peers
    wide = x_ref.shape[1]

    def here(peer):
        return (grp, peer)

    spectrum = spec_ref[...].astype(jnp.float32)
    real_part = spectrum[:, :wide]
    imag_part = spectrum[:, wide:]
    x_ref[...] = real_part * real_part + imag_part * imag_part
    if greet:
        _greet(peers, here)
    scatter = []
    for k in range(1, peers):
        peer = (me + k) % peers
        copy = pltpu.make_async_remote_copy(
            src_ref=x_ref.at[pl.ds(pl.multiple_of(peer * rows, rows), rows)],
            dst_ref=parts.at[me],
            send_sem=send_a.at[peer],
            recv_sem=recv_a.at[me],
            device_id=here(peer),
            device_id_type=MESH,
        )
        copy.start()
        scatter.append(copy)
    own = x_ref[pl.ds(pl.multiple_of(me * rows, rows), rows), :]
    for k in range(1, peers):
        src = (me + peers - k) % peers
        pltpu.make_async_remote_copy(
            src_ref=x_ref.at[pl.ds(0, rows)],
            dst_ref=parts.at[src],
            send_sem=send_a.at[src],
            recv_sem=recv_a.at[src],
            device_id=here(src),
            device_id_type=MESH,
        ).wait_recv()
    for copy in scatter:
        copy.wait_send()
    parts[me] = own
    total = parts[0]
    for src in range(1, peers):
        total = total + parts[src]
    out_ref[pl.ds(pl.multiple_of(me * rows, rows), rows), :] = total
    gather = []
    for k in range(1, peers):
        peer = (me + k) % peers
        copy = pltpu.make_async_remote_copy(
            src_ref=out_ref.at[pl.ds(pl.multiple_of(me * rows, rows), rows)],
            dst_ref=out_ref.at[pl.ds(pl.multiple_of(me * rows, rows), rows)],
            send_sem=send_b.at[peer],
            recv_sem=recv_b.at[me],
            device_id=here(peer),
            device_id_type=MESH,
        )
        copy.start()
        gather.append(copy)
    for k in range(1, peers):
        src = (me + peers - k) % peers
        pltpu.make_async_remote_copy(
            src_ref=out_ref.at[pl.ds(pl.multiple_of(src * rows, rows), rows)],
            dst_ref=out_ref.at[pl.ds(pl.multiple_of(src * rows, rows), rows)],
            send_sem=send_b.at[src],
            recv_sem=recv_b.at[src],
            device_id=here(src),
            device_id_type=MESH,
        ).wait_recv()
    for copy in gather:
        copy.wait_send()
    factor = lax.rsqrt(out_ref[...] / peers + 1e-05)
    factor = factor * valid_ref[...].astype(jnp.float32)
    white = (spectrum * jnp.concatenate([factor, factor], axis=1)).astype(white_ref.dtype)
    white_ref[...] = white
    count = white.shape[0]
    left_ref[pl.ds(0, count), :] = white
    left_ref[pl.ds(count, count), :] = jnp.concatenate([white[:, wide:], -white[:, :wide]], axis=1)


def freq_whiten(spectra, valid, peers):
    chans, double_width = spectra.shape
    wide = double_width // 2
    return pl.pallas_call(
        functools.partial(_whiten_kernel, peers, True),
        out_shape=(
            jax.ShapeDtypeStruct((chans, double_width), spectra.dtype),
            jax.ShapeDtypeStruct((2 * chans, double_width), spectra.dtype),
        ),
        in_specs=[pl.BlockSpec(memory_space=pltpu.VMEM)] * 2,
        out_specs=(pl.BlockSpec(memory_space=pltpu.VMEM), pl.BlockSpec(memory_space=pltpu.VMEM)),
        scratch_shapes=[
            pltpu.VMEM((chans, wide), jnp.float32),
            pltpu.VMEM((chans, wide), jnp.float32),
            pltpu.VMEM((peers, chans // peers, wide), jnp.float32),
            pltpu.SemaphoreType.DMA((peers,)),
            pltpu.SemaphoreType.DMA((peers,)),
            pltpu.SemaphoreType.DMA((peers,)),
            pltpu.SemaphoreType.DMA((peers,)),
        ],
        compiler_params=pltpu.CompilerParams(collective_id=0, has_side_effects=True),
    )(spectra, valid)


def _gather_kernel(peers, x_ref, out_ref, send_sem, recv_sem):
    me = lax.axis_index("freq")
    grp = lax.axis_index("grp")

    def here(peer):
        return (grp, peer)

    _greet(peers, here)
    sent = []
    for k in range(1, peers):
        peer = (me + k) % peers
        copy = pltpu.make_async_remote_copy(
            src_ref=x_ref,
            dst_ref=out_ref.at[me],
            send_sem=send_sem.at[peer],
            recv_sem=recv_sem.at[me],
            device_id=here(peer),
            device_id_type=MESH,
        )
        copy.start()
        sent.append(copy)
    out_ref[me] = x_ref[...]
    for k in range(1, peers):
        src = (me + peers - k) % peers
        pltpu.make_async_remote_copy(
            src_ref=x_ref,
            dst_ref=out_ref.at[src],
            send_sem=send_sem.at[src],
            recv_sem=recv_sem.at[src],
            device_id=here(src),
            device_id_type=MESH,
        ).wait_recv()
    for copy in sent:
        copy.wait_send()


def freq_gather(x, peers):
    return pl.pallas_call(
        functools.partial(_gather_kernel, peers),
        out_shape=jax.ShapeDtypeStruct((peers, *x.shape), x.dtype),
        in_specs=[pl.BlockSpec(memory_space=pltpu.VMEM)],
        out_specs=pl.BlockSpec(memory_space=pltpu.VMEM),
        scratch_shapes=[
            pltpu.SemaphoreType.DMA((peers,)),
            pltpu.SemaphoreType.DMA((peers,)),
        ],
        compiler_params=pltpu.CompilerParams(collective_id=1, has_side_effects=True),
    )(x)


def _rows_kernel(chips, x_ref, out_ref, pair, held, send_sem, recv_sem):
    me = lax.axis_index("grp")
    band = lax.axis_index("freq")
    core = me % 2
    chip = me // 2
    partner = me + 1 - 2 * core

    def dev(g):
        return (g, band)

    barrier = pltpu.get_barrier_semaphore()
    pl.semaphore_signal(barrier, inc=1, device_id=dev(partner), device_id_type=MESH)
    for k in range(1, chips):
        pl.semaphore_signal(barrier, inc=1, device_id=dev(((chip + k) % chips) * 2 + core), device_id_type=MESH)
    pl.semaphore_wait(barrier, chips)

    first = pltpu.make_async_remote_copy(
        src_ref=x_ref, dst_ref=pair, send_sem=send_sem.at[0], recv_sem=recv_sem.at[0],
        device_id=dev(partner), device_id_type=MESH,
    )
    first.start()
    first.wait_recv()
    first.wait_send()
    held[chip] = (x_ref[...].astype(jnp.float32) + pair[...].astype(jnp.float32)).astype(held.dtype)
    sent = []
    for k in range(1, chips):
        peer = (chip + k) % chips
        copy = pltpu.make_async_remote_copy(
            src_ref=held.at[chip], dst_ref=held.at[chip], send_sem=send_sem.at[1 + peer],
            recv_sem=recv_sem.at[1 + chip], device_id=dev(peer * 2 + core), device_id_type=MESH,
        )
        copy.start()
        sent.append(copy)
    for k in range(1, chips):
        src = (chip + chips - k) % chips
        pltpu.make_async_remote_copy(
            src_ref=held.at[src], dst_ref=held.at[src], send_sem=send_sem.at[1 + src],
            recv_sem=recv_sem.at[1 + src], device_id=dev(src * 2 + core), device_id_type=MESH,
        ).wait_recv()
    for copy in sent:
        copy.wait_send()
    total = held[0].astype(jnp.float32)
    for c in range(1, chips):
        total = total + held[c].astype(jnp.float32)
    out_ref[...] = total.astype(out_ref.dtype)


def grp_rows_sum(x, chips):
    return pl.pallas_call(
        functools.partial(_rows_kernel, chips),
        out_shape=jax.ShapeDtypeStruct(x.shape, x.dtype),
        in_specs=[pl.BlockSpec(memory_space=pltpu.VMEM)],
        out_specs=pl.BlockSpec(memory_space=pltpu.VMEM),
        scratch_shapes=[
            pltpu.VMEM(x.shape, x.dtype),
            pltpu.VMEM((chips, *x.shape), x.dtype),
            pltpu.SemaphoreType.DMA((chips + 1,)),
            pltpu.SemaphoreType.DMA((chips + 1,)),
        ],
        compiler_params=pltpu.CompilerParams(collective_id=2, has_side_effects=True),
    )(x)


def _cross_kernel(zs, bands, scaling, spec_ref, valid_ref, sel_ref, cross_ref, bins_ref, held, stage, picked,
                  send_sem, recv_ring, recv_x, recv_sib, out_sem, recv_f, x_ref, left_ref, power, summed, parts,
                  send_a, recv_a, send_b, recv_b):
    me = lax.axis_index("grp")
    band = lax.axis_index("freq")
    c = me % 2
    xl = (me // 2) % 2
    z = me // 4
    step = 1 - 2 * c
    width = x_ref.shape[0]
    half = width // 2

    def blk(zz, xx, cc):
        return (zz * 2 + xx) * 2 + cc

    def dev(g):
        return (g, band)

    sib = blk(z, xl, 1 - c)
    partner = blk(z, 1 - xl, c)
    nxt = blk((z + step + zs) % zs, xl, c)
    prv = blk((z - step + zs) % zs, xl, c)

    barrier = pltpu.get_barrier_semaphore()
    for g in (sib, partner, nxt, prv):
        pl.semaphore_signal(barrier, inc=1, device_id=dev(g), device_id_type=MESH)
    for k in range(1, bands):
        pl.semaphore_signal(barrier, inc=1, device_id=(me, (band + k) % bands), device_id_type=MESH)
    pl.semaphore_wait(barrier, 4 + bands - 1)
    _whiten_kernel(bands, False, spec_ref, valid_ref, x_ref, left_ref, power, summed, parts,
                   send_a, recv_a, send_b, recv_b)

    sends = []
    outs = []

    def send(src, dst, recv, g):
        copy = pltpu.make_async_remote_copy(
            src_ref=src, dst_ref=dst, send_sem=send_sem.at[len(sends)], recv_sem=recv,
            device_id=dev(g), device_id_type=MESH,
        )
        copy.start()
        sends.append(copy)

    def wait(dst, recv, g):
        pltpu.make_async_remote_copy(
            src_ref=dst, dst_ref=dst, send_sem=send_sem.at[0], recv_sem=recv,
            device_id=dev(g), device_id_type=MESH,
        ).wait_recv()

    def rows(b, h):
        return held.at[b, pl.ds(pl.multiple_of(h * half, half), half)]

    def compute(b):
        block = held[b]
        prod = lax.dot_general(
            left_ref[...], block, (((1,), (1,)), ((), ())), preferred_element_type=jnp.float32
        )
        slot = len(outs) % 2
        if len(outs) >= 2:
            outs[-2].wait()
        stage[slot] = (prod * scaling).astype(stage.dtype).reshape(stage.shape[1:])
        copy = pltpu.make_async_copy(
            stage.at[slot], cross_ref.at[:, :, pl.ds(pl.multiple_of(b * width, width), width)], out_sem.at[slot]
        )
        copy.start()
        outs.append(copy)
        columns = b * width + lax.broadcasted_iota(jnp.int32, (stations, width), 1)
        chosen = (station_ids == columns).astype(block.dtype)
        picked[...] += jnp.dot(chosen, block, preferred_element_type=jnp.float32)

    picked[...] = jnp.zeros_like(picked)
    stations = picked.shape[0]
    place = lax.broadcasted_iota(jnp.int32, (stations, width), 0)
    station_ids = jnp.zeros((stations, width), jnp.int32)
    for k in range(stations):
        station_ids = jnp.where(place == k, sel_ref[k], station_ids)
    own = blk(z, xl, c)
    held[own] = x_ref[...]
    send(x_ref.at[pl.ds(pl.multiple_of((1 - xl) * half, half), half)], rows(own, 1 - xl), recv_x.at[0], partner)
    send(x_ref.at[pl.ds(pl.multiple_of(xl * half, half), half)], rows(own, xl), recv_x.at[zs], partner)
    send(x_ref, held.at[own], recv_sib.at[0], sib)
    send(x_ref.at[pl.ds(0, half)], rows(own, 0), recv_ring.at[0, 0], nxt)
    send(x_ref.at[pl.ds(half, half)], rows(own, 1), recv_ring.at[0, 1], nxt)
    compute(own)
    across = blk(z, 1 - xl, c)
    wait(rows(across, xl), recv_x.at[0], partner)
    send(rows(across, xl), rows(across, xl), recv_ring.at[0, 2], nxt)
    wait(rows(across, 1 - xl), recv_x.at[zs], partner)
    send(held.at[across], held.at[across], recv_sib.at[1], sib)
    compute(across)

    def finish(t):
        zo = (z - step * (t + 1) + 2 * zs) % zs
        part = blk(zo, 1 - xl, c)
        wait(rows(part, 1 - xl), recv_x.at[1 + t], partner)
        send(rows(part, 1 - xl), rows(part, 1 - xl), recv_sib.at[2 + 3 * (zs - 1) + t], sib)
        compute(part)
        zt = (z + step * (t + 1) + 2 * zs) % zs
        sfull = blk(zt, xl, 1 - c)
        spart = blk(zt, 1 - xl, 1 - c)
        for k, (b, h) in enumerate(((sfull, 0), (sfull, 1), (spart, xl))):
            wait(rows(b, h), recv_sib.at[2 + 3 * t + k], sib)
        compute(sfull)
        wait(rows(spart, 1 - xl), recv_sib.at[2 + 3 * (zs - 1) + t], sib)
        compute(spart)

    for s in range(zs - 1):
        zo = (z - step * (s + 1) + 2 * zs) % zs
        full = blk(zo, xl, c)
        part = blk(zo, 1 - xl, c)
        pieces = ((full, 0), (full, 1), (part, xl))
        for k, (b, h) in enumerate(pieces):
            wait(rows(b, h), recv_ring.at[s, k], prv)
            if s < zs - 2:
                send(rows(b, h), rows(b, h), recv_ring.at[s + 1, k], nxt)
        send(rows(full, xl), rows(full, xl), recv_x.at[1 + s], partner)
        for k, (b, h) in enumerate(pieces):
            send(rows(b, h), rows(b, h), recv_sib.at[2 + 3 * s + k], sib)
        compute(full)
        if s == 0:
            wait(held.at[sib], recv_sib.at[0], sib)
            compute(sib)
            sib_across = blk(z, 1 - xl, 1 - c)
            wait(held.at[sib_across], recv_sib.at[1], sib)
            compute(sib_across)
        else:
            finish(s - 1)
    finish(zs - 2)
    station = picked[...]
    wide = station.shape[1] // 2
    swapped = jnp.concatenate([station[:, wide:], -station[:, :wide]], axis=1)
    left = jnp.concatenate([station, swapped], axis=0).astype(x_ref.dtype)
    values = lax.dot_general(
        left, x_ref[...], (((1,), (1,)), ((), ())), preferred_element_type=jnp.float32
    ) * scaling
    bins_ref[band] = values.reshape(bins_ref.shape[1:])
    for k in range(1, bands):
        peer = (band + k) % bands
        copy = pltpu.make_async_remote_copy(
            src_ref=bins_ref.at[band], dst_ref=bins_ref.at[band], send_sem=send_sem.at[len(sends)],
            recv_sem=recv_f.at[band], device_id=(me, peer), device_id_type=MESH,
        )
        copy.start()
        sends.append(copy)
    for k in range(1, bands):
        src = (band + bands - k) % bands
        pltpu.make_async_remote_copy(
            src_ref=bins_ref.at[src], dst_ref=bins_ref.at[src], send_sem=send_sem.at[0],
            recv_sem=recv_f.at[src], device_id=(me, src), device_id_type=MESH,
        ).wait_recv()
    for copy in outs[-2:]:
        copy.wait()
    for copy in sends:
        copy.wait_send()


def grp_cross(spectra, valid, selector, scaling, zs):
    groups = lax.axis_size("grp")
    bands = lax.axis_size("freq")
    width, cols = spectra.shape
    whitened = spectra
    wide = cols // 2
    return pl.pallas_call(
        functools.partial(_cross_kernel, zs, bands, scaling),
        out_shape=(
            jax.ShapeDtypeStruct((2, width, groups * width), whitened.dtype),
            jax.ShapeDtypeStruct((bands, 2, selector.shape[0], width), jnp.float32),
        ),
        in_specs=[pl.BlockSpec(memory_space=pltpu.VMEM)] * 2 + [pl.BlockSpec(memory_space=pltpu.SMEM)],
        out_specs=(pl.BlockSpec(memory_space=pl.ANY), pl.BlockSpec(memory_space=pltpu.VMEM)),
        scratch_shapes=[
            pltpu.VMEM((groups, width, cols), whitened.dtype),
            pltpu.VMEM((2, 2, width, width), whitened.dtype),
            pltpu.VMEM((selector.shape[0], cols), jnp.float32),
            pltpu.SemaphoreType.DMA((8 * zs + 16,)),
            pltpu.SemaphoreType.DMA((zs - 1, 3)),
            pltpu.SemaphoreType.DMA((zs + 1,)),
            pltpu.SemaphoreType.DMA((2 + 4 * (zs - 1),)),
            pltpu.SemaphoreType.DMA((2,)),
            pltpu.SemaphoreType.DMA((bands,)),
            pltpu.VMEM((width, cols), spectra.dtype),
            pltpu.VMEM((2 * width, cols), spectra.dtype),
            pltpu.VMEM((width, wide), jnp.float32),
            pltpu.VMEM((width, wide), jnp.float32),
            pltpu.VMEM((bands, width // bands, wide), jnp.float32),
            pltpu.SemaphoreType.DMA((bands,)),
            pltpu.SemaphoreType.DMA((bands,)),
            pltpu.SemaphoreType.DMA((bands,)),
            pltpu.SemaphoreType.DMA((bands,)),
        ],
        compiler_params=pltpu.CompilerParams(
            collective_id=3, has_side_effects=True, vmem_limit_bytes=56 * 1024 * 1024
        ),
    )(spectra, valid, selector)


def on_device(spectra, valid, station_index):
    bin_count, chan_count, double_width = spectra.shape
    window_count = double_width // 2
    freq_count = lax.axis_size("freq")
    total_bins = bin_count * freq_count
    scaling = 1.0 / math.sqrt(window_count)
    station_count = station_index.shape[0]
    selector = station_index
    cross, all_bins = grp_cross(
        spectra[0], valid, selector, scaling, lax.axis_size("grp") // 4
    )
    cross = cross[None]

    lag_share = LAGS // freq_count
    freq_index = lax.axis_index("freq")
    bin_values = jnp.arange(total_bins, dtype=jnp.float32) + 1.0
    lag_values = (freq_index * lag_share + jnp.arange(lag_share, dtype=jnp.int32)).astype(jnp.float32)
    phase = math.pi * bin_values[:, None] * lag_values[None, :] / LAGS
    lag_table = jnp.stack([jnp.cos(phase), -jnp.sin(phase)], axis=1)
    station_gather = jnp.einsum(
        "frsc,frl->scl", all_bins, lag_table, precision=lax.Precision.HIGHEST
    ) / math.sqrt(total_bins)
    return (cross, station_gather)


def solution(mesh):
    placed = (P("freq", "grp", None), P("grp", None), P())
    return jax.shard_map(
        on_device,
        mesh=mesh,
        in_specs=placed,
        out_specs=(P("freq", None, "grp", None), P(None, "grp", "freq")),
        check_vma=False,
    )
```
